32 devices in a mesh: dp: 4 (over z), context: 8 (over y, x, core).
Axes of the slice: x: 2, y: 2, z: 4, core: 2. Of those that a mesh axis runs over, the one named last changes fastest.
Arguments:
- queries: bfloat16 [4, 1536, 4096], P('dp', 'context'), may hold values from -6 to 6
- key_rows: bfloat16 [4, 1536, 4096], P('dp', 'context'), may hold values from -6 to 6
- value_rows: bfloat16 [4, 1536, 4096], P('dp', 'context'), may hold values from -6 to 6
- out_grad: bfloat16 [4, 1536, 4096], P('dp', 'context'), may hold values from -6 to 6
- log_decay: float32 [4, 1536, 32], P('dp', 'context'), may hold values from -0.8 to 0
- norm_gain: float32 [4096], replicated, may hold values from 0.1 to 1.9
Outputs:
- query_grad: bfloat16 [4, 1536, 4096], P('dp', 'context')
- key_grad: bfloat16 [4, 1536, 4096], P('dp', 'context')
- value_grad: bfloat16 [4, 1536, 4096], P('dp', 'context')
- gain_grad: float32 [4096], P(('dp', 'context'))
The draws below stay inside these ranges and needn't reach their ends.
All inputs are finite; a program needn't handle non-finite values.
Results may differ from the reference program's by a relative error of at most 0.0058.
Values sent between devices are 32-bit elements; how exact they have to be, the bound alone decides.
A program may use at most 128 MiB of HBM per device.

```python
import jax
import jax.numpy as jnp
from jax import lax

LOCAL_HEADS = 32
HD = 128
TOK_DEV = 192
SEQUENCE_COUNT = 4
SEQUENCE_LENGTH = 1536
FEAT = 4096


def draw_log_decay(key, part):
    random_key_quick, random_key_jitter, random_key_block, random_key_locate, random_key_spike = jax.random.split(key, 5)
    fast_share = 0.5
    fast_heads = jax.random.uniform(random_key_quick, (SEQUENCE_COUNT, 1, LOCAL_HEADS)) < fast_share
    jitter_amount = jax.random.uniform(random_key_jitter, (SEQUENCE_COUNT, SEQUENCE_LENGTH, LOCAL_HEADS), minval=0.5, maxval=1.5)
    block_count = SEQUENCE_LENGTH // TOK_DEV
    per_block_values = jnp.exp(jax.random.uniform(random_key_block, (SEQUENCE_COUNT, block_count, 1, LOCAL_HEADS), minval=-0.7, maxval=0.7))
    per_block_values = jnp.broadcast_to(per_block_values, (SEQUENCE_COUNT, block_count, TOK_DEV, LOCAL_HEADS)).reshape(SEQUENCE_COUNT, SEQUENCE_LENGTH, LOCAL_HEADS)
    baseline_rate = jnp.where(fast_heads, 1.0 / 40.0, 0.5 / SEQUENCE_LENGTH)
    locations = jax.random.randint(random_key_locate, (SEQUENCE_COUNT, 3, LOCAL_HEADS), 0, SEQUENCE_LENGTH)
    token_position = lax.broadcasted_iota(jnp.int32, (SEQUENCE_COUNT, SEQUENCE_LENGTH, LOCAL_HEADS), 1)
    spike_count = (token_position == locations[:, 0:1, :]) | (token_position == locations[:, 1:2, :]) | (token_position == locations[:, 2:3, :])
    spike_logits = jnp.log(jax.random.uniform(random_key_spike, (SEQUENCE_COUNT, SEQUENCE_LENGTH, LOCAL_HEADS), minval=0.5, maxval=0.8))
    return (-(baseline_rate * jitter_amount * per_block_values) + jnp.where(spike_count, spike_logits, 0.0)).astype(jnp.float32)


def spiked(values, own_key, source, target, shards_of, factor):
    def block_of(axis_at):
        return (jnp.arange(values.shape[axis_at]) // (values.shape[axis_at] // shards_of)).reshape((-1,) + (1,) * (values.ndim - 1 - axis_at))

    first = jax.random.permutation(own_key, shards_of)[block_of(target)]
    far = (block_of(target) + shards_of // 2) % shards_of
    return jnp.where((block_of(source) == first) | (block_of(source) == far), factor * values, values)


def shard_levels(own_key, shape, cuts, low, largest):
    def one(axis_at, shards_of):
        heights = jax.random.uniform(jax.random.fold_in(jax.random.fold_in(own_key, 6), axis_at), (shards_of,), jnp.float32, low / len(cuts), largest / len(cuts))
        return jnp.repeat(jnp.exp(heights), shape[axis_at] // shards_of).reshape((-1,) + (1,) * (len(shape) - axis_at - 1))

    level = one(*cuts[0])
    for cut in cuts[1:]:
        level = level * one(*cut)
    return level


def centred(stream_key, shape, scale, most, cuts=(), kind=jnp.bfloat16):
    loudness = shard_levels(stream_key, shape, cuts, -0.22, 0.18) if cuts else 1.0
    array = jax.random.normal(stream_key, shape, jnp.float32) * scale * loudness
    return jnp.minimum(jnp.maximum(array, -most), most).astype(kind)


def noise_with(stream_key, extent, scale, bound, pieces, heavy, held_as=jnp.bfloat16):
    result = scale * jax.random.normal(stream_key, extent, jnp.float32)
    if pieces:
        result = result * shard_levels(stream_key, extent, pieces, -0.22, 0.18)
    return jnp.clip(spiked(result, jax.random.fold_in(stream_key, 3), *heavy), -bound, bound).astype(held_as)


def setup_inputs(seed: int = 0) -> dict:
    seeds = jax.random.split(jax.random.key(seed), 7)
    return {
        "queries": centred(seeds[0], (SEQUENCE_COUNT, SEQUENCE_LENGTH, FEAT), 1.0, 6.0, ((0, 4), (1, 8))),
        "key_rows": centred(seeds[1], (SEQUENCE_COUNT, SEQUENCE_LENGTH, FEAT), 1.0, 6.0, ((0, 4), (1, 8))),
        "value_rows": centred(seeds[2], (SEQUENCE_COUNT, SEQUENCE_LENGTH, FEAT), 1.0, 6.0, ((0, 4), (1, 8))),
        "out_grad": noise_with(seeds[3], (SEQUENCE_COUNT, SEQUENCE_LENGTH, FEAT), 1.0, 6.0, ((0, 4), (1, 8)), (1, 2, 8, 2.0)),
        "log_decay": draw_log_decay(jax.random.fold_in(seeds[6], 71), 0),
        "norm_gain": jnp.clip(1.0 + 0.18 * jax.random.normal(seeds[5], (FEAT,), jnp.float32), 0.1, 1.9),
    }


EPSILON = 1e-06
HIGHEST = lax.Precision.HIGHEST

def rounded(values_in):
    return lax.optimization_barrier(values_in.astype(jnp.bfloat16)).astype(jnp.float32)

def decay_table(cumulative):
    positions = cumulative.shape[0]
    turned = jnp.transpose(cumulative)
    exponent = turned[:, :, None] - turned[:, None, :]
    row_ids = lax.broadcasted_iota(jnp.int32, (positions, positions), 0)
    col_ids = lax.broadcasted_iota(jnp.int32, (positions, positions), 1)
    return jnp.exp(jnp.where((row_ids >= col_ids)[None], exponent, -jnp.inf))

def ref_state(random_key_block, value_block, decay_block):
    cumulative = jnp.cumsum(decay_block, axis=0)
    block_log = cumulative[-1]
    shrink = jnp.exp(block_log[None, :] - cumulative)[:, :, None]
    key_late = rounded(random_key_block.astype(jnp.float32) * shrink)
    state_local = jnp.einsum('uhk,uhd->hkd', key_late, value_block.astype(jnp.float32), precision=HIGHEST)
    return (block_log, state_local)

def ref_main(query_block, random_key_block, value_block, grad_block, decay_block, incoming, norm_gain):
    positions, head_count, head_size = query_block.shape
    query_wide = query_block.astype(jnp.float32)
    key_wide = random_key_block.astype(jnp.float32)
    value_wide = value_block.astype(jnp.float32)
    cumulative = jnp.cumsum(decay_block, axis=0)
    growth = jnp.exp(cumulative)[:, :, None]
    decay = decay_table(cumulative)
    scores = jnp.einsum('thd,uhd->htu', query_wide, key_wide, precision=HIGHEST)
    fwd_weights = rounded(scores * decay)
    attended = jnp.einsum('htu,uhd->thd', fwd_weights, value_wide, precision=HIGHEST)
    attended = attended + jnp.einsum('thk,hkd->thd', query_wide * growth, incoming, precision=HIGHEST)
    attended = attended.reshape(positions, head_count * head_size)
    inverse = lax.rsqrt(lax.optimization_barrier(jnp.mean(attended * attended, axis=1, keepdims=True)) + EPSILON)
    normed = attended * inverse
    grad_wide = grad_block.astype(jnp.float32)
    scaled = norm_gain[None, :] * grad_wide
    projected = lax.optimization_barrier(jnp.mean(scaled * normed, axis=1, keepdims=True))
    out_delta = rounded(inverse * (scaled - normed * projected)).reshape(positions, head_count, head_size)
    delta_scores = jnp.einsum('thd,uhd->htu', out_delta, value_wide, precision=HIGHEST)
    bwd_weights = rounded(delta_scores * decay)
    query_early = rounded(query_wide * growth)
    moment = jnp.einsum('thk,thd->hkd', query_early, out_delta, precision=HIGHEST)
    query_grad = jnp.einsum('htu,uhd->thd', bwd_weights, key_wide, precision=HIGHEST)
    query_grad = query_grad + jnp.einsum('thd,hkd->thk', out_delta * growth, incoming, precision=HIGHEST)
    key_local = jnp.einsum('htu,thd->uhd', bwd_weights, query_wide, precision=HIGHEST)
    value_local = jnp.einsum('htu,thd->uhd', fwd_weights, out_delta, precision=HIGHEST)
    gain_term = lax.optimization_barrier(jnp.sum(grad_wide * normed, axis=0))
    return (query_grad.astype(jnp.bfloat16), key_local, value_local, moment, gain_term)

def ref_finish(random_key_block, value_block, decay_block, key_local, value_local, later):
    cumulative = jnp.cumsum(decay_block, axis=0)
    block_log = cumulative[-1]
    shrink = jnp.exp(block_log[None, :] - cumulative)[:, :, None]
    key_grad = key_local + jnp.einsum('uhd,hkd->uhk', value_block.astype(jnp.float32) * shrink, later, precision=HIGHEST)
    value_grad = value_local + jnp.einsum('uhk,hkd->uhd', random_key_block.astype(jnp.float32) * shrink, later, precision=HIGHEST)
    return (key_grad.astype(jnp.bfloat16), value_grad.astype(jnp.bfloat16))

def reference(queries, key_rows, value_rows, out_grad, log_decay, norm_gain):
    block_count = SEQUENCE_LENGTH // TOK_DEV
    query_list, key_list, value_list = ([], [], [])
    gain_total = jnp.zeros((FEAT,), jnp.float32)
    zeros_state = jnp.zeros((LOCAL_HEADS, HD, HD), jnp.float32)
    for sequence in range(SEQUENCE_COUNT):
        query_blocks = queries[sequence].reshape(block_count, TOK_DEV, LOCAL_HEADS, HD)
        key_blocks = key_rows[sequence].reshape(block_count, TOK_DEV, LOCAL_HEADS, HD)
        value_blocks = value_rows[sequence].reshape(block_count, TOK_DEV, LOCAL_HEADS, HD)
        grad_blocks = out_grad[sequence].reshape(block_count, TOK_DEV, FEAT)
        decay_blocks = log_decay[sequence].reshape(block_count, TOK_DEV, LOCAL_HEADS)
        block_logs, local_states = lax.map(lambda inputs: ref_state(*inputs), (key_blocks, value_blocks, decay_blocks))

        def forward_step(running, element):
            block_log, state_local = element
            return (jnp.exp(block_log)[:, None, None] * running + state_local, running)
        unused_end, incoming = lax.scan(forward_step, zeros_state, (block_logs, local_states))
        query_grad, key_local, value_local, moments, gain_terms = lax.map(lambda inputs: ref_main(*inputs, norm_gain), (query_blocks, key_blocks, value_blocks, grad_blocks, decay_blocks, incoming))

        def backward_step(running, element):
            block_log, moment = element
            return (moment + jnp.exp(block_log)[:, None, None] * running, running)
        unused_start, later = lax.scan(backward_step, zeros_state, (block_logs, moments), reverse=True)
        key_grad, value_grad = lax.map(lambda inputs: ref_finish(*inputs), (key_blocks, value_blocks, decay_blocks, key_local, value_local, later))
        query_list.append(query_grad.reshape(SEQUENCE_LENGTH, FEAT))
        key_list.append(key_grad.reshape(SEQUENCE_LENGTH, FEAT))
        value_list.append(value_grad.reshape(SEQUENCE_LENGTH, FEAT))
        gain_total = gain_total + lax.optimization_barrier(jnp.sum(gain_terms, axis=0))
    gain_grad = gain_total / jnp.sqrt(jnp.float32(SEQUENCE_COUNT * SEQUENCE_LENGTH))
    return (jnp.stack(query_list), jnp.stack(key_list), jnp.stack(value_list), gain_grad)
```

```python
import functools
import math

import jax
import jax.numpy as jnp
from jax import lax
from jax.experimental import pallas as pl
from jax.experimental.pallas import tpu as pltpu
from jax.sharding import PartitionSpec as P

EPSILON = 1e-06
F32 = jnp.float32
BF16 = jnp.bfloat16
LANES = 128
LAG = 3
LEAD = 2


def dot_nn(a, b):
    return lax.dot_general(a, b, (((1,), (0,)), ((), ())), preferred_element_type=F32)


def dot_nt(a, b):
    return lax.dot_general(a, b, (((1,), (1,)), ((), ())), preferred_element_type=F32)


def dot_tn(a, b):
    return lax.dot_general(a, b, (((0,), (0,)), ((), ())), preferred_element_type=F32)


def body(
    cfg,
    q_hbm, k_hbm, v_hbm, g_hbm, ld_ref, gain_ref,
    qg_ref, kg_ref, vg_ref, gg_ref,
    q_ref, k_ref, v_ref, g_ref, in_sem,
    cumc, cum_t, colb, att, vloc, fw, od_ref, acc_s, acc_p,
    gath, rows, coef, gp, gx, gy, gz,
    st_f, pr_f, tot_f, rx_f, sd_f, inc, pf_f,
    st_b, pr_b, tot_b, rx_b, sd_b, later, pf_b,
    ga_s, ga_r, gx_s, gx_r, gy_s, gy_r,
    d1s_f, d1r_f, xs_f, xr_f, d2s_f, d2r_f,
    d1s_b, d1r_b, xs_b, xr_b, d2s_b, d2r_b,
):
    n, n_dp, steps, heads = cfg["n"], cfg["n_dp"], cfg["steps"], cfg["heads"]
    half = heads // 2
    pos = q_ref.shape[0]
    feat = q_ref.shape[1]
    size = feat // heads
    width = feat // (n * n_dp)
    me = lax.axis_index("context")
    dp = lax.axis_index("dp")
    core = me % 2
    chip = me // 2
    mate = chip * 2 + (1 - core)

    barrier = pltpu.get_barrier_semaphore()
    for r in range(1, n):
        pl.semaphore_signal(barrier, inc=1, device_id={"context": (me + r) % n}, device_id_type=pl.DeviceIdType.MESH)
    for r in range(1, n_dp):
        pl.semaphore_signal(barrier, inc=1, device_id={"dp": (dp + r) % n_dp}, device_id_type=pl.DeviceIdType.MESH)

    loads = [
        pltpu.make_async_copy(src, dst, in_sem.at[i])
        for i, (src, dst) in enumerate(
            [(k_hbm, k_ref), (v_hbm, v_ref), (q_hbm, q_ref), (g_hbm, g_ref)]
        )
    ]
    for load in loads:
        load.start()

    def remote(src, dst, send, recv, **where):
        return pltpu.make_async_remote_copy(
            src_ref=src, dst_ref=dst, send_sem=send, recv_sem=recv,
            device_id=where, device_id_type=pl.DeviceIdType.MESH,
        )

    row_i = lax.broadcasted_iota(jnp.int32, (pos, pos), 0)
    col_i = lax.broadcasted_iota(jnp.int32, (pos, pos), 1)
    tri = jnp.where(row_i <= col_i, 1.0, 0.0).astype(F32)
    cum_t[...] = jnp.zeros_like(cum_t)
    cum_t[:heads, :] = lax.dot_general(
        ld_ref[...], tri, (((1,), (0,)), ((), ())),
        precision=lax.Precision.HIGHEST, preferred_element_type=F32,
    )
    cumc[...] = jnp.transpose(cum_t[...])
    cum = cumc[...]
    gath[me] = jnp.broadcast_to(cum[pos - 1 : pos, :], (8, LANES))
    pl.semaphore_wait(barrier, (n - 1) + (n_dp - 1))

    def gather_copy(r):
        return remote(gath.at[me], gath.at[me], ga_s.at[r], ga_r.at[r], context=(me + r) % n)

    def gather_wait(r):
        src = (me + n - r) % n
        return remote(gath.at[src], gath.at[src], ga_s.at[r], ga_r.at[r], context=(me + r) % n)

    for r in range(1, n):
        gather_copy(r).start()
    for h in range(heads):
        colb[h] = jnp.broadcast_to(cum[:, h : h + 1], (pos, LANES))
    loads[0].wait()
    loads[1].wait()

    def lanes(h):
        return pl.ds(pl.multiple_of(h * size, size), size)

    def column(h):
        return colb[h]

    def block_last(h):
        return colb[h, pos - 1 : pos, :]

    def decay_of(h):
        col = colb[h]
        wide = jnp.concatenate([col] * (-(-pos // LANES)), axis=1)[:, :pos]
        return jnp.exp(jnp.where(row_i >= col_i, wide - cum_t[pl.ds(h, 1), :], -jnp.inf))

    class Scan:
        def __init__(self, forward, st, pr, tot, rx, sd, result, pf, d1s, d1r, xs, xr, d2s, d2r):
            self.forward, self.st, self.pr, self.tot, self.rx = forward, st, pr, tot, rx
            self.sd, self.result, self.pf = sd, result, pf
            self.d1s, self.d1r, self.xs, self.xr, self.d2s, self.d2r = d1s, d1r, xs, xr, d2s, d2r
            self.first = (core == 0) if forward else (core == 1)
            self.base = 0 if forward else 6 + 3 * steps
            self.bits, self.partner, self.ups = [], [], []
            for s in range(steps):
                bit = (chip // (2**s)) % 2
                self.bits.append(bit)
                self.partner.append((chip + (1 - 2 * bit) * (2**s)) * 2 + core)
                self.ups.append((bit == 0) if forward else (bit == 1))

        def c(self, row, h):
            return coef[self.base + row, pl.ds(h, 1), :]

        def fill(self, last):
            ids = lax.broadcasted_iota(jnp.int32, last.shape, 0)
            chips = ids // 2

            def put(row, mask, keep=None):
                total = jnp.sum(jnp.where(mask, last, 0.0), axis=0, keepdims=True)
                value = jnp.exp(total)
                if keep is not None:
                    value = value * keep
                rows[self.base + row : self.base + row + 1, :] = value

            one = jnp.where(self.first, 1, 0)
            put(0, (ids == mate) & (one == 1))
            put(1, (ids == me) & (one == 0))
            put(2, (ids == mate) & (one == 0))
            put(3, (ids == me) & (one == 1))
            for s in range(steps):
                up = jnp.where(self.ups[s], 1, 0)
                mine = (chips // (2**s)) == (chip // (2**s))
                other = (chips // (2**s)) == ((self.partner[s] // 2) // (2**s))
                put(4 + 3 * s, other & (up == 1))
                put(5 + 3 * s, mine & (up == 0))
                ahead = (chips < chip) if self.forward else (chips > chip)
                put(6 + 3 * s, mine & ahead, keep=jnp.where(self.ups[s], 0.0, 1.0))
            if steps == 2:
                far, near = self.partner[1] // 2, self.partner[0] // 2

                def between(a, b):
                    return (chips > jnp.minimum(a, b)) & (chips < jnp.maximum(a, b))

                put(4 + 3 * steps, between(far, chip))
                put(5 + 3 * steps, between(far, near))

        def die1(self, k):
            return remote(self.st.at[(1 - core) * half + k], self.pr.at[k], self.d1s.at[k], self.d1r.at[k], context=mate)

        def link(self, s, k, slot=None):
            return remote(self.tot.at[s if slot is None else slot, k], self.rx.at[s, k], self.xs.at[s, k], self.xr.at[s, k], context=self.partner[s])

        def die2(self, k):
            return remote(self.sd.at[k], self.result.at[core * half + k], self.d2s.at[k], self.d2r.at[k], context=mate)

        def die2_in(self, k):
            return remote(self.sd.at[k], self.result.at[(1 - core) * half + k], self.d2s.at[k], self.d2r.at[k], context=mate)

        def send(self, s, k):
            if s < steps - 1:
                self.link(s, k).start()
            else:
                @pl.when(self.ups[s])
                def _():
                    self.link(s, k).start()

        def send_first(self, k):
            if steps != 2:
                self.send(0, k)
                return

            @pl.when(k % 2 == 0)
            def _():
                self.send(0, k)

            @pl.when((k % 2 == 1) & self.ups[1])
            def _():
                self.link(1, k, 0).start()

        def step(self, s, k):
            if steps != 2:
                self.stage(s, k)
                return
            h = core * half + k
            up0, up1 = self.ups[0], self.ups[1]
            down0, down1 = jnp.logical_not(up0), jnp.logical_not(up1)
            even, odd = k % 2 == 0, k % 2 == 1

            @pl.when(even)
            def _():
                self.stage(s, k)

            if s == 0:
                @pl.when(odd & up1 & up0)
                def _():
                    self.tot[1, k] = self.tot[0, k]
                    self.pf[k] = jnp.zeros_like(self.pf[k])

                @pl.when(odd & up1 & down0)
                def _():
                    self.pf[k] = jnp.zeros_like(self.pf[k])

                @pl.when(odd & down1)
                def _():
                    self.link(1, k, 0).wait_recv()
                    got = self.rx[1, k]
                    own = jnp.where(up0, 1.0, 0.0)
                    self.tot[1, k] = self.c(5 + 3 * steps, h) * got + own * self.tot[0, k]
                    self.pf[k] = self.c(4 + 3 * steps, h) * got

                @pl.when(odd & (up0 | down1))
                def _():
                    self.link(0, k, 1).start()
            else:
                @pl.when(odd & (down0 | down1))
                def _():
                    self.link(0, k, 1).wait_recv()
                    self.pf[k] = self.pf[k] + self.rx[0, k]

                @pl.when(odd)
                def _():
                    self.hand(k)

        def combine(self, k):
            h = core * half + k
            self.die1(k).wait_recv()
            self.tot[0, k] = self.c(0, h) * self.st[h] + self.c(1, h) * self.pr[k]
            self.send_first(k)

        def stage(self, s, k):
            h = core * half + k
            if s < steps - 1:
                self.link(s, k).wait_recv()
                got = self.rx[s, k]
                self.tot[s + 1, k] = self.c(4 + 3 * s, h) * self.tot[s, k] + self.c(5 + 3 * s, h) * got
                self.send(s + 1, k)
                part = self.c(6 + 3 * s, h) * got
                self.pf[k] = part if s == 0 else self.pf[k] + part
                return

            @pl.when(jnp.logical_not(self.ups[s]))
            def _():
                self.link(s, k).wait_recv()
                part = self.c(6 + 3 * s, h) * self.rx[s, k]
                self.pf[k] = part if s == 0 else self.pf[k] + part

            if s == 0:
                @pl.when(self.ups[s])
                def _():
                    self.pf[k] = jnp.zeros_like(self.pf[k])

            self.hand(k)

        def hand(self, k):
            h = core * half + k
            prefix = self.pf[k]
            head_first = jnp.where(self.first, 1.0, 0.0)
            self.sd[k] = self.c(3, h) * prefix + head_first * self.st[h]
            self.die2(k).start()
            self.result[h] = self.c(2, h) * prefix + (1.0 - head_first) * self.pr[k]

        def drain(self):
            def one(k, carry):
                self.die1(k).wait_send()
                self.die2(k).wait_send()
                even = (k % 2 == 0) | (steps != 2)

                @pl.when(even)
                def _():
                    for s in range(steps - 1):
                        self.link(s, k).wait_send()

                @pl.when(even & self.ups[steps - 1])
                def _():
                    self.link(steps - 1, k).wait_send()

                if steps == 2:
                    @pl.when((k % 2 == 1) & self.ups[1])
                    def _():
                        self.link(1, k, 0).wait_send()

                    @pl.when((k % 2 == 1) & (self.ups[0] | jnp.logical_not(self.ups[1])))
                    def _():
                        self.link(0, k, 1).wait_send()

                return carry

            lax.fori_loop(0, half, one, 0)

    fwd = Scan(True, st_f, pr_f, tot_f, rx_f, sd_f, inc, pf_f, d1s_f, d1r_f, xs_f, xr_f, d2s_f, d2r_f)
    bwd = Scan(False, st_b, pr_b, tot_b, rx_b, sd_b, later, pf_b, d1s_b, d1r_b, xs_b, xr_b, d2s_b, d2r_b)

    def guarded(k, run):
        @pl.when((k >= 0) & (k < half))
        def _():
            run(k)

    def own_state(h):
        shrink = jnp.exp(block_last(h) - column(h))
        late = (k_ref[:, lanes(h)].astype(F32) * shrink).astype(BF16)
        st_f[h] = dot_tn(late, v_ref[:, lanes(h)])

    def states(k):
        own_state((1 - core) * half + k)
        fwd.die1(k).start()
        own_state(core * half + k)

    def lead(k, carry):
        states(k)
        return carry

    lax.fori_loop(0, LEAD, lead, 0)
    for r in range(1, n):
        gather_wait(r).wait_recv()
    rows[...] = jnp.zeros_like(rows)
    last = gath[:, 0, :]
    fwd.fill(last)
    bwd.fill(last)
    turned = jnp.transpose(rows[...])
    for r in range(2 * (6 + 3 * steps)):
        coef[r] = jnp.broadcast_to(turned[:heads, r : r + 1], (heads, LANES))

    def rest(k, carry):
        guarded(k, states)
        fwd.combine(k - LEAD)
        return carry

    lax.fori_loop(LEAD, half + LEAD, rest, 0)
    acc_s[...] = jnp.zeros_like(acc_s)
    acc_p[...] = jnp.zeros_like(acc_p)

    def intra(h):
        s = dot_nt(q_ref[:, lanes(h)], k_ref[:, lanes(h)])
        w = (s * decay_of(h)).astype(BF16)
        fw[h] = w
        att[:, lanes(h)] = dot_nn(w, v_ref[:, lanes(h)])

    def scaled_of(h):
        return gain_ref[:, lanes(h)] * g_ref[:, lanes(h)].astype(F32)

    def inter(h):
        far = dot_nn(q_ref[:, lanes(h)], inc[h].astype(BF16))
        a = att[:, lanes(h)] + jnp.exp(column(h)) * far
        att[:, lanes(h)] = a
        acc_s[...] += a * a
        acc_p[...] += scaled_of(h) * a

    lags = [0, half] if steps == 2 else [LAG * s for s in range(steps)]
    lag_in = max(lags[-1] + LAG, half)

    def pass_loop(scan, local, finish, low=0, high=None):
        def one(it, carry):
            for s in range(steps):
                guarded(it - lags[s], functools.partial(scan.step, s))
            guarded(it, lambda k: local(core * half + k))
            guarded(it - half, lambda k: local((1 - core) * half + k))
            guarded(it - lags[-1], lambda k: finish(core * half + k))

            def arrived(k):
                scan.die2_in(k).wait_recv()
                finish((1 - core) * half + k)

            guarded(it - lag_in, arrived)
            return carry

        lax.fori_loop(low, half + lag_in if high is None else high, one, 0)

    loads[2].wait()
    loads[3].wait()
    pass_loop(fwd, intra, inter)

    mean_sq = jnp.sum(acc_s[...], axis=1, keepdims=True) * (1.0 / feat)
    inverse = lax.rsqrt(mean_sq + EPSILON)
    proj = inverse * (jnp.sum(acc_p[...], axis=1, keepdims=True) * (1.0 / feat))
    acc_s[...] = jnp.broadcast_to(inverse, acc_s.shape)
    acc_p[...] = jnp.broadcast_to(proj, acc_p.shape)

    def delta(h):
        inv = acc_s[...]
        normed = att[:, lanes(h)] * inv
        wide = g_ref[:, lanes(h)].astype(F32)
        scaled = gain_ref[:, lanes(h)] * wide
        od = (inv * (scaled - normed * acc_p[...])).astype(BF16)
        od_ref[:, lanes(h)] = od
        gp[:, lanes(h)] = jnp.sum((wide * normed).reshape(pos // 8, 8, size), axis=0)
        early = (q_ref[:, lanes(h)].astype(F32) * jnp.exp(column(h))).astype(BF16)
        st_b[h] = dot_tn(early, od)

    def deltas(k):
        delta((1 - core) * half + k)
        bwd.die1(k).start()
        delta(core * half + k)

    def back(k, carry):
        guarded(k, deltas)
        guarded(k - LEAD, bwd.combine)
        return carry

    lax.fori_loop(0, half + LEAD, back, 0)

    part = feat // n_dp

    def gx_copy(r):
        to = (dp + r) % n_dp
        return remote(gp.at[:, pl.ds(pl.multiple_of(to * part, LANES), part)], gx.at[r], gx_s.at[r], gx_r.at[r], dp=to)

    for r in range(1, n_dp):
        gx_copy(r).start()

    def local_back(h):
        od = od_ref[:, lanes(h)]
        q = q_ref[:, lanes(h)]
        key = k_ref[:, lanes(h)]
        bw = (dot_nt(od, v_ref[:, lanes(h)]) * decay_of(h)).astype(BF16)
        far = dot_nt(od, inc[h].astype(BF16))
        qg_ref[:, lanes(h)] = (dot_nn(bw, key) + jnp.exp(column(h)) * far).astype(BF16)
        att[:, lanes(h)] = dot_tn(bw, q)
        vloc[:, lanes(h)] = dot_tn(fw[h], od)

    def finish_back(h):
        shrink = jnp.exp(block_last(h) - column(h))
        lt = later[h].astype(BF16)
        kg_ref[:, lanes(h)] = (att[:, lanes(h)] + shrink * dot_nt(v_ref[:, lanes(h)], lt)).astype(BF16)
        vg_ref[:, lanes(h)] = (vloc[:, lanes(h)] + shrink * dot_nn(k_ref[:, lanes(h)], lt)).astype(BF16)

    pass_loop(bwd, local_back, finish_back, 0, half // 2)
    for r in range(1, n_dp):
        gx_copy(r).wait_recv()
    total = gp[:, pl.ds(pl.multiple_of(dp * part, LANES), part)]
    for r in range(1, n_dp):
        total = total + gx[r]
    total = jnp.sum(total, axis=0, keepdims=True)
    for i in range(n):
        gy[i] = jnp.broadcast_to(total[:, i * width : (i + 1) * width], (8, width))

    def gy_copy(r):
        return remote(gy.at[(me + r) % n], gz.at[r], gy_s.at[r], gy_r.at[r], context=(me + r) % n)

    for r in range(1, n):
        gy_copy(r).start()

    pass_loop(bwd, local_back, finish_back, half // 2)

    out = gy[me]
    for r in range(1, n):
        gy_copy(r).wait_recv()
        out = out + gz[r]
    gg_ref[...] = out[0:1, :] * cfg["norm"]

    for r in range(1, n):
        gather_copy(r).wait_send()
        gy_copy(r).wait_send()
    for r in range(1, n_dp):
        gx_copy(r).wait_send()
    fwd.drain()
    bwd.drain()


def settle(count, *refs):
    srcs, dsts, sems = refs[:count], refs[count : 2 * count], refs[2 * count]
    copies = [pltpu.make_async_copy(srcs[i], dsts[i], sems.at[i]) for i in range(count)]
    for copy in copies:
        copy.start()
    for copy in copies:
        copy.wait()


def settled(arrays):
    count = len(arrays)
    return pl.pallas_call(
        functools.partial(settle, count),
        out_shape=tuple(jax.ShapeDtypeStruct(a.shape, a.dtype) for a in arrays),
        in_specs=[pl.BlockSpec(memory_space=pltpu.VMEM)] * count,
        out_specs=(pl.BlockSpec(memory_space=pl.ANY),) * count,
        scratch_shapes=[pltpu.SemaphoreType.DMA((count,))],
        compiler_params=pltpu.CompilerParams(vmem_limit_bytes=1 << 20),
    )(*[pltpu.with_memory_space_constraint(a, pltpu.VMEM) for a in arrays])


def per_device(queries, key_rows, value_rows, out_grad, log_decay, norm_gain):
    pos, feat = queries.shape[1:]
    heads = log_decay.shape[2]
    size = feat // heads
    half = heads // 2
    n, n_dp = lax.axis_size("context"), lax.axis_size("dp")
    steps = (n // 2).bit_length() - 1
    width = feat // (n * n_dp)
    cfg = dict(n=n, n_dp=n_dp, steps=steps, heads=heads, norm=1.0 / math.sqrt(pos * n * n_dp))
    vmem = pl.BlockSpec(memory_space=pltpu.VMEM)
    sem = pltpu.SemaphoreType.DMA

    def scan_buffers():
        return [
            pltpu.VMEM((heads, size, size), F32),
            pltpu.VMEM((half, size, size), F32),
            pltpu.VMEM((steps, half, size, size), F32),
            pltpu.VMEM((steps, half, size, size), F32),
            pltpu.VMEM((half, size, size), F32),
            pltpu.VMEM((heads, size, size), F32),
            pltpu.VMEM((half, size, size), F32),
        ]

    def scan_sems():
        return [sem((half,)), sem((half,)), sem((steps, half)), sem((steps, half)), sem((half,)), sem((half,))]

    rows_bf = pltpu.VMEM((pos, feat), BF16)
    scratch = [
        *([rows_bf] * 4), sem((4,)),
        pltpu.VMEM((pos, LANES), F32),
        pltpu.VMEM((LANES, pos), F32),
        pltpu.VMEM((heads, pos, LANES), F32),
        pltpu.VMEM((pos, feat), F32),
        pltpu.VMEM((pos, feat), F32),
        pltpu.VMEM((heads, pos, pos), BF16),
        pltpu.VMEM((pos, feat), BF16),
        pltpu.VMEM((pos, LANES), F32),
        pltpu.VMEM((pos, LANES), F32),
        pltpu.VMEM((n, 8, LANES), F32),
        pltpu.VMEM((LANES, LANES), F32),
        pltpu.VMEM((2 * (6 + 3 * steps), heads, LANES), F32),
        pltpu.VMEM((8, feat), F32),
        pltpu.VMEM((n_dp, 8, feat // n_dp), F32),
        pltpu.VMEM((n, 8, width), F32),
        pltpu.VMEM((n, 8, width), F32),
        *scan_buffers(),
        *scan_buffers(),
        sem((n,)), sem((n,)), sem((n_dp,)), sem((n_dp,)), sem((n,)), sem((n,)),
        *scan_sems(),
        *scan_sems(),
    ]
    grid_out = pltpu.VMEM((pos, feat), BF16)
    spare = 3 * pos * feat * 2 + (1 << 20)
    qg, kg, vg, gg = pl.pallas_call(
        functools.partial(body, cfg),
        out_shape=(grid_out, grid_out, grid_out, pltpu.VMEM((1, width), F32)),
        in_specs=[pl.BlockSpec(memory_space=pl.ANY)] * 4 + [vmem] * 2,
        out_specs=(vmem,) * 4,
        scratch_shapes=scratch,
        compiler_params=pltpu.CompilerParams(
            collective_id=0, has_side_effects=True, vmem_limit_bytes=67043328 - spare
        ),
    )(queries[0], key_rows[0], value_rows[0], out_grad[0], log_decay[0].T, norm_gain[None])
    qg, kg, vg, gg = settled((qg, kg, vg, gg))
    return qg[None], kg[None], vg[None], gg[0]


def solution(mesh):
    rows = P("dp", "context", None)
    return jax.shard_map(
        per_device,
        mesh=mesh,
        in_specs=(rows,) * 5 + (P(),),
        out_specs=(rows, rows, rows, P(("dp", "context"))),
        check_vma=False,
    )
```

```python
import functools
import math

import jax
import jax.numpy as jnp
from jax import lax
from jax.experimental import pallas as pl
from jax.experimental.pallas import tpu as pltpu
from jax.sharding import PartitionSpec as P

EPSILON = 1e-06
F32 = jnp.float32
BF16 = jnp.bfloat16
LANES = 128
LAG = 3
LEAD = 2


def dot_nn(a, b):
    return lax.dot_general(a, b, (((1,), (0,)), ((), ())), preferred_element_type=F32)


def dot_nt(a, b):
    return lax.dot_general(a, b, (((1,), (1,)), ((), ())), preferred_element_type=F32)


def dot_tn(a, b):
    return lax.dot_general(a, b, (((0,), (0,)), ((), ())), preferred_element_type=F32)


def body(
    cfg,
    q_hbm, k_hbm, v_hbm, g_hbm, ld_ref, gain_ref,
    qg_ref, kg_ref, vg_ref, gg_ref,
    q_ref, k_ref, v_ref, g_ref, in_sem,
    cumc, cum_t, colb, att, vloc, fw, od_ref, acc_s, acc_p,
    gath, rows, coef, gp, gx, gy, gz,
    st_f, pr_f, tot_f, rx_f, sd_f, inc, pf_f,
    st_b, pr_b, tot_b, rx_b, sd_b, later, pf_b,
    ga_s, ga_r, gx_s, gx_r, gy_s, gy_r,
    d1s_f, d1r_f, xs_f, xr_f, d2s_f, d2r_f,
    d1s_b, xs_b, xr_b, d2s_b,
):
    n, n_dp, steps, heads = cfg["n"], cfg["n_dp"], cfg["steps"], cfg["heads"]
    half = heads // 2
    pos = q_ref.shape[0]
    feat = q_ref.shape[1]
    size = feat // heads
    width = feat // (n * n_dp)
    me = lax.axis_index("context")
    dp = lax.axis_index("dp")
    core = me % 2
    chip = me // 2
    mate = chip * 2 + (1 - core)

    barrier = pltpu.get_barrier_semaphore()
    for r in range(1, n):
        pl.semaphore_signal(barrier, inc=1, device_id={"context": (me + r) % n}, device_id_type=pl.DeviceIdType.MESH)
    for r in range(1, n_dp):
        pl.semaphore_signal(barrier, inc=1, device_id={"dp": (dp + r) % n_dp}, device_id_type=pl.DeviceIdType.MESH)

    loads = [
        pltpu.make_async_copy(src, dst, in_sem.at[i])
        for i, (src, dst) in enumerate(
            [(k_hbm, k_ref), (v_hbm, v_ref), (q_hbm, q_ref), (g_hbm, g_ref)]
        )
    ]
    for load in loads:
        load.start()

    def remote(src, dst, send, recv, **where):
        return pltpu.make_async_remote_copy(
            src_ref=src, dst_ref=dst, send_sem=send, recv_sem=recv,
            device_id=where, device_id_type=pl.DeviceIdType.MESH,
        )

    row_i = lax.broadcasted_iota(jnp.int32, (pos, pos), 0)
    col_i = lax.broadcasted_iota(jnp.int32, (pos, pos), 1)
    tri = jnp.where(row_i <= col_i, 1.0, 0.0).astype(F32)
    cum_t[...] = jnp.zeros_like(cum_t)
    cum_t[:heads, :] = lax.dot_general(
        ld_ref[...], tri, (((1,), (0,)), ((), ())),
        precision=lax.Precision.HIGHEST, preferred_element_type=F32,
    )
    cumc[...] = jnp.transpose(cum_t[...])
    cum = cumc[...]
    gath[me] = jnp.broadcast_to(cum[pos - 1 : pos, :], (8, LANES))
    pl.semaphore_wait(barrier, (n - 1) + (n_dp - 1))

    def gather_copy(r):
        return remote(gath.at[me], gath.at[me], ga_s, ga_r, context=(me + r) % n)

    def gather_all():
        span = gath.at[pl.ds(0, n - 1)]
        return remote(span, span, ga_s, ga_r, context=mate)

    for r in range(1, n):
        gather_copy(r).start()
    for h in range(heads):
        colb[h] = jnp.broadcast_to(cum[:, h : h + 1], (pos, LANES))
    loads[0].wait()
    loads[1].wait()

    def lanes(h):
        return pl.ds(pl.multiple_of(h * size, size), size)

    def column(h):
        return colb[h]

    def block_last(h):
        return colb[h, pos - 1 : pos, :]

    def decay_of(h):
        col = colb[h]
        wide = jnp.concatenate([col] * (-(-pos // LANES)), axis=1)[:, :pos]
        return jnp.exp(jnp.where(row_i >= col_i, wide - cum_t[pl.ds(h, 1), :], -jnp.inf))

    class Scan:
        def __init__(self, forward, st, pr, tot, rx, sd, result, pf, d1s, d1r, xs, xr, d2s, d2r):
            self.forward, self.st, self.pr, self.tot, self.rx = forward, st, pr, tot, rx
            self.sd, self.result, self.pf = sd, result, pf
            self.d1s, self.d1r, self.xs, self.xr, self.d2s, self.d2r = d1s, d1r, xs, xr, d2s, d2r
            self.first = (core == 0) if forward else (core == 1)
            self.base = 0 if forward else 6 + 3 * steps
            self.bits, self.partner, self.ups = [], [], []
            for s in range(steps):
                bit = (chip // (2**s)) % 2
                self.bits.append(bit)
                self.partner.append((chip + (1 - 2 * bit) * (2**s)) * 2 + core)
                self.ups.append((bit == 0) if forward else (bit == 1))

        def c(self, row, h):
            return coef[self.base + row, pl.ds(h, 1), :]

        def fill(self, last):
            ids = lax.broadcasted_iota(jnp.int32, last.shape, 0)
            chips = ids // 2

            def put(row, mask, keep=None):
                total = jnp.sum(jnp.where(mask, last, 0.0), axis=0, keepdims=True)
                value = jnp.exp(total)
                if keep is not None:
                    value = value * keep
                rows[self.base + row : self.base + row + 1, :] = value

            one = jnp.where(self.first, 1, 0)
            put(0, (ids == mate) & (one == 1))
            put(1, (ids == me) & (one == 0))
            put(2, (ids == mate) & (one == 0))
            put(3, (ids == me) & (one == 1))
            for s in range(steps):
                up = jnp.where(self.ups[s], 1, 0)
                mine = (chips // (2**s)) == (chip // (2**s))
                other = (chips // (2**s)) == ((self.partner[s] // 2) // (2**s))
                put(4 + 3 * s, other & (up == 1))
                put(5 + 3 * s, mine & (up == 0))
                ahead = (chips < chip) if self.forward else (chips > chip)
                put(6 + 3 * s, mine & ahead, keep=jnp.where(self.ups[s], 0.0, 1.0))
            if steps == 2:
                far, near = self.partner[1] // 2, self.partner[0] // 2

                def between(a, b):
                    return (chips > jnp.minimum(a, b)) & (chips < jnp.maximum(a, b))

                put(4 + 3 * steps, between(far, chip))
                put(5 + 3 * steps, between(far, near))

        def die1(self, k):
            return remote(self.st.at[(1 - core) * half + k], self.pr.at[k], self.d1s, self.d1r.at[k], context=mate)

        def link(self, s, k, slot=None):
            group = self.xs.at[steps if slot == 1 else s]
            return remote(self.tot.at[s if slot is None else slot, k], self.rx.at[s, k], group, self.xr.at[s, k], context=self.partner[s])

        def sent(self, group, count):
            span = self.rx.at[0, pl.ds(0, count)]
            return remote(span, span, self.xs.at[group], self.xr.at[0, 0], context=mate)

        def die2(self, k):
            return remote(self.sd.at[k], self.result.at[core * half + k], self.d2s, self.d2r.at[k], context=mate)

        def die2_in(self, k):
            return remote(self.sd.at[k], self.result.at[(1 - core) * half + k], self.d2s, self.d2r.at[k], context=mate)

        def send(self, s, k):
            if s < steps - 1:
                self.link(s, k).start()
            else:
                @pl.when(self.ups[s])
                def _():
                    self.link(s, k).start()

        def send_first(self, k):
            if steps != 2:
                self.send(0, k)
                return

            @pl.when(k % 2 == 0)
            def _():
                self.send(0, k)

            @pl.when((k % 2 == 1) & self.ups[1])
            def _():
                self.link(1, k, 0).start()

        def step(self, s, k):
            if steps != 2:
                self.stage(s, k)
                return
            h = core * half + k
            up0, up1 = self.ups[0], self.ups[1]
            down0, down1 = jnp.logical_not(up0), jnp.logical_not(up1)
            even, odd = k % 2 == 0, k % 2 == 1

            @pl.when(even)
            def _():
                self.stage(s, k)

            if s == 0:
                @pl.when(odd & up1 & up0)
                def _():
                    self.tot[1, k] = self.tot[0, k]
                    self.pf[k] = jnp.zeros_like(self.pf[k])

                @pl.when(odd & up1 & down0)
                def _():
                    self.pf[k] = jnp.zeros_like(self.pf[k])

                @pl.when(odd & down1)
                def _():
                    self.link(1, k, 0).wait_recv()
                    got = self.rx[1, k]
                    own = jnp.where(up0, 1.0, 0.0)
                    self.tot[1, k] = self.c(5 + 3 * steps, h) * got + own * self.tot[0, k]
                    self.pf[k] = self.c(4 + 3 * steps, h) * got

                @pl.when(odd & (up0 | down1))
                def _():
                    self.link(0, k, 1).start()
            else:
                @pl.when(odd & (down0 | down1))
                def _():
                    self.link(0, k, 1).wait_recv()
                    self.pf[k] = self.pf[k] + self.rx[0, k]

                @pl.when(odd)
                def _():
                    self.hand(k)

        def combine(self, k):
            h = core * half + k
            self.die1(k).wait_recv()
            self.tot[0, k] = self.c(0, h) * self.st[h] + self.c(1, h) * self.pr[k]
            self.send_first(k)

        def stage(self, s, k):
            h = core * half + k
            if s < steps - 1:
                self.link(s, k).wait_recv()
                got = self.rx[s, k]
                self.tot[s + 1, k] = self.c(4 + 3 * s, h) * self.tot[s, k] + self.c(5 + 3 * s, h) * got
                self.send(s + 1, k)
                part = self.c(6 + 3 * s, h) * got
                self.pf[k] = part if s == 0 else self.pf[k] + part
                return

            @pl.when(jnp.logical_not(self.ups[s]))
            def _():
                self.link(s, k).wait_recv()
                part = self.c(6 + 3 * s, h) * self.rx[s, k]
                self.pf[k] = part if s == 0 else self.pf[k] + part

            if s == 0:
                @pl.when(self.ups[s])
                def _():
                    self.pf[k] = jnp.zeros_like(self.pf[k])

            self.hand(k)

        def hand(self, k):
            h = core * half + k
            prefix = self.pf[k]
            head_first = jnp.where(self.first, 1.0, 0.0)
            self.sd[k] = self.c(3, h) * prefix + head_first * self.st[h]
            self.die2(k).start()
            self.result[h] = self.c(2, h) * prefix + (1.0 - head_first) * self.pr[k]

        def drain(self):
            for group in (self.d1s, self.d2s):
                remote(self.sd, self.sd, group, self.d1r.at[0], context=mate).wait_send()
            if steps != 2:
                for s in range(steps - 1):
                    self.sent(s, half).wait_send()

                @pl.when(self.ups[steps - 1])
                def _():
                    self.sent(steps - 1, half).wait_send()

                return
            self.sent(0, half // 2).wait_send()

            @pl.when(self.ups[1])
            def _():
                self.sent(1, half).wait_send()

            @pl.when(self.ups[0] | jnp.logical_not(self.ups[1]))
            def _():
                self.sent(2, half // 2).wait_send()

    fwd = Scan(True, st_f, pr_f, tot_f, rx_f, sd_f, inc, pf_f, d1s_f, d1r_f, xs_f, xr_f, d2s_f, d2r_f)
    bwd = Scan(False, st_b, pr_b, tot_b, rx_b, sd_b, later, pf_b, d1s_b, d1r_f, xs_b, xr_b, d2s_b, d2r_f)

    def guarded(k, run):
        @pl.when((k >= 0) & (k < half))
        def _():
            run(k)

    def own_state(h):
        shrink = jnp.exp(block_last(h) - column(h))
        late = (k_ref[:, lanes(h)].astype(F32) * shrink).astype(BF16)
        st_f[h] = dot_tn(late, v_ref[:, lanes(h)])

    def states(k):
        own_state((1 - core) * half + k)
        fwd.die1(k).start()
        own_state(core * half + k)

    def lead(k, carry):
        states(k)
        return carry

    lax.fori_loop(0, LEAD, lead, 0)
    gather_all().wait_recv()
    rows[...] = jnp.zeros_like(rows)
    last = gath[:, 0, :]
    fwd.fill(last)
    bwd.fill(last)
    turned = jnp.transpose(rows[...])
    for r in range(2 * (6 + 3 * steps)):
        coef[r] = jnp.broadcast_to(turned[:heads, r : r + 1], (heads, LANES))

    def rest(k, carry):
        guarded(k, states)
        fwd.combine(k - LEAD)
        return carry

    lax.fori_loop(LEAD, half + LEAD, rest, 0)
    acc_s[...] = jnp.zeros_like(acc_s)
    acc_p[...] = jnp.zeros_like(acc_p)

    def intra(h):
        s = dot_nt(q_ref[:, lanes(h)], k_ref[:, lanes(h)])
        w = (s * decay_of(h)).astype(BF16)
        fw[h] = w
        att[:, lanes(h)] = dot_nn(w, v_ref[:, lanes(h)])

    def scaled_of(h):
        return gain_ref[:, lanes(h)] * g_ref[:, lanes(h)].astype(F32)

    def inter(h):
        far = dot_nn(q_ref[:, lanes(h)], inc[h].astype(BF16))
        a = att[:, lanes(h)] + jnp.exp(column(h)) * far
        att[:, lanes(h)] = a
        acc_s[...] += a * a
        acc_p[...] += scaled_of(h) * a

    lags = [0, half] if steps == 2 else [LAG * s for s in range(steps)]
    lag_in = max(lags[-1] + LAG, half)

    def pass_loop(scan, local, finish, low=0, high=None):
        def one(it, carry):
            for s in range(steps):
                guarded(it - lags[s], functools.partial(scan.step, s))
            guarded(it, lambda k: local(core * half + k))
            guarded(it - half, lambda k: local((1 - core) * half + k))
            guarded(it - lags[-1], lambda k: finish(core * half + k))

            def arrived(k):
                scan.die2_in(k).wait_recv()
                finish((1 - core) * half + k)

            guarded(it - lag_in, arrived)
            return carry

        lax.fori_loop(low, half + lag_in if high is None else high, one, 0)

    loads[2].wait()
    loads[3].wait()
    pass_loop(fwd, intra, inter)

    mean_sq = jnp.sum(acc_s[...], axis=1, keepdims=True) * (1.0 / feat)
    inverse = lax.rsqrt(mean_sq + EPSILON)
    proj = inverse * (jnp.sum(acc_p[...], axis=1, keepdims=True) * (1.0 / feat))
    acc_s[...] = jnp.broadcast_to(inverse, acc_s.shape)
    acc_p[...] = jnp.broadcast_to(proj, acc_p.shape)

    def delta(h):
        inv = acc_s[...]
        normed = att[:, lanes(h)] * inv
        wide = g_ref[:, lanes(h)].astype(F32)
        scaled = gain_ref[:, lanes(h)] * wide
        od = (inv * (scaled - normed * acc_p[...])).astype(BF16)
        od_ref[:, lanes(h)] = od
        gp[:, lanes(h)] = jnp.sum((wide * normed).reshape(pos // 8, 8, size), axis=0)
        early = (q_ref[:, lanes(h)].astype(F32) * jnp.exp(column(h))).astype(BF16)
        st_b[h] = dot_tn(early, od)

    def deltas(k):
        delta((1 - core) * half + k)
        bwd.die1(k).start()
        delta(core * half + k)

    def back(k, carry):
        guarded(k, deltas)
        guarded(k - LEAD, bwd.combine)
        return carry

    lax.fori_loop(0, half + LEAD, back, 0)

    part = feat // n_dp

    def gx_copy(r):
        to = (dp + r) % n_dp
        return remote(gp.at[:, pl.ds(pl.multiple_of(to * part, LANES), part)], gx.at[r], gx_s, gx_r, dp=to)

    def gx_all():
        span = gx.at[pl.ds(1, n_dp - 1)]
        return remote(span, span, gx_s, gx_r, dp=(dp + 1) % n_dp)

    for r in range(1, n_dp):
        gx_copy(r).start()

    def local_back(h):
        od = od_ref[:, lanes(h)]
        q = q_ref[:, lanes(h)]
        key = k_ref[:, lanes(h)]
        bw = (dot_nt(od, v_ref[:, lanes(h)]) * decay_of(h)).astype(BF16)
        far = dot_nt(od, inc[h].astype(BF16))
        qg_ref[:, lanes(h)] = (dot_nn(bw, key) + jnp.exp(column(h)) * far).astype(BF16)
        att[:, lanes(h)] = dot_tn(bw, q)
        vloc[:, lanes(h)] = dot_tn(fw[h], od)

    def finish_back(h):
        shrink = jnp.exp(block_last(h) - column(h))
        lt = later[h].astype(BF16)
        kg_ref[:, lanes(h)] = (att[:, lanes(h)] + shrink * dot_nt(v_ref[:, lanes(h)], lt)).astype(BF16)
        vg_ref[:, lanes(h)] = (vloc[:, lanes(h)] + shrink * dot_nn(k_ref[:, lanes(h)], lt)).astype(BF16)

    pass_loop(bwd, local_back, finish_back, 0, half // 2)
    if n_dp > 1:
        gx_all().wait_recv()
    total = gp[:, pl.ds(pl.multiple_of(dp * part, LANES), part)]
    for r in range(1, n_dp):
        total = total + gx[r]
    total = jnp.sum(total, axis=0, keepdims=True)
    for i in range(n):
        gy[i] = jnp.broadcast_to(total[:, i * width : (i + 1) * width], (8, width))

    def gy_copy(r):
        return remote(gy.at[(me + r) % n], gz.at[r], gy_s, gy_r, context=(me + r) % n)

    def gy_all():
        span = gz.at[pl.ds(1, n - 1)]
        return remote(span, span, gy_s, gy_r, context=mate)

    for r in range(1, n):
        gy_copy(r).start()

    pass_loop(bwd, local_back, finish_back, half // 2)

    out = gy[me]
    gy_all().wait_recv()
    for r in range(1, n):
        out = out + gz[r]
    gg_ref[...] = out[0:1, :] * cfg["norm"]

    gather_all().wait_send()
    gy_all().wait_send()
    if n_dp > 1:
        gx_all().wait_send()
    fwd.drain()
    bwd.drain()


def settle(count, *refs):
    srcs, dsts, sems = refs[:count], refs[count : 2 * count], refs[2 * count]
    copies = [pltpu.make_async_copy(srcs[i], dsts[i], sems.at[i]) for i in range(count)]
    for copy in copies:
        copy.start()
    for copy in copies:
        copy.wait()


def settled(arrays):
    count = len(arrays)
    return pl.pallas_call(
        functools.partial(settle, count),
        out_shape=tuple(jax.ShapeDtypeStruct(a.shape, a.dtype) for a in arrays),
        in_specs=[pl.BlockSpec(memory_space=pltpu.VMEM)] * count,
        out_specs=(pl.BlockSpec(memory_space=pl.ANY),) * count,
        scratch_shapes=[pltpu.SemaphoreType.DMA((count,))],
        compiler_params=pltpu.CompilerParams(vmem_limit_bytes=1 << 20),
    )(*[pltpu.with_memory_space_constraint(a, pltpu.VMEM) for a in arrays])


def per_device(queries, key_rows, value_rows, out_grad, log_decay, norm_gain):
    pos, feat = queries.shape[1:]
    heads = log_decay.shape[2]
    size = feat // heads
    half = heads // 2
    n, n_dp = lax.axis_size("context"), lax.axis_size("dp")
    steps = (n // 2).bit_length() - 1
    width = feat // (n * n_dp)
    cfg = dict(n=n, n_dp=n_dp, steps=steps, heads=heads, norm=1.0 / math.sqrt(pos * n * n_dp))
    vmem = pl.BlockSpec(memory_space=pltpu.VMEM)
    sem = pltpu.SemaphoreType.DMA

    def scan_buffers():
        return [
            pltpu.VMEM((heads, size, size), F32),
            pltpu.VMEM((half, size, size), F32),
            pltpu.VMEM((steps, half, size, size), F32),
            pltpu.VMEM((steps, half, size, size), F32),
            pltpu.VMEM((half, size, size), F32),
            pltpu.VMEM((heads, size, size), F32),
            pltpu.VMEM((half, size, size), F32),
        ]

    def scan_sems():
        return [sem(()), sem((half,)), sem((steps + 1,)), sem((steps, half)), sem(()), sem((half,))]

    rows_bf = pltpu.VMEM((pos, feat), BF16)
    scratch = [
        *([rows_bf] * 4), sem((4,)),
        pltpu.VMEM((pos, LANES), F32),
        pltpu.VMEM((LANES, pos), F32),
        pltpu.VMEM((heads, pos, LANES), F32),
        pltpu.VMEM((pos, feat), F32),
        pltpu.VMEM((pos, feat), F32),
        pltpu.VMEM((heads, pos, pos), BF16),
        pltpu.VMEM((pos, feat), BF16),
        pltpu.VMEM((pos, LANES), F32),
        pltpu.VMEM((pos, LANES), F32),
        pltpu.VMEM((n, 8, LANES), F32),
        pltpu.VMEM((LANES, LANES), F32),
        pltpu.VMEM((2 * (6 + 3 * steps), heads, LANES), F32),
        pltpu.VMEM((8, feat), F32),
        pltpu.VMEM((n_dp, 8, feat // n_dp), F32),
        pltpu.VMEM((n, 8, width), F32),
        pltpu.VMEM((n, 8, width), F32),
        *scan_buffers(),
        *scan_buffers(),
        *[sem(())] * 6,
        *scan_sems(),
        *[scan_sems()[i] for i in (0, 2, 3, 4)],
    ]
    grid_out = pltpu.VMEM((pos, feat), BF16)
    spare = 3 * pos * feat * 2 + (1 << 20)
    qg, kg, vg, gg = pl.pallas_call(
        functools.partial(body, cfg),
        out_shape=(grid_out, grid_out, grid_out, pltpu.VMEM((1, width), F32)),
        in_specs=[pl.BlockSpec(memory_space=pl.ANY)] * 4 + [vmem] * 2,
        out_specs=(vmem,) * 4,
        scratch_shapes=scratch,
        compiler_params=pltpu.CompilerParams(
            collective_id=0, has_side_effects=True, vmem_limit_bytes=67043328 - spare
        ),
    )(queries[0], key_rows[0], value_rows[0], out_grad[0], log_decay[0].T, norm_gain[None])
    qg, kg, vg, gg = settled((qg, kg, vg, gg))
    return qg[None], kg[None], vg[None], gg[0]


def solution(mesh):
    rows = P("dp", "context", None)
    return jax.shard_map(
        per_device,
        mesh=mesh,
        in_specs=(rows,) * 5 + (P(),),
        out_specs=(rows, rows, rows, P(("dp", "context"))),
        check_vma=False,
    )
```

```python
import functools
import math

import jax
import jax.numpy as jnp
from jax import lax
from jax.experimental import pallas as pl
from jax.experimental.pallas import tpu as pltpu
from jax.sharding import PartitionSpec as P

EPSILON = 1e-06
F32 = jnp.float32
BF16 = jnp.bfloat16
LANES = 128
LAG = 2
LEAD = 2


def dot_nn(a, b):
    return lax.dot_general(a, b, (((1,), (0,)), ((), ())), preferred_element_type=F32)


def dot_nt(a, b):
    return lax.dot_general(a, b, (((1,), (1,)), ((), ())), preferred_element_type=F32)


def dot_tn(a, b):
    return lax.dot_general(a, b, (((0,), (0,)), ((), ())), preferred_element_type=F32)


def body(
    cfg,
    q_hbm, k_hbm, v_hbm, g_hbm, ld_ref, gain_ref,
    qg_ref, kg_ref, vg_ref, gg_ref,
    q_ref, k_ref, v_ref, g_ref, in_sem,
    cumc, cum_t, colb, att, vloc, fw, od_ref, acc_s, acc_p,
    gath, rows, coef, gp, gx, gy, gz,
    st_f, pr_f, tot_f, rx_f, sd_f, inc, pf_f,
    st_b, pr_b, tot_b, rx_b, sd_b, later, pf_b,
    ga_s, ga_r, gx_s, gx_r, gy_s, gy_r,
    d1s_f, d1r_f, xs_f, xr_f, d2s_f, d2r_f,
    d1s_b, xs_b, xr_b, d2s_b,
):
    n, n_dp, steps, heads = cfg["n"], cfg["n_dp"], cfg["steps"], cfg["heads"]
    half = heads // 2
    pos = q_ref.shape[0]
    feat = q_ref.shape[1]
    size = feat // heads
    width = feat // (n * n_dp)
    me = lax.axis_index("context")
    dp = lax.axis_index("dp")
    core = me % 2
    chip = me // 2
    mate = chip * 2 + (1 - core)

    barrier = pltpu.get_barrier_semaphore()
    for r in range(1, n):
        pl.semaphore_signal(barrier, inc=1, device_id={"context": (me + r) % n}, device_id_type=pl.DeviceIdType.MESH)
    for r in range(1, n_dp):
        pl.semaphore_signal(barrier, inc=1, device_id={"dp": (dp + r) % n_dp}, device_id_type=pl.DeviceIdType.MESH)

    loads = [
        pltpu.make_async_copy(src, dst, in_sem.at[i])
        for i, (src, dst) in enumerate(
            [(k_hbm, k_ref), (v_hbm, v_ref), (q_hbm, q_ref), (g_hbm, g_ref)]
        )
    ]
    for load in loads[:2]:
        load.start()

    def remote(src, dst, send, recv, **where):
        return pltpu.make_async_remote_copy(
            src_ref=src, dst_ref=dst, send_sem=send, recv_sem=recv,
            device_id=where, device_id_type=pl.DeviceIdType.MESH,
        )

    row_i = lax.broadcasted_iota(jnp.int32, (pos, pos), 0)
    col_i = lax.broadcasted_iota(jnp.int32, (pos, pos), 1)
    tri = jnp.where(row_i <= col_i, 1.0, 0.0).astype(F32)
    cum_t[...] = jnp.zeros_like(cum_t)
    cum_t[:heads, :] = lax.dot_general(
        ld_ref[...], tri, (((1,), (0,)), ((), ())),
        precision=lax.Precision.HIGHEST, preferred_element_type=F32,
    )
    cumc[...] = jnp.transpose(cum_t[...])
    cum = cumc[...]
    gath[me] = jnp.broadcast_to(cum[pos - 1 : pos, :], (8, LANES))
    pl.semaphore_wait(barrier, (n - 1) + (n_dp - 1))

    def gather_copy(r):
        return remote(gath.at[me], gath.at[me], ga_s, ga_r, context=(me + r) % n)

    def gather_all():
        span = gath.at[pl.ds(0, n - 1)]
        return remote(span, span, ga_s, ga_r, context=mate)

    for r in range(1, n):
        gather_copy(r).start()
    loads[0].wait()
    loads[1].wait()
    loads[2].start()
    loads[3].start()

    def lanes(h):
        return pl.ds(pl.multiple_of(h * size, size), size)

    def column(h):
        return colb[h]

    def block_last(h):
        return colb[h, pos - 1 : pos, :]

    def decay_of(h):
        col = colb[h]
        wide = jnp.concatenate([col] * (-(-pos // LANES)), axis=1)[:, :pos]
        return jnp.exp(jnp.where(row_i >= col_i, wide - cum_t[pl.ds(h, 1), :], -jnp.inf))

    class Scan:
        def __init__(self, forward, st, pr, tot, rx, sd, result, pf, d1s, d1r, xs, xr, d2s, d2r):
            self.forward, self.st, self.pr, self.tot, self.rx = forward, st, pr, tot, rx
            self.sd, self.result, self.pf = sd, result, pf
            self.d1s, self.d1r, self.xs, self.xr, self.d2s, self.d2r = d1s, d1r, xs, xr, d2s, d2r
            self.first = (core == 0) if forward else (core == 1)
            self.base = 0 if forward else 6 + 3 * steps
            self.bits, self.partner, self.ups = [], [], []
            for s in range(steps):
                bit = (chip // (2**s)) % 2
                self.bits.append(bit)
                self.partner.append((chip + (1 - 2 * bit) * (2**s)) * 2 + core)
                self.ups.append((bit == 0) if forward else (bit == 1))

        def c(self, row, h):
            return coef[self.base + row, pl.ds(h, 1), :]

        def fill(self, last):
            ids = lax.broadcasted_iota(jnp.int32, last.shape, 0)
            chips = ids // 2

            def put(row, mask, keep=None):
                total = jnp.sum(jnp.where(mask, last, 0.0), axis=0, keepdims=True)
                value = jnp.exp(total)
                if keep is not None:
                    value = value * keep
                rows[self.base + row : self.base + row + 1, :] = value

            one = jnp.where(self.first, 1, 0)
            put(0, (ids == mate) & (one == 1))
            put(1, (ids == me) & (one == 0))
            put(2, (ids == mate) & (one == 0))
            put(3, (ids == me) & (one == 1))
            for s in range(steps):
                up = jnp.where(self.ups[s], 1, 0)
                mine = (chips // (2**s)) == (chip // (2**s))
                other = (chips // (2**s)) == ((self.partner[s] // 2) // (2**s))
                put(4 + 3 * s, other & (up == 1))
                put(5 + 3 * s, mine & (up == 0))
                ahead = (chips < chip) if self.forward else (chips > chip)
                put(6 + 3 * s, mine & ahead, keep=jnp.where(self.ups[s], 0.0, 1.0))
            if steps == 2:
                far, near = self.partner[1] // 2, self.partner[0] // 2

                def between(a, b):
                    return (chips > jnp.minimum(a, b)) & (chips < jnp.maximum(a, b))

                put(4 + 3 * steps, between(far, chip))
                put(5 + 3 * steps, between(far, near))

        def die1(self, k):
            return remote(self.st.at[(1 - core) * half + k], self.pr.at[k], self.d1s, self.d1r.at[k], context=mate)

        def link(self, s, k, slot=None):
            group = self.xs.at[steps if slot == 1 else s]
            return remote(self.tot.at[s if slot is None else slot, k], self.rx.at[s, k], group, self.xr.at[s, k], context=self.partner[s])

        def sent(self, group, count):
            span = self.rx.at[0, pl.ds(0, count)]
            return remote(span, span, self.xs.at[group], self.xr.at[0, 0], context=mate)

        def die2(self, k):
            return remote(self.sd.at[k], self.result.at[core * half + k], self.d2s, self.d2r.at[k], context=mate)

        def die2_in(self, k):
            return remote(self.sd.at[k], self.result.at[(1 - core) * half + k], self.d2s, self.d2r.at[k], context=mate)

        def send(self, s, k):
            if s < steps - 1:
                self.link(s, k).start()
            else:
                @pl.when(self.ups[s])
                def _():
                    self.link(s, k).start()

        def send_first(self, k):
            if steps != 2:
                self.send(0, k)
                return

            @pl.when(k % 2 == 0)
            def _():
                self.send(0, k)

            @pl.when((k % 2 == 1) & self.ups[1])
            def _():
                self.link(1, k, 0).start()

        def step(self, s, k):
            if steps != 2:
                self.stage(s, k)
                return
            h = core * half + k
            up0, up1 = self.ups[0], self.ups[1]
            down0, down1 = jnp.logical_not(up0), jnp.logical_not(up1)
            even, odd = k % 2 == 0, k % 2 == 1

            @pl.when(even)
            def _():
                self.stage(s, k)

            if s == 0:
                @pl.when(odd & up1 & up0)
                def _():
                    self.tot[1, k] = self.tot[0, k]
                    self.pf[k] = jnp.zeros_like(self.pf[k])

                @pl.when(odd & up1 & down0)
                def _():
                    self.pf[k] = jnp.zeros_like(self.pf[k])

                @pl.when(odd & down1)
                def _():
                    self.link(1, k, 0).wait_recv()
                    got = self.rx[1, k]
                    own = jnp.where(up0, 1.0, 0.0)
                    self.tot[1, k] = self.c(5 + 3 * steps, h) * got + own * self.tot[0, k]
                    self.pf[k] = self.c(4 + 3 * steps, h) * got

                @pl.when(odd & (up0 | down1))
                def _():
                    self.link(0, k, 1).start()
            else:
                @pl.when(odd & (down0 | down1))
                def _():
                    self.link(0, k, 1).wait_recv()
                    self.pf[k] = self.pf[k] + self.rx[0, k]

                @pl.when(odd)
                def _():
                    self.hand(k)

        def combine(self, k):
            h = core * half + k
            self.die1(k).wait_recv()
            self.tot[0, k] = self.c(0, h) * self.st[h] + self.c(1, h) * self.pr[k]
            self.send_first(k)

        def stage(self, s, k):
            h = core * half + k
            if s < steps - 1:
                self.link(s, k).wait_recv()
                got = self.rx[s, k]
                self.tot[s + 1, k] = self.c(4 + 3 * s, h) * self.tot[s, k] + self.c(5 + 3 * s, h) * got
                self.send(s + 1, k)
                part = self.c(6 + 3 * s, h) * got
                self.pf[k] = part if s == 0 else self.pf[k] + part
                return

            @pl.when(jnp.logical_not(self.ups[s]))
            def _():
                self.link(s, k).wait_recv()
                part = self.c(6 + 3 * s, h) * self.rx[s, k]
                self.pf[k] = part if s == 0 else self.pf[k] + part

            if s == 0:
                @pl.when(self.ups[s])
                def _():
                    self.pf[k] = jnp.zeros_like(self.pf[k])

            self.hand(k)

        def hand(self, k):
            h = core * half + k
            prefix = self.pf[k]
            head_first = jnp.where(self.first, 1.0, 0.0)
            self.sd[k] = self.c(3, h) * prefix + head_first * self.st[h]
            self.die2(k).start()
            self.result[h] = self.c(2, h) * prefix + (1.0 - head_first) * self.pr[k]

        def drain(self):
            for group in (self.d1s, self.d2s):
                remote(self.sd, self.sd, group, self.d1r.at[0], context=mate).wait_send()
            if steps != 2:
                for s in range(steps - 1):
                    self.sent(s, half).wait_send()

                @pl.when(self.ups[steps - 1])
                def _():
                    self.sent(steps - 1, half).wait_send()

                return
            self.sent(0, half // 2).wait_send()

            @pl.when(self.ups[1])
            def _():
                self.sent(1, half).wait_send()

            @pl.when(self.ups[0] | jnp.logical_not(self.ups[1]))
            def _():
                self.sent(2, half // 2).wait_send()

    fwd = Scan(True, st_f, pr_f, tot_f, rx_f, sd_f, inc, pf_f, d1s_f, d1r_f, xs_f, xr_f, d2s_f, d2r_f)
    bwd = Scan(False, st_b, pr_b, tot_b, rx_b, sd_b, later, pf_b, d1s_b, d1r_f, xs_b, xr_b, d2s_b, d2r_f)

    def guarded(k, run):
        @pl.when((k >= 0) & (k < half))
        def _():
            run(k)

    def own_states(hs):
        made = []
        for h in hs:
            col = jnp.transpose(jnp.broadcast_to(cum_t[pl.ds(h, 1), :], (LANES, pos)))
            shrink = jnp.exp(col[pos - 1 : pos, :] - col)
            late = (k_ref[:, lanes(h)].astype(F32) * shrink).astype(BF16)
            made.append((h, col, dot_tn(late, v_ref[:, lanes(h)])))
        return made

    def keep_state(made):
        h, col, state = made
        st_f[h] = state
        colb[h] = col

    def states(k):
        far, near = own_states([(1 - core) * half + k, core * half + k])
        keep_state(far)
        fwd.die1(k).start()
        keep_state(near)

    def lead(k, carry):
        states(k)
        return carry

    lax.fori_loop(0, LEAD, lead, 0)
    gather_all().wait_recv()
    rows[...] = jnp.zeros_like(rows)
    last = gath[:, 0, :]
    fwd.fill(last)
    bwd.fill(last)
    turned = jnp.transpose(rows[...])
    for r in range(2 * (6 + 3 * steps)):
        coef[r] = jnp.broadcast_to(turned[:heads, r : r + 1], (heads, LANES))

    def rest(k, carry):
        guarded(k, states)
        fwd.combine(k - LEAD)
        return carry

    lax.fori_loop(LEAD, half + LEAD, rest, 0)
    acc_s[...] = jnp.zeros_like(acc_s)
    acc_p[...] = jnp.zeros_like(acc_p)

    def intra(hs):
        made = []
        for h in hs:
            s = dot_nt(q_ref[:, lanes(h)], k_ref[:, lanes(h)])
            w = (s * decay_of(h)).astype(BF16)
            made.append((h, w, dot_nn(w, v_ref[:, lanes(h)])))
        for h, w, a in made:
            fw[h] = w
            att[:, lanes(h)] = a

    def scaled_of(h):
        return gain_ref[:, lanes(h)] * g_ref[:, lanes(h)].astype(F32)

    def inter(hs):
        made = []
        for h in hs:
            far = dot_nn(q_ref[:, lanes(h)], inc[h].astype(BF16))
            a = att[:, lanes(h)] + jnp.exp(column(h)) * far
            made.append((h, a, scaled_of(h) * a))
        square, cross = acc_s[...], acc_p[...]
        for h, a, p in made:
            square, cross = square + a * a, cross + p
        acc_s[...], acc_p[...] = square, cross
        for h, a, p in made:
            att[:, lanes(h)] = a

    unit = 2 if half % 2 == 0 else 1
    count = half // unit
    spread = -(-LAG // unit)
    lags = [0, count] if steps == 2 else [spread * s for s in range(steps)]
    lag_in = max(lags[-1] + spread, count)

    def group(base):
        return [base + i for i in range(unit)]

    def pass_loop(scan, local, finish, low=0, high=None):
        def one(it, carry):
            for s in range(steps):
                at = it - lags[s]

                @pl.when((at >= 0) & (at < count))
                def _():
                    for k in group(at * unit):
                        scan.step(s, k)

            @pl.when(it < 2 * count)
            def _():
                late = it // count
                who = core + late * (1 - 2 * core)
                local(group(who * half + (it - late * count) * unit))

            own = it - lags[-1]

            @pl.when((own >= 0) & (own < count))
            def _():
                finish(group(core * half + own * unit))

            come = it - lag_in

            @pl.when((come >= 0) & (come < count))
            def _():
                for k in group(come * unit):
                    scan.die2_in(k).wait_recv()
                finish(group((1 - core) * half + come * unit))

            return carry

        lax.fori_loop(low, count + lag_in if high is None else high, one, 0)

    loads[2].wait()
    loads[3].wait()
    pass_loop(fwd, intra, inter)

    mean_sq = jnp.sum(acc_s[...], axis=1, keepdims=True) * (1.0 / feat)
    inverse = lax.rsqrt(mean_sq + EPSILON)
    proj = inverse * (jnp.sum(acc_p[...], axis=1, keepdims=True) * (1.0 / feat))
    acc_s[...] = jnp.broadcast_to(inverse, acc_s.shape)
    acc_p[...] = jnp.broadcast_to(proj, acc_p.shape)

    def delta(h):
        inv = acc_s[...]
        normed = att[:, lanes(h)] * inv
        wide = g_ref[:, lanes(h)].astype(F32)
        scaled = gain_ref[:, lanes(h)] * wide
        od = (inv * (scaled - normed * acc_p[...])).astype(BF16)
        terms = jnp.sum((wide * normed).reshape(pos // 8, 8, size), axis=0)
        early = (q_ref[:, lanes(h)].astype(F32) * jnp.exp(column(h))).astype(BF16)
        return h, od, terms, dot_tn(early, od)

    def keep_delta(made):
        h, od, terms, state = made
        st_b[h] = state
        od_ref[:, lanes(h)] = od
        gp[:, lanes(h)] = terms

    def deltas(k):
        far, near = delta((1 - core) * half + k), delta(core * half + k)
        keep_delta(far)
        bwd.die1(k).start()
        keep_delta(near)

    def back(k, carry):
        guarded(k, deltas)
        guarded(k - LEAD, bwd.combine)
        return carry

    lax.fori_loop(0, half + LEAD, back, 0)

    part = feat // n_dp

    def gx_copy(r):
        to = (dp + r) % n_dp
        return remote(gp.at[:, pl.ds(pl.multiple_of(to * part, LANES), part)], gx.at[r], gx_s, gx_r, dp=to)

    def gx_all():
        span = gx.at[pl.ds(1, n_dp - 1)]
        return remote(span, span, gx_s, gx_r, dp=(dp + 1) % n_dp)

    for r in range(1, n_dp):
        gx_copy(r).start()

    def local_back(hs):
        made = []
        for h in hs:
            od = od_ref[:, lanes(h)]
            q = q_ref[:, lanes(h)]
            key = k_ref[:, lanes(h)]
            bw = (dot_nt(od, v_ref[:, lanes(h)]) * decay_of(h)).astype(BF16)
            far = dot_nt(od, inc[h].astype(BF16))
            qg = (dot_nn(bw, key) + jnp.exp(column(h)) * far).astype(BF16)
            made.append((h, qg, dot_tn(bw, q), dot_tn(fw[h], od)))
        for h, qg, kl, vl in made:
            qg_ref[:, lanes(h)] = qg
            att[:, lanes(h)] = kl
            vloc[:, lanes(h)] = vl

    def finish_back(hs):
        made = []
        for h in hs:
            shrink = jnp.exp(block_last(h) - column(h))
            lt = later[h].astype(BF16)
            kg = att[:, lanes(h)] + shrink * dot_nt(v_ref[:, lanes(h)], lt)
            vg = vloc[:, lanes(h)] + shrink * dot_nn(k_ref[:, lanes(h)], lt)
            made.append((h, kg.astype(BF16), vg.astype(BF16)))
        for h, kg, vg in made:
            kg_ref[:, lanes(h)] = kg
            vg_ref[:, lanes(h)] = vg

    pass_loop(bwd, local_back, finish_back, 0, count // 2)
    if n_dp > 1:
        gx_all().wait_recv()
    total = gp[:, pl.ds(pl.multiple_of(dp * part, LANES), part)]
    for r in range(1, n_dp):
        total = total + gx[r]
    total = jnp.sum(total, axis=0, keepdims=True)
    for i in range(n):
        gy[i] = jnp.broadcast_to(total[:, i * width : (i + 1) * width], (8, width))

    def gy_copy(r):
        return remote(gy.at[(me + r) % n], gz.at[r], gy_s, gy_r, context=(me + r) % n)

    def gy_all():
        span = gz.at[pl.ds(1, n - 1)]
        return remote(span, span, gy_s, gy_r, context=mate)

    for r in range(1, n):
        gy_copy(r).start()

    pass_loop(bwd, local_back, finish_back, count // 2)

    out = gy[me]
    gy_all().wait_recv()
    for r in range(1, n):
        out = out + gz[r]
    gg_ref[...] = out[0:1, :] * cfg["norm"]

    gather_all().wait_send()
    gy_all().wait_send()
    if n_dp > 1:
        gx_all().wait_send()
    fwd.drain()
    bwd.drain()


def settle(count, *refs):
    srcs, dsts, sems = refs[:count], refs[count : 2 * count], refs[2 * count]
    copies = [pltpu.make_async_copy(srcs[i], dsts[i], sems.at[i]) for i in range(count)]
    for copy in copies:
        copy.start()
    for copy in copies:
        copy.wait()


def settled(arrays):
    count = len(arrays)
    return pl.pallas_call(
        functools.partial(settle, count),
        out_shape=tuple(jax.ShapeDtypeStruct(a.shape, a.dtype) for a in arrays),
        in_specs=[pl.BlockSpec(memory_space=pltpu.VMEM)] * count,
        out_specs=(pl.BlockSpec(memory_space=pl.ANY),) * count,
        scratch_shapes=[pltpu.SemaphoreType.DMA((count,))],
        compiler_params=pltpu.CompilerParams(vmem_limit_bytes=1 << 20),
    )(*[pltpu.with_memory_space_constraint(a, pltpu.VMEM) for a in arrays])


def per_device(queries, key_rows, value_rows, out_grad, log_decay, norm_gain):
    pos, feat = queries.shape[1:]
    heads = log_decay.shape[2]
    size = feat // heads
    half = heads // 2
    n, n_dp = lax.axis_size("context"), lax.axis_size("dp")
    steps = (n // 2).bit_length() - 1
    width = feat // (n * n_dp)
    cfg = dict(n=n, n_dp=n_dp, steps=steps, heads=heads, norm=1.0 / math.sqrt(pos * n * n_dp))
    vmem = pl.BlockSpec(memory_space=pltpu.VMEM)
    sem = pltpu.SemaphoreType.DMA

    def scan_buffers():
        return [
            pltpu.VMEM((heads, size, size), F32),
            pltpu.VMEM((half, size, size), F32),
            pltpu.VMEM((steps, half, size, size), F32),
            pltpu.VMEM((steps, half, size, size), F32),
            pltpu.VMEM((half, size, size), F32),
            pltpu.VMEM((heads, size, size), F32),
            pltpu.VMEM((half, size, size), F32),
        ]

    def scan_sems():
        return [sem(()), sem((half,)), sem((steps + 1,)), sem((steps, half)), sem(()), sem((half,))]

    rows_bf = pltpu.VMEM((pos, feat), BF16)
    scratch = [
        *([rows_bf] * 4), sem((4,)),
        pltpu.VMEM((pos, LANES), F32),
        pltpu.VMEM((LANES, pos), F32),
        pltpu.VMEM((heads, pos, LANES), F32),
        pltpu.VMEM((pos, feat), F32),
        pltpu.VMEM((pos, feat), F32),
        pltpu.VMEM((heads, pos, pos), BF16),
        pltpu.VMEM((pos, feat), BF16),
        pltpu.VMEM((pos, LANES), F32),
        pltpu.VMEM((pos, LANES), F32),
        pltpu.VMEM((n, 8, LANES), F32),
        pltpu.VMEM((LANES, LANES), F32),
        pltpu.VMEM((2 * (6 + 3 * steps), heads, LANES), F32),
        pltpu.VMEM((8, feat), F32),
        pltpu.VMEM((n_dp, 8, feat // n_dp), F32),
        pltpu.VMEM((n, 8, width), F32),
        pltpu.VMEM((n, 8, width), F32),
        *scan_buffers(),
        *scan_buffers(),
        *[sem(())] * 6,
        *scan_sems(),
        *[scan_sems()[i] for i in (0, 2, 3, 4)],
    ]
    grid_out = pltpu.VMEM((pos, feat), BF16)
    spare = 3 * pos * feat * 2 + (1 << 20)
    qg, kg, vg, gg = pl.pallas_call(
        functools.partial(body, cfg),
        out_shape=(grid_out, grid_out, grid_out, pltpu.VMEM((1, width), F32)),
        in_specs=[pl.BlockSpec(memory_space=pl.ANY)] * 4 + [vmem] * 2,
        out_specs=(vmem,) * 4,
        scratch_shapes=scratch,
        compiler_params=pltpu.CompilerParams(
            collective_id=0, has_side_effects=True, vmem_limit_bytes=67043328 - spare
        ),
    )(queries[0], key_rows[0], value_rows[0], out_grad[0], log_decay[0].T, norm_gain[None])
    qg, kg, vg, gg = settled((qg, kg, vg, gg))
    return qg[None], kg[None], vg[None], gg[0]


def solution(mesh):
    rows = P("dp", "context", None)
    return jax.shard_map(
        per_device,
        mesh=mesh,
        in_specs=(rows,) * 5 + (P(),),
        out_specs=(rows, rows, rows, P(("dp", "context"))),
        check_vma=False,
    )
```

```python
import functools
import math

import jax
import jax.numpy as jnp
from jax import lax
from jax.experimental import pallas as pl
from jax.experimental.pallas import tpu as pltpu
from jax.sharding import PartitionSpec as P

EPSILON = 1e-06
F32 = jnp.float32
BF16 = jnp.bfloat16
LANES = 128
LAG = 2
LEAD = 2


def dot_nn(a, b):
    return lax.dot_general(a, b, (((1,), (0,)), ((), ())), preferred_element_type=F32)


def dot_nt(a, b):
    return lax.dot_general(a, b, (((1,), (1,)), ((), ())), preferred_element_type=F32)


def dot_tn(a, b):
    return lax.dot_general(a, b, (((0,), (0,)), ((), ())), preferred_element_type=F32)


def body(
    cfg,
    q_hbm, k_hbm, v_hbm, g_hbm, ld_ref, gain_ref,
    qg_ref, kg_ref, vg_ref, gg_ref,
    q_ref, k_ref, v_ref, g_ref, in_sem,
    cumc, cum_t, colb, att, vloc, fw, od_ref, acc_s, acc_p,
    gath, rows, coef, gp, gx, gy, gz,
    st_f, pr_f, tot_f, rx_f, sd_f, inc, pf_f,
    st_b, pr_b, tot_b, rx_b, sd_b, later, pf_b,
    entry, ga_s, ga_r, gx_s, gx_r, gy_s, gy_r, gz_s, gz_r,
    d1s_f, d1r_f, xs_f, xr_f, d2s_f, d2r_f,
    d1s_b, xs_b, xr_b, d2s_b,
):
    n, n_dp, steps, heads = cfg["n"], cfg["n_dp"], cfg["steps"], cfg["heads"]
    half = heads // 2
    pos = q_ref.shape[0]
    feat = q_ref.shape[1]
    size = feat // heads
    width = feat // (n * n_dp)
    me = lax.axis_index("context")
    dp = lax.axis_index("dp")
    core = me % 2
    chip = me // 2
    mate = chip * 2 + (1 - core)

    lead_of = n - 1
    leads = me == lead_of
    barrier = pltpu.get_barrier_semaphore()
    for r in range(1, n):
        peer = (me + r) % n

        @pl.when(peer != lead_of)
        def _():
            pl.semaphore_signal(barrier, inc=1, device_id={"context": peer}, device_id_type=pl.DeviceIdType.MESH)

    for r in range(1, n_dp):
        @pl.when(leads)
        def _():
            pl.semaphore_signal(barrier, inc=1, device_id={"dp": (dp + r) % n_dp}, device_id_type=pl.DeviceIdType.MESH)

    loads = [
        pltpu.make_async_copy(src, dst, in_sem.at[i])
        for i, (src, dst) in enumerate(
            [(k_hbm, k_ref), (v_hbm, v_ref), (q_hbm, q_ref), (g_hbm, g_ref)]
        )
    ]
    for load in loads[:2]:
        load.start()

    def remote(src, dst, send, recv, **where):
        return pltpu.make_async_remote_copy(
            src_ref=src, dst_ref=dst, send_sem=send, recv_sem=recv,
            device_id=where, device_id_type=pl.DeviceIdType.MESH,
        )

    row_i = lax.broadcasted_iota(jnp.int32, (pos, pos), 0)
    col_i = lax.broadcasted_iota(jnp.int32, (pos, pos), 1)
    tri = jnp.where(row_i <= col_i, 1.0, 0.0).astype(F32)
    cum_t[...] = jnp.zeros_like(cum_t)
    cum_t[:heads, :] = lax.dot_general(
        ld_ref[...], tri, (((1,), (0,)), ((), ())),
        precision=lax.Precision.HIGHEST, preferred_element_type=F32,
    )
    cumc[...] = jnp.transpose(cum_t[...])
    cum = cumc[...]
    gath[me] = jnp.broadcast_to(cum[pos - 1 : pos, :], (8, LANES))

    @pl.when(jnp.logical_not(leads))
    def _():
        pl.semaphore_wait(barrier, n - 1)

    @pl.when(me == lead_of - 1)
    def _():
        pl.semaphore_signal(entry, inc=1, device_id={"context": lead_of}, device_id_type=pl.DeviceIdType.MESH)

    @pl.when(leads)
    def _():
        pl.semaphore_wait(entry, 1)

    def gather_copy(r):
        return remote(gath.at[me], gath.at[me], ga_s, ga_r, context=(me + r) % n)

    def gather_all():
        span = gath.at[pl.ds(0, n - 1)]
        return remote(span, span, ga_s, ga_r, context=mate)

    for r in range(1, n):
        gather_copy(r).start()
    loads[0].wait()
    loads[1].wait()
    loads[2].start()
    loads[3].start()

    def lanes(h):
        return pl.ds(pl.multiple_of(h * size, size), size)

    def column(h):
        return colb[h]

    def block_last(h):
        return colb[h, pos - 1 : pos, :]

    def decay_of(h):
        col = colb[h]
        wide = jnp.concatenate([col] * (-(-pos // LANES)), axis=1)[:, :pos]
        return jnp.exp(jnp.where(row_i >= col_i, wide - cum_t[pl.ds(h, 1), :], -jnp.inf))

    class Scan:
        def __init__(self, forward, st, pr, tot, rx, sd, result, pf, d1s, d1r, xs, xr, d2s, d2r):
            self.forward, self.st, self.pr, self.tot, self.rx = forward, st, pr, tot, rx
            self.sd, self.result, self.pf = sd, result, pf
            self.d1s, self.d1r, self.xs, self.xr, self.d2s, self.d2r = d1s, d1r, xs, xr, d2s, d2r
            self.first = (core == 0) if forward else (core == 1)
            self.base = 0 if forward else 6 + 3 * steps
            self.bits, self.partner, self.ups = [], [], []
            for s in range(steps):
                bit = (chip // (2**s)) % 2
                self.bits.append(bit)
                self.partner.append((chip + (1 - 2 * bit) * (2**s)) * 2 + core)
                self.ups.append((bit == 0) if forward else (bit == 1))

        def c(self, row, h):
            return coef[self.base + row, pl.ds(h, 1), :]

        def fill(self, last):
            ids = lax.broadcasted_iota(jnp.int32, last.shape, 0)
            chips = ids // 2

            def put(row, mask, keep=None):
                total = jnp.sum(jnp.where(mask, last, 0.0), axis=0, keepdims=True)
                value = jnp.exp(total)
                if keep is not None:
                    value = value * keep
                rows[self.base + row : self.base + row + 1, :] = value

            one = jnp.where(self.first, 1, 0)
            put(0, (ids == mate) & (one == 1))
            put(1, (ids == me) & (one == 0))
            put(2, (ids == mate) & (one == 0))
            put(3, (ids == me) & (one == 1))
            for s in range(steps):
                up = jnp.where(self.ups[s], 1, 0)
                mine = (chips // (2**s)) == (chip // (2**s))
                other = (chips // (2**s)) == ((self.partner[s] // 2) // (2**s))
                put(4 + 3 * s, other & (up == 1))
                put(5 + 3 * s, mine & (up == 0))
                ahead = (chips < chip) if self.forward else (chips > chip)
                put(6 + 3 * s, mine & ahead, keep=jnp.where(self.ups[s], 0.0, 1.0))
            if steps == 2:
                far, near = self.partner[1] // 2, self.partner[0] // 2

                def between(a, b):
                    return (chips > jnp.minimum(a, b)) & (chips < jnp.maximum(a, b))

                put(4 + 3 * steps, between(far, chip))
                put(5 + 3 * steps, between(far, near))

        def die1(self, k):
            return remote(self.st.at[(1 - core) * half + k], self.pr.at[k], self.d1s, self.d1r.at[k], context=mate)

        def link(self, s, k, slot=None):
            group = self.xs.at[steps if slot == 1 else s]
            return remote(self.tot.at[s if slot is None else slot, k], self.rx.at[s, k], group, self.xr.at[s, k], context=self.partner[s])

        def sent(self, group, count):
            span = self.rx.at[0, pl.ds(0, count)]
            return remote(span, span, self.xs.at[group], self.xr.at[0, 0], context=mate)

        def die2(self, k):
            return remote(self.sd.at[k], self.result.at[core * half + k], self.d2s, self.d2r.at[k], context=mate)

        def die2_in(self, k):
            return remote(self.sd.at[k], self.result.at[(1 - core) * half + k], self.d2s, self.d2r.at[k], context=mate)

        def send(self, s, k):
            if s < steps - 1:
                self.link(s, k).start()
            else:
                @pl.when(self.ups[s])
                def _():
                    self.link(s, k).start()

        def send_first(self, k):
            if steps != 2:
                self.send(0, k)
                return

            @pl.when(k % 2 == 0)
            def _():
                self.send(0, k)

            @pl.when((k % 2 == 1) & self.ups[1])
            def _():
                self.link(1, k, 0).start()

        def step(self, s, k):
            if steps != 2:
                self.stage(s, k)
                return
            h = core * half + k
            up0, up1 = self.ups[0], self.ups[1]
            down0, down1 = jnp.logical_not(up0), jnp.logical_not(up1)
            even, odd = k % 2 == 0, k % 2 == 1

            @pl.when(even)
            def _():
                self.stage(s, k)

            if s == 0:
                @pl.when(odd & up1 & up0)
                def _():
                    self.tot[1, k] = self.tot[0, k]
                    self.pf[k] = jnp.zeros_like(self.pf[k])

                @pl.when(odd & up1 & down0)
                def _():
                    self.pf[k] = jnp.zeros_like(self.pf[k])

                @pl.when(odd & down1)
                def _():
                    self.link(1, k, 0).wait_recv()
                    got = self.rx[1, k]
                    own = jnp.where(up0, 1.0, 0.0)
                    self.tot[1, k] = self.c(5 + 3 * steps, h) * got + own * self.tot[0, k]
                    self.pf[k] = self.c(4 + 3 * steps, h) * got

                @pl.when(odd & (up0 | down1))
                def _():
                    self.link(0, k, 1).start()
            else:
                @pl.when(odd & (down0 | down1))
                def _():
                    self.link(0, k, 1).wait_recv()
                    self.pf[k] = self.pf[k] + self.rx[0, k]

                @pl.when(odd)
                def _():
                    self.hand(k)

        def combine(self, k):
            h = core * half + k
            self.die1(k).wait_recv()
            self.tot[0, k] = self.c(0, h) * self.st[h] + self.c(1, h) * self.pr[k]
            self.send_first(k)

        def stage(self, s, k):
            h = core * half + k
            if s < steps - 1:
                self.link(s, k).wait_recv()
                got = self.rx[s, k]
                self.tot[s + 1, k] = self.c(4 + 3 * s, h) * self.tot[s, k] + self.c(5 + 3 * s, h) * got
                self.send(s + 1, k)
                part = self.c(6 + 3 * s, h) * got
                self.pf[k] = part if s == 0 else self.pf[k] + part
                return

            @pl.when(jnp.logical_not(self.ups[s]))
            def _():
                self.link(s, k).wait_recv()
                part = self.c(6 + 3 * s, h) * self.rx[s, k]
                self.pf[k] = part if s == 0 else self.pf[k] + part

            if s == 0:
                @pl.when(self.ups[s])
                def _():
                    self.pf[k] = jnp.zeros_like(self.pf[k])

            self.hand(k)

        def hand(self, k):
            h = core * half + k
            prefix = self.pf[k]
            head_first = jnp.where(self.first, 1.0, 0.0)
            self.sd[k] = self.c(3, h) * prefix + head_first * self.st[h]
            self.die2(k).start()
            self.result[h] = self.c(2, h) * prefix + (1.0 - head_first) * self.pr[k]

        def drain(self):
            for group in (self.d1s, self.d2s):
                remote(self.sd, self.sd, group, self.d1r.at[0], context=mate).wait_send()
            if steps != 2:
                for s in range(steps - 1):
                    self.sent(s, half).wait_send()

                @pl.when(self.ups[steps - 1])
                def _():
                    self.sent(steps - 1, half).wait_send()

                return
            self.sent(0, half // 2).wait_send()

            @pl.when(self.ups[1])
            def _():
                self.sent(1, half).wait_send()

            @pl.when(self.ups[0] | jnp.logical_not(self.ups[1]))
            def _():
                self.sent(2, half // 2).wait_send()

    fwd = Scan(True, st_f, pr_f, tot_f, rx_f, sd_f, inc, pf_f, d1s_f, d1r_f, xs_f, xr_f, d2s_f, d2r_f)
    bwd = Scan(False, st_b, pr_b, tot_b, rx_b, sd_b, later, pf_b, d1s_b, d1r_f, xs_b, xr_b, d2s_b, d2r_f)

    def guarded(k, run):
        @pl.when((k >= 0) & (k < half))
        def _():
            run(k)

    def own_states(hs):
        made = []
        for h in hs:
            col = jnp.transpose(jnp.broadcast_to(cum_t[pl.ds(h, 1), :], (LANES, pos)))
            shrink = jnp.exp(col[pos - 1 : pos, :] - col)
            late = (k_ref[:, lanes(h)].astype(F32) * shrink).astype(BF16)
            made.append((h, col, dot_tn(late, v_ref[:, lanes(h)])))
        return made

    def keep_state(made):
        h, col, state = made
        st_f[h] = state
        colb[h] = col

    def states(k):
        far, near = own_states([(1 - core) * half + k, core * half + k])
        keep_state(far)
        fwd.die1(k).start()
        keep_state(near)

    def lead(k, carry):
        states(k)
        return carry

    lax.fori_loop(0, LEAD, lead, 0)
    gather_all().wait_recv()
    rows[...] = jnp.zeros_like(rows)
    last = gath[:, 0, :]
    fwd.fill(last)
    bwd.fill(last)
    turned = jnp.transpose(rows[...])
    for r in range(2 * (6 + 3 * steps)):
        coef[r] = jnp.broadcast_to(turned[:heads, r : r + 1], (heads, LANES))

    def rest(k, carry):
        guarded(k, states)
        fwd.combine(k - LEAD)
        return carry

    lax.fori_loop(LEAD, half + LEAD, rest, 0)
    acc_s[...] = jnp.zeros_like(acc_s)
    acc_p[...] = jnp.zeros_like(acc_p)

    def intra(hs):
        made = []
        for h in hs:
            s = dot_nt(q_ref[:, lanes(h)], k_ref[:, lanes(h)])
            w = (s * decay_of(h)).astype(BF16)
            made.append((h, w, dot_nn(w, v_ref[:, lanes(h)])))
        for h, w, a in made:
            fw[h] = w
            att[:, lanes(h)] = a

    def scaled_of(h):
        return gain_ref[:, lanes(h)] * g_ref[:, lanes(h)].astype(F32)

    def inter(hs):
        made = []
        for h in hs:
            far = dot_nn(q_ref[:, lanes(h)], inc[h].astype(BF16))
            a = att[:, lanes(h)] + jnp.exp(column(h)) * far
            made.append((h, a, scaled_of(h) * a))
        square, cross = acc_s[...], acc_p[...]
        for h, a, p in made:
            square, cross = square + a * a, cross + p
        acc_s[...], acc_p[...] = square, cross
        for h, a, p in made:
            att[:, lanes(h)] = a

    unit = 2 if half % 2 == 0 else 1
    count = half // unit
    spread = -(-LAG // unit)
    lags = [0, count] if steps == 2 else [spread * s for s in range(steps)]
    lag_in = max(lags[-1] + spread, count)

    def group(base):
        return [base + i for i in range(unit)]

    def pass_loop(scan, local, finish, extra=None):
        def one(it, carry):
            for s in range(steps):
                at = it - lags[s]

                @pl.when((at >= 0) & (at < count))
                def _():
                    for k in group(at * unit):
                        scan.step(s, k)

            @pl.when(it < 2 * count)
            def _():
                late = it // count
                who = core + late * (1 - 2 * core)
                local(group(who * half + (it - late * count) * unit))

            if extra is not None:
                extra(it)

            own = it - lags[-1]

            @pl.when((own >= 0) & (own < count))
            def _():
                finish(group(core * half + own * unit))

            come = it - lag_in

            @pl.when((come >= 0) & (come < count))
            def _():
                for k in group(come * unit):
                    scan.die2_in(k).wait_recv()
                finish(group((1 - core) * half + come * unit))

            return carry

        lax.fori_loop(0, count + lag_in, one, 0)

    loads[2].wait()
    loads[3].wait()
    pass_loop(fwd, intra, inter)

    mean_sq = jnp.sum(acc_s[...], axis=1, keepdims=True) * (1.0 / feat)
    inverse = lax.rsqrt(mean_sq + EPSILON)
    proj = inverse * (jnp.sum(acc_p[...], axis=1, keepdims=True) * (1.0 / feat))
    acc_s[...] = jnp.broadcast_to(inverse, acc_s.shape)
    acc_p[...] = jnp.broadcast_to(proj, acc_p.shape)

    def delta(h):
        inv = acc_s[...]
        normed = att[:, lanes(h)] * inv
        wide = g_ref[:, lanes(h)].astype(F32)
        scaled = gain_ref[:, lanes(h)] * wide
        od = (inv * (scaled - normed * acc_p[...])).astype(BF16)
        terms = jnp.sum(wide * normed, axis=0, keepdims=True)
        early = (q_ref[:, lanes(h)].astype(F32) * jnp.exp(column(h))).astype(BF16)
        return h, od, terms, dot_tn(early, od)

    def keep_delta(made):
        h, od, terms, state = made
        st_b[h] = state
        od_ref[:, lanes(h)] = od
        gp[:, lanes(h)] = terms

    def deltas(k):
        far, near = delta((1 - core) * half + k), delta(core * half + k)
        keep_delta(far)
        bwd.die1(k).start()
        keep_delta(near)

    def back(k, carry):
        guarded(k, deltas)
        guarded(k - LEAD, bwd.combine)
        return carry

    lax.fori_loop(0, half + LEAD, back, 0)

    part = feat // n_dp

    def gain_in():
        return remote(gp, gx.at[me], gx_s, gx_r, context=lead_of)

    def gain_in_all():
        span = gx.at[pl.ds(0, n - 1)]
        return remote(span, span, gx_s, gx_r, context=lead_of - 1)

    def gain_across(r):
        to = (dp + r) % n_dp
        return remote(gp.at[:, pl.ds(pl.multiple_of(to * part, LANES), part)], gz.at[r], gy_s, gy_r, dp=to)

    def gain_across_all():
        span = gz.at[pl.ds(1, n_dp - 1)]
        return remote(span, span, gy_s, gy_r, dp=(dp + 1) % n_dp)

    def gain_out(i):
        return remote(gy.at[i], gy.at[lead_of], gz_s, gz_r, context=i)

    def gain_out_all():
        span = gy.at[pl.ds(0, n - 1)]
        return remote(span, span, gz_s, gz_r, context=lead_of - 1)

    @pl.when(jnp.logical_not(leads))
    def _():
        gain_in().start()

    def gain_step(it):
        @pl.when(leads & (it == count // 2))
        def _():
            gain_in_all().wait_recv()
            total = gp[...]
            for r in range(n - 1):
                total = total + gx[r]
            gp[...] = total
            if n_dp > 1:
                pl.semaphore_wait(barrier, n_dp - 1)
                for r in range(1, n_dp):
                    gain_across(r).start()

        @pl.when(leads & (it == count))
        def _():
            total = gp[:, pl.ds(pl.multiple_of(dp * part, LANES), part)]
            if n_dp > 1:
                gain_across_all().wait_recv()
                for r in range(1, n_dp):
                    total = total + gz[r]
            for i in range(n):
                gy[i] = jnp.broadcast_to(total[:, i * width : (i + 1) * width], (8, width))
            for i in range(n - 1):
                gain_out(i).start()

    def local_back(hs):
        made = []
        for h in hs:
            od = od_ref[:, lanes(h)]
            q = q_ref[:, lanes(h)]
            key = k_ref[:, lanes(h)]
            bw = (dot_nt(od, v_ref[:, lanes(h)]) * decay_of(h)).astype(BF16)
            far = dot_nt(od, inc[h].astype(BF16))
            qg = (dot_nn(bw, key) + jnp.exp(column(h)) * far).astype(BF16)
            made.append((h, qg, dot_tn(bw, q), dot_tn(fw[h], od)))
        for h, qg, kl, vl in made:
            qg_ref[:, lanes(h)] = qg
            att[:, lanes(h)] = kl
            vloc[:, lanes(h)] = vl

    def finish_back(hs):
        made = []
        for h in hs:
            shrink = jnp.exp(block_last(h) - column(h))
            lt = later[h].astype(BF16)
            kg = att[:, lanes(h)] + shrink * dot_nt(v_ref[:, lanes(h)], lt)
            vg = vloc[:, lanes(h)] + shrink * dot_nn(k_ref[:, lanes(h)], lt)
            made.append((h, kg.astype(BF16), vg.astype(BF16)))
        for h, kg, vg in made:
            kg_ref[:, lanes(h)] = kg
            vg_ref[:, lanes(h)] = vg

    pass_loop(bwd, local_back, finish_back, gain_step)

    @pl.when(jnp.logical_not(leads))
    def _():
        gain_out(0).wait_recv()
        gain_in().wait_send()

    @pl.when(leads)
    def _():
        gain_out_all().wait_send()
        if n_dp > 1:
            gain_across_all().wait_send()

    gg_ref[...] = gy[lead_of][0:1, :] * cfg["norm"]
    gather_all().wait_send()
    fwd.drain()
    bwd.drain()


def settle(count, *refs):
    srcs, dsts, sems = refs[:count], refs[count : 2 * count], refs[2 * count]
    copies = [pltpu.make_async_copy(srcs[i], dsts[i], sems.at[i]) for i in range(count)]
    for copy in copies:
        copy.start()
    for copy in copies:
        copy.wait()


def settled(arrays):
    count = len(arrays)
    return pl.pallas_call(
        functools.partial(settle, count),
        out_shape=tuple(jax.ShapeDtypeStruct(a.shape, a.dtype) for a in arrays),
        in_specs=[pl.BlockSpec(memory_space=pltpu.VMEM)] * count,
        out_specs=(pl.BlockSpec(memory_space=pl.ANY),) * count,
        scratch_shapes=[pltpu.SemaphoreType.DMA((count,))],
        compiler_params=pltpu.CompilerParams(vmem_limit_bytes=1 << 20),
    )(*[pltpu.with_memory_space_constraint(a, pltpu.VMEM) for a in arrays])


def per_device(queries, key_rows, value_rows, out_grad, log_decay, norm_gain):
    pos, feat = queries.shape[1:]
    heads = log_decay.shape[2]
    size = feat // heads
    half = heads // 2
    n, n_dp = lax.axis_size("context"), lax.axis_size("dp")
    steps = (n // 2).bit_length() - 1
    width = feat // (n * n_dp)
    cfg = dict(n=n, n_dp=n_dp, steps=steps, heads=heads, norm=1.0 / math.sqrt(pos * n * n_dp))
    vmem = pl.BlockSpec(memory_space=pltpu.VMEM)
    sem = pltpu.SemaphoreType.DMA

    def scan_buffers():
        return [
            pltpu.VMEM((heads, size, size), F32),
            pltpu.VMEM((half, size, size), F32),
            pltpu.VMEM((steps, half, size, size), F32),
            pltpu.VMEM((steps, half, size, size), F32),
            pltpu.VMEM((half, size, size), F32),
            pltpu.VMEM((heads, size, size), F32),
            pltpu.VMEM((half, size, size), F32),
        ]

    def scan_sems():
        return [sem(()), sem((half,)), sem((steps + 1,)), sem((steps, half)), sem(()), sem((half,))]

    rows_bf = pltpu.VMEM((pos, feat), BF16)
    scratch = [
        *([rows_bf] * 4), sem((4,)),
        pltpu.VMEM((pos, LANES), F32),
        pltpu.VMEM((LANES, pos), F32),
        pltpu.VMEM((heads, pos, LANES), F32),
        pltpu.VMEM((pos, feat), F32),
        pltpu.VMEM((pos, feat), F32),
        pltpu.VMEM((heads, pos, pos), BF16),
        pltpu.VMEM((pos, feat), BF16),
        pltpu.VMEM((pos, LANES), F32),
        pltpu.VMEM((pos, LANES), F32),
        pltpu.VMEM((n, 8, LANES), F32),
        pltpu.VMEM((LANES, LANES), F32),
        pltpu.VMEM((2 * (6 + 3 * steps), heads, LANES), F32),
        pltpu.VMEM((1, feat), F32),
        pltpu.VMEM((n - 1, 1, feat), F32),
        pltpu.VMEM((n, 8, width), F32),
        pltpu.VMEM((n_dp, 1, feat // n_dp), F32),
        *scan_buffers(),
        *scan_buffers(),
        pltpu.SemaphoreType.REGULAR(()), *[sem(())] * 8,
        *scan_sems(),
        *[scan_sems()[i] for i in (0, 2, 3, 4)],
    ]
    grid_out = pltpu.VMEM((pos, feat), BF16)
    spare = 3 * pos * feat * 2 + (1 << 20)
    qg, kg, vg, gg = pl.pallas_call(
        functools.partial(body, cfg),
        out_shape=(grid_out, grid_out, grid_out, pltpu.VMEM((1, width), F32)),
        in_specs=[pl.BlockSpec(memory_space=pl.ANY)] * 4 + [vmem] * 2,
        out_specs=(vmem,) * 4,
        scratch_shapes=scratch,
        compiler_params=pltpu.CompilerParams(
            collective_id=0, has_side_effects=True, vmem_limit_bytes=67043328 - spare
        ),
    )(queries[0], key_rows[0], value_rows[0], out_grad[0], log_decay[0].T, norm_gain[None])
    qg, kg, vg, gg = settled((qg, kg, vg, gg))
    return qg[None], kg[None], vg[None], gg[0]


def solution(mesh):
    rows = P("dp", "context", None)
    return jax.shard_map(
        per_device,
        mesh=mesh,
        in_specs=(rows,) * 5 + (P(),),
        out_specs=(rows, rows, rows, P(("dp", "context"))),
        check_vma=False,
    )
```

```python
import functools
import math

import jax
import jax.numpy as jnp
from jax import lax
from jax.experimental import pallas as pl
from jax.experimental.pallas import tpu as pltpu
from jax.sharding import PartitionSpec as P

EPSILON = 1e-06
F32 = jnp.float32
BF16 = jnp.bfloat16
LANES = 128
LAG = 2
LEAD = 2
SOLO = 6


def dot_nn(a, b):
    return lax.dot_general(a, b, (((1,), (0,)), ((), ())), preferred_element_type=F32)


def dot_nt(a, b):
    return lax.dot_general(a, b, (((1,), (1,)), ((), ())), preferred_element_type=F32)


def dot_tn(a, b):
    return lax.dot_general(a, b, (((0,), (0,)), ((), ())), preferred_element_type=F32)


def body(
    cfg,
    q_hbm, k_hbm, v_hbm, g_hbm, ld_hbm, gain_hbm,
    qg_ref, kg_ref, vg_ref, gg_ref,
    q_ref, k_ref, v_ref, g_ref, ld_ref, gain_ref, in_sem,
    cumc, cum_t, colb, att, vloc, fw, od_ref, acc_s, acc_p,
    gath, rows, coef, gp, gx, gy, gz,
    st_f, pr_f, tot_f, rx_f, sd_f, inc, pf_f,
    st_b, pr_b, tot_b, rx_b, sd_b, later, pf_b,
    entry, gm_s, gm_r, ga_s, ga_r, gx_s, gx_r, gy_s, gy_r, gz_s, gz_r,
    d1s_f, d1r_f, xs_f, xr_f, d2s_f, d2r_f,
    d1s_b, xs_b, xr_b, d2s_b,
):
    n, n_dp, steps, heads = cfg["n"], cfg["n_dp"], cfg["steps"], cfg["heads"]
    half = heads // 2
    pos = q_ref.shape[0]
    feat = q_ref.shape[1]
    size = feat // heads
    width = feat // (n * n_dp)
    me = lax.axis_index("context")
    dp = lax.axis_index("dp")
    core = me % 2
    chip = me // 2
    mate = chip * 2 + (1 - core)

    fetch = [
        pltpu.make_async_copy(src, dst, in_sem.at[i])
        for i, (src, dst) in enumerate(
            [(ld_hbm, ld_ref), (q_hbm, q_ref), (g_hbm, g_ref), (gain_hbm, gain_ref)]
        )
    ]
    fetch[0].start()
    head_start = max(1, half // 4)

    def columns(src, dst, low, high, i):
        for side in (1 - core, core):
            at = pl.ds(pl.multiple_of((side * half + low) * size, LANES), (high - low) * size)
            pltpu.make_async_copy(src.at[:, at], dst.at[:, at], in_sem.at[i]).start()

    def columns_wait(src, dst, low, high, i):
        at = pl.ds(0, 2 * (high - low) * size)
        pltpu.make_async_copy(src.at[:, at], dst.at[:, at], in_sem.at[i]).wait()

    columns(k_hbm, k_ref, 0, head_start, 4)
    columns(v_hbm, v_ref, 0, head_start, 5)
    columns(k_hbm, k_ref, head_start, half, 6)
    columns(v_hbm, v_ref, head_start, half, 7)

    lead_of = n - 1
    leads = me == lead_of
    barrier = pltpu.get_barrier_semaphore()
    for r in range(1, n):
        peer = (me + r) % n

        @pl.when(peer != lead_of)
        def _():
            pl.semaphore_signal(barrier, inc=1, device_id={"context": peer}, device_id_type=pl.DeviceIdType.MESH)

    for r in range(1, n_dp):
        @pl.when(leads)
        def _():
            pl.semaphore_signal(barrier, inc=1, device_id={"dp": (dp + r) % n_dp}, device_id_type=pl.DeviceIdType.MESH)

    def remote(src, dst, send, recv, **where):
        return pltpu.make_async_remote_copy(
            src_ref=src, dst_ref=dst, send_sem=send, recv_sem=recv,
            device_id=where, device_id_type=pl.DeviceIdType.MESH,
        )

    row_i = lax.broadcasted_iota(jnp.int32, (pos, pos), 0)
    col_i = lax.broadcasted_iota(jnp.int32, (pos, pos), 1)
    tri = jnp.where(row_i <= col_i, 1.0, 0.0).astype(F32)
    cum_t[...] = jnp.zeros_like(cum_t)
    fetch[0].wait()
    cum_t[:heads, :] = lax.dot_general(
        ld_ref[...], tri, (((1,), (0,)), ((), ())),
        precision=lax.Precision.HIGHEST, preferred_element_type=F32,
    )
    cumc[...] = jnp.transpose(cum_t[...])
    cum = cumc[...]
    gath[me] = jnp.broadcast_to(cum[pos - 1 : pos, :], (8, LANES))

    @pl.when(jnp.logical_not(leads))
    def _():
        pl.semaphore_wait(barrier, n - 1)

    @pl.when(me == lead_of - 1)
    def _():
        pl.semaphore_signal(entry, inc=1, device_id={"context": lead_of}, device_id_type=pl.DeviceIdType.MESH)

    @pl.when(leads)
    def _():
        pl.semaphore_wait(entry, 1)

    def gather_copy(r):
        return remote(gath.at[me], gath.at[me], ga_s, ga_r, context=(me + r) % n)

    def gather_mate():
        return remote(gath.at[me], gath.at[me], gm_s, gm_r, context=mate)

    def gather_all():
        span = gath.at[pl.ds(0, n - 2)]
        return remote(span, span, ga_s, ga_r, context=mate)

    gather_mate().start()
    for r in range(1, n):
        @pl.when((me + r) % n != mate)
        def _():
            gather_copy(r).start()

    columns_wait(k_hbm, k_ref, 0, head_start, 4)
    columns_wait(v_hbm, v_ref, 0, head_start, 5)

    def lanes(h):
        return pl.ds(pl.multiple_of(h * size, size), size)

    def column(h):
        return colb[h]

    def block_last(h):
        return colb[h, pos - 1 : pos, :]

    def decay_of(h):
        col = colb[h]
        wide = jnp.concatenate([col] * (-(-pos // LANES)), axis=1)[:, :pos]
        return jnp.exp(jnp.where(row_i >= col_i, wide - cum_t[pl.ds(h, 1), :], -jnp.inf))

    class Scan:
        def __init__(self, forward, st, pr, tot, rx, sd, result, pf, d1s, d1r, xs, xr, d2s, d2r):
            self.forward, self.st, self.pr, self.tot, self.rx = forward, st, pr, tot, rx
            self.sd, self.result, self.pf = sd, result, pf
            self.d1s, self.d1r, self.xs, self.xr, self.d2s, self.d2r = d1s, d1r, xs, xr, d2s, d2r
            self.first = (core == 0) if forward else (core == 1)
            self.base = 0 if forward else 6 + 3 * steps
            self.bits, self.partner, self.ups = [], [], []
            for s in range(steps):
                bit = (chip // (2**s)) % 2
                self.bits.append(bit)
                self.partner.append((chip + (1 - 2 * bit) * (2**s)) * 2 + core)
                self.ups.append((bit == 0) if forward else (bit == 1))

        def c(self, row, h):
            return coef[self.base + row, pl.ds(h, 1), :]

        def fill_near(self, mine, other):
            one = jnp.where(self.first, 1.0, 0.0)
            values = [one * other, (1.0 - one) * mine, (1.0 - one) * other, one * mine]
            for row, total in enumerate(values):
                rows[self.base + row : self.base + row + 1, :] = jnp.exp(total)

        def fill(self, last):
            ids = lax.broadcasted_iota(jnp.int32, last.shape, 0)
            chips = ids // 2

            def put(row, mask, keep=None):
                total = jnp.sum(jnp.where(mask, last, 0.0), axis=0, keepdims=True)
                value = jnp.exp(total)
                if keep is not None:
                    value = value * keep
                rows[self.base + row : self.base + row + 1, :] = value

            for s in range(steps):
                up = jnp.where(self.ups[s], 1, 0)
                mine = (chips // (2**s)) == (chip // (2**s))
                other = (chips // (2**s)) == ((self.partner[s] // 2) // (2**s))
                put(4 + 3 * s, other & (up == 1))
                put(5 + 3 * s, mine & (up == 0))
                ahead = (chips < chip) if self.forward else (chips > chip)
                put(6 + 3 * s, mine & ahead, keep=jnp.where(self.ups[s], 0.0, 1.0))
            if steps == 2:
                far, near = self.partner[1] // 2, self.partner[0] // 2

                def between(a, b):
                    return (chips > jnp.minimum(a, b)) & (chips < jnp.maximum(a, b))

                put(4 + 3 * steps, between(far, chip))
                put(5 + 3 * steps, between(far, near))

        def die1(self, k):
            return remote(self.st.at[(1 - core) * half + k], self.pr.at[k], self.d1s, self.d1r.at[k], context=mate)

        def link(self, s, k, slot=None):
            group = self.xs.at[steps if slot == 1 else s]
            return remote(self.tot.at[s if slot is None else slot, k], self.rx.at[s, k], group, self.xr.at[s, k], context=self.partner[s])

        def sent(self, group, count):
            span = self.rx.at[0, pl.ds(0, count)]
            return remote(span, span, self.xs.at[group], self.xr.at[0, 0], context=mate)

        def die2(self, k):
            return remote(self.sd.at[k], self.result.at[core * half + k], self.d2s, self.d2r.at[k], context=mate)

        def die2_in(self, k):
            return remote(self.sd.at[k], self.result.at[(1 - core) * half + k], self.d2s, self.d2r.at[k], context=mate)

        def send(self, s, k):
            if s < steps - 1:
                self.link(s, k).start()
            else:
                @pl.when(self.ups[s])
                def _():
                    self.link(s, k).start()

        def send_first(self, k):
            if steps != 2:
                self.send(0, k)
                return

            @pl.when(k % 2 == 0)
            def _():
                self.send(0, k)

            @pl.when((k % 2 == 1) & self.ups[1])
            def _():
                self.link(1, k, 0).start()

        def step(self, s, k):
            if steps != 2:
                self.stage(s, k)
                return
            h = core * half + k
            up0, up1 = self.ups[0], self.ups[1]
            down0, down1 = jnp.logical_not(up0), jnp.logical_not(up1)
            even, odd = k % 2 == 0, k % 2 == 1

            @pl.when(even)
            def _():
                self.stage(s, k)

            if s == 0:
                @pl.when(odd & up1 & up0)
                def _():
                    self.tot[1, k] = self.tot[0, k]
                    self.pf[k] = jnp.zeros_like(self.pf[k])

                @pl.when(odd & up1 & down0)
                def _():
                    self.pf[k] = jnp.zeros_like(self.pf[k])

                @pl.when(odd & down1)
                def _():
                    self.link(1, k, 0).wait_recv()
                    got = self.rx[1, k]
                    own = jnp.where(up0, 1.0, 0.0)
                    self.tot[1, k] = self.c(5 + 3 * steps, h) * got + own * self.tot[0, k]
                    self.pf[k] = self.c(4 + 3 * steps, h) * got

                @pl.when(odd & (up0 | down1))
                def _():
                    self.link(0, k, 1).start()
            else:
                @pl.when(odd & (down0 | down1))
                def _():
                    self.link(0, k, 1).wait_recv()
                    self.pf[k] = self.pf[k] + self.rx[0, k]

                @pl.when(odd)
                def _():
                    self.hand(k)

        def combine(self, k):
            h = core * half + k
            self.die1(k).wait_recv()
            self.tot[0, k] = self.c(0, h) * self.st[h] + self.c(1, h) * self.pr[k]
            self.send_first(k)

        def stage(self, s, k):
            h = core * half + k
            if s < steps - 1:
                self.link(s, k).wait_recv()
                got = self.rx[s, k]
                self.tot[s + 1, k] = self.c(4 + 3 * s, h) * self.tot[s, k] + self.c(5 + 3 * s, h) * got
                self.send(s + 1, k)
                part = self.c(6 + 3 * s, h) * got
                self.pf[k] = part if s == 0 else self.pf[k] + part
                return

            @pl.when(jnp.logical_not(self.ups[s]))
            def _():
                self.link(s, k).wait_recv()
                part = self.c(6 + 3 * s, h) * self.rx[s, k]
                self.pf[k] = part if s == 0 else self.pf[k] + part

            if s == 0:
                @pl.when(self.ups[s])
                def _():
                    self.pf[k] = jnp.zeros_like(self.pf[k])

            self.hand(k)

        def hand(self, k):
            h = core * half + k
            prefix = self.pf[k]
            head_first = jnp.where(self.first, 1.0, 0.0)
            self.sd[k] = self.c(3, h) * prefix + head_first * self.st[h]
            self.die2(k).start()
            self.result[h] = self.c(2, h) * prefix + (1.0 - head_first) * self.pr[k]

        def drain(self):
            for group in (self.d1s, self.d2s):
                remote(self.sd, self.sd, group, self.d1r.at[0], context=mate).wait_send()
            if steps != 2:
                for s in range(steps - 1):
                    self.sent(s, half).wait_send()

                @pl.when(self.ups[steps - 1])
                def _():
                    self.sent(steps - 1, half).wait_send()

                return
            self.sent(0, half // 2).wait_send()

            @pl.when(self.ups[1])
            def _():
                self.sent(1, half).wait_send()

            @pl.when(self.ups[0] | jnp.logical_not(self.ups[1]))
            def _():
                self.sent(2, half // 2).wait_send()

    fwd = Scan(True, st_f, pr_f, tot_f, rx_f, sd_f, inc, pf_f, d1s_f, d1r_f, xs_f, xr_f, d2s_f, d2r_f)
    bwd = Scan(False, st_b, pr_b, tot_b, rx_b, sd_b, later, pf_b, d1s_b, d1r_f, xs_b, xr_b, d2s_b, d2r_f)

    def guarded(k, run):
        @pl.when((k >= 0) & (k < half))
        def _():
            run(k)

    def own_states(hs):
        made = []
        for h in hs:
            col = jnp.transpose(jnp.broadcast_to(cum_t[pl.ds(h, 1), :], (LANES, pos)))
            shrink = jnp.exp(col[pos - 1 : pos, :] - col)
            late = (k_ref[:, lanes(h)].astype(F32) * shrink).astype(BF16)
            made.append((h, col, dot_tn(late, v_ref[:, lanes(h)])))
        return made

    def keep_state(made):
        h, col, state = made
        st_f[h] = state
        colb[h] = col

    def states(k):
        far, near = own_states([(1 - core) * half + k, core * half + k])
        keep_state(far)
        fwd.die1(k).start()
        keep_state(near)

    def lead(k, carry):
        states(k)
        return carry

    lax.fori_loop(0, LEAD, lead, 0)
    gather_mate().wait_recv()
    rows[...] = jnp.zeros_like(rows)
    mine, other = gath[me, 0:1, :], gath[mate, 0:1, :]
    fwd.fill_near(mine, other)
    bwd.fill_near(mine, other)

    def spread_rows(picked):
        turned = jnp.transpose(rows[...])
        for r in picked:
            coef[r] = jnp.broadcast_to(turned[:heads, r : r + 1], (heads, LANES))

    near = [scan.base + row for scan in (fwd, bwd) for row in range(4)]
    spread_rows(near)
    columns_wait(k_hbm, k_ref, head_start, half, 6)
    columns_wait(v_hbm, v_ref, head_start, half, 7)
    for i in (1, 2, 3):
        fetch[i].start()
    unit = 2 if half % 2 == 0 else 1
    count = half // unit
    ahead = (half + LEAD - SOLO) // 2 if unit == 2 and half > SOLO else 0

    def group(base):
        return [base + i for i in range(unit)]

    def feed(scan, produce, local, ready):
        def alone(k, carry):
            guarded(k, produce)
            guarded(k - LEAD, scan.combine)
            return carry

        def paired(j, carry):
            for i in range(2):
                k = SOLO + 2 * j + i
                guarded(k, produce)
                guarded(k - LEAD, scan.combine)
            local(group(core * half + 2 * j))
            return carry

        lax.fori_loop(scan.begun, SOLO if ahead else half + LEAD, alone, 0)
        ready()
        lax.fori_loop(0, ahead, paired, 0)

    def intra(hs):
        made = []
        for h in hs:
            s = dot_nt(q_ref[:, lanes(h)], k_ref[:, lanes(h)])
            w = (s * decay_of(h)).astype(BF16)
            made.append((h, w, dot_nn(w, v_ref[:, lanes(h)])))
        for h, w, a in made:
            fw[h] = w
            att[:, lanes(h)] = a

    fwd.begun, bwd.begun = LEAD, 0

    def ready():
        for i in (1, 2, 3):
            fetch[i].wait()

    feed(fwd, states, intra, ready)
    gather_all().wait_recv()
    last = gath[:, 0, :]
    fwd.fill(last)
    bwd.fill(last)
    spread_rows([r for r in range(2 * (6 + 3 * steps)) if r not in near])
    acc_s[...] = jnp.zeros_like(acc_s)
    acc_p[...] = jnp.zeros_like(acc_p)

    def scaled_of(h):
        return gain_ref[:, lanes(h)] * g_ref[:, lanes(h)].astype(F32)

    def inter(hs):
        made = []
        for h in hs:
            far = dot_nn(q_ref[:, lanes(h)], inc[h].astype(BF16))
            a = att[:, lanes(h)] + jnp.exp(column(h)) * far
            made.append((h, a, scaled_of(h) * a))
        square, cross = acc_s[...], acc_p[...]
        for h, a, p in made:
            square, cross = square + a * a, cross + p
        acc_s[...], acc_p[...] = square, cross
        for h, a, p in made:
            att[:, lanes(h)] = a

    spread = -(-LAG // unit)
    lags = [0, count] if steps == 2 else [spread * s for s in range(steps)]
    lag_in = max(lags[-1] + spread, count)

    def pass_loop(scan, local, finish, extra=None):
        def one(it, carry):
            for s in range(steps):
                at = it - lags[s]

                @pl.when((at >= 0) & (at < count))
                def _():
                    for k in group(at * unit):
                        scan.step(s, k)

            turn = it + ahead

            @pl.when(turn < 2 * count)
            def _():
                late = turn // count
                who = core + late * (1 - 2 * core)
                local(group(who * half + (turn - late * count) * unit))

            if extra is not None:
                extra(it)

            own = it - lags[-1]

            @pl.when((own >= 0) & (own < count))
            def _():
                finish(group(core * half + own * unit))

            come = it - lag_in

            @pl.when((come >= 0) & (come < count))
            def _():
                for k in group(come * unit):
                    scan.die2_in(k).wait_recv()
                finish(group((1 - core) * half + come * unit))

            return carry

        lax.fori_loop(0, count + lag_in, one, 0)

    pass_loop(fwd, intra, inter)

    mean_sq = jnp.sum(acc_s[...], axis=1, keepdims=True) * (1.0 / feat)
    inverse = lax.rsqrt(mean_sq + EPSILON)
    proj = inverse * (jnp.sum(acc_p[...], axis=1, keepdims=True) * (1.0 / feat))
    acc_s[...] = jnp.broadcast_to(inverse, acc_s.shape)
    acc_p[...] = jnp.broadcast_to(proj, acc_p.shape)

    def delta(h):
        inv = acc_s[...]
        normed = att[:, lanes(h)] * inv
        wide = g_ref[:, lanes(h)].astype(F32)
        scaled = gain_ref[:, lanes(h)] * wide
        od = (inv * (scaled - normed * acc_p[...])).astype(BF16)
        terms = jnp.sum(wide * normed, axis=0, keepdims=True)
        early = (q_ref[:, lanes(h)].astype(F32) * jnp.exp(column(h))).astype(BF16)
        return h, od, terms, dot_tn(early, od)

    def keep_delta(made):
        h, od, terms, state = made
        st_b[h] = state
        od_ref[:, lanes(h)] = od
        gp[:, lanes(h)] = terms

    def deltas(k):
        far, near = delta((1 - core) * half + k), delta(core * half + k)
        keep_delta(far)
        bwd.die1(k).start()
        keep_delta(near)

    def local_back(hs):
        made = []
        for h in hs:
            od = od_ref[:, lanes(h)]
            q = q_ref[:, lanes(h)]
            key = k_ref[:, lanes(h)]
            bw = (dot_nt(od, v_ref[:, lanes(h)]) * decay_of(h)).astype(BF16)
            far = dot_nt(od, inc[h].astype(BF16))
            qg = (dot_nn(bw, key) + jnp.exp(column(h)) * far).astype(BF16)
            made.append((h, qg, dot_tn(bw, q), dot_tn(fw[h], od)))
        for h, qg, kl, vl in made:
            qg_ref[:, lanes(h)] = qg
            att[:, lanes(h)] = kl
            vloc[:, lanes(h)] = vl

    feed(bwd, deltas, local_back, lambda: None)

    part = feat // n_dp

    def gain_in():
        return remote(gp, gx.at[me], gx_s, gx_r, context=lead_of)

    def gain_in_all():
        span = gx.at[pl.ds(0, n - 1)]
        return remote(span, span, gx_s, gx_r, context=lead_of - 1)

    def gain_across(r):
        to = (dp + r) % n_dp
        return remote(gp.at[:, pl.ds(pl.multiple_of(to * part, LANES), part)], gz.at[r], gy_s, gy_r, dp=to)

    def gain_across_all():
        span = gz.at[pl.ds(1, n_dp - 1)]
        return remote(span, span, gy_s, gy_r, dp=(dp + 1) % n_dp)

    def gain_out(i):
        return remote(gy.at[i], gy.at[lead_of], gz_s, gz_r, context=i)

    def gain_out_all():
        span = gy.at[pl.ds(0, n - 1)]
        return remote(span, span, gz_s, gz_r, context=lead_of - 1)

    @pl.when(jnp.logical_not(leads))
    def _():
        gain_in().start()

    def gain_step(it):
        @pl.when(leads & (it == count // 2))
        def _():
            gain_in_all().wait_recv()
            total = gp[...]
            for r in range(n - 1):
                total = total + gx[r]
            gp[...] = total
            if n_dp > 1:
                pl.semaphore_wait(barrier, n_dp - 1)
                for r in range(1, n_dp):
                    gain_across(r).start()

        @pl.when(leads & (it == count))
        def _():
            total = gp[:, pl.ds(pl.multiple_of(dp * part, LANES), part)]
            if n_dp > 1:
                gain_across_all().wait_recv()
                for r in range(1, n_dp):
                    total = total + gz[r]
            for i in range(n):
                gy[i] = jnp.broadcast_to(total[:, i * width : (i + 1) * width], (8, width))
            for i in range(n - 1):
                gain_out(i).start()

    def finish_back(hs):
        made = []
        for h in hs:
            shrink = jnp.exp(block_last(h) - column(h))
            lt = later[h].astype(BF16)
            kg = att[:, lanes(h)] + shrink * dot_nt(v_ref[:, lanes(h)], lt)
            vg = vloc[:, lanes(h)] + shrink * dot_nn(k_ref[:, lanes(h)], lt)
            made.append((h, kg.astype(BF16), vg.astype(BF16)))
        for h, kg, vg in made:
            kg_ref[:, lanes(h)] = kg
            vg_ref[:, lanes(h)] = vg

    pass_loop(bwd, local_back, finish_back, gain_step)

    @pl.when(jnp.logical_not(leads))
    def _():
        gain_out(0).wait_recv()
        gain_in().wait_send()

    @pl.when(leads)
    def _():
        gain_out_all().wait_send()
        if n_dp > 1:
            gain_across_all().wait_send()

    gg_ref[...] = gy[lead_of][0:1, :] * cfg["norm"]
    gather_mate().wait_send()
    gather_all().wait_send()
    fwd.drain()
    bwd.drain()


def settle(count, *refs):
    srcs, dsts, sems = refs[:count], refs[count : 2 * count], refs[2 * count]
    copies = [pltpu.make_async_copy(srcs[i], dsts[i], sems.at[i]) for i in range(count)]
    for copy in copies:
        copy.start()
    for copy in copies:
        copy.wait()


def settled(arrays):
    count = len(arrays)
    return pl.pallas_call(
        functools.partial(settle, count),
        out_shape=tuple(jax.ShapeDtypeStruct(a.shape, a.dtype) for a in arrays),
        in_specs=[pl.BlockSpec(memory_space=pltpu.VMEM)] * count,
        out_specs=(pl.BlockSpec(memory_space=pl.ANY),) * count,
        scratch_shapes=[pltpu.SemaphoreType.DMA((count,))],
        compiler_params=pltpu.CompilerParams(vmem_limit_bytes=1 << 20),
    )(*[pltpu.with_memory_space_constraint(a, pltpu.VMEM) for a in arrays])


def per_device(queries, key_rows, value_rows, out_grad, log_decay, norm_gain):
    pos, feat = queries.shape[1:]
    heads = log_decay.shape[2]
    size = feat // heads
    half = heads // 2
    n, n_dp = lax.axis_size("context"), lax.axis_size("dp")
    steps = (n // 2).bit_length() - 1
    width = feat // (n * n_dp)
    cfg = dict(n=n, n_dp=n_dp, steps=steps, heads=heads, norm=1.0 / math.sqrt(pos * n * n_dp))
    vmem = pl.BlockSpec(memory_space=pltpu.VMEM)
    sem = pltpu.SemaphoreType.DMA

    def scan_buffers():
        return [
            pltpu.VMEM((heads, size, size), F32),
            pltpu.VMEM((half, size, size), F32),
            pltpu.VMEM((steps, half, size, size), F32),
            pltpu.VMEM((steps, half, size, size), F32),
            pltpu.VMEM((half, size, size), F32),
            pltpu.VMEM((heads, size, size), F32),
            pltpu.VMEM((half, size, size), F32),
        ]

    def scan_sems():
        return [sem(()), sem((half,)), sem((steps + 1,)), sem((steps, half)), sem(()), sem((half,))]

    rows_bf = pltpu.VMEM((pos, feat), BF16)
    scratch = [
        *([rows_bf] * 4), pltpu.VMEM((heads, pos), F32), pltpu.VMEM((1, feat), F32), sem((8,)),
        pltpu.VMEM((pos, LANES), F32),
        pltpu.VMEM((LANES, pos), F32),
        pltpu.VMEM((heads, pos, LANES), F32),
        pltpu.VMEM((pos, feat), F32),
        pltpu.VMEM((pos, feat), F32),
        pltpu.VMEM((heads, pos, pos), BF16),
        pltpu.VMEM((pos, feat), BF16),
        pltpu.VMEM((pos, LANES), F32),
        pltpu.VMEM((pos, LANES), F32),
        pltpu.VMEM((n, 8, LANES), F32),
        pltpu.VMEM((LANES, LANES), F32),
        pltpu.VMEM((2 * (6 + 3 * steps), heads, LANES), F32),
        pltpu.VMEM((1, feat), F32),
        pltpu.VMEM((n - 1, 1, feat), F32),
        pltpu.VMEM((n, 8, width), F32),
        pltpu.VMEM((n_dp, 1, feat // n_dp), F32),
        *scan_buffers(),
        *scan_buffers(),
        pltpu.SemaphoreType.REGULAR(()), *[sem(())] * 10,
        *scan_sems(),
        *[scan_sems()[i] for i in (0, 2, 3, 4)],
    ]
    grid_out = pltpu.VMEM((pos, feat), BF16)
    spare = 3 * pos * feat * 2 + (1 << 20)
    qg, kg, vg, gg = pl.pallas_call(
        functools.partial(body, cfg),
        out_shape=(grid_out, grid_out, grid_out, pltpu.VMEM((1, width), F32)),
        in_specs=[pl.BlockSpec(memory_space=pl.ANY)] * 6,
        out_specs=(vmem,) * 4,
        scratch_shapes=scratch,
        compiler_params=pltpu.CompilerParams(
            collective_id=0, has_side_effects=True, vmem_limit_bytes=67043328 - spare
        ),
    )(queries[0], key_rows[0], value_rows[0], out_grad[0], log_decay[0].T, norm_gain[None])
    qg, kg, vg, gg = settled((qg, kg, vg, gg))
    return qg[None], kg[None], vg[None], gg[0]


def solution(mesh):
    rows = P("dp", "context", None)
    return jax.shard_map(
        per_device,
        mesh=mesh,
        in_specs=(rows,) * 5 + (P(),),
        out_specs=(rows, rows, rows, P(("dp", "context"))),
        check_vma=False,
    )
```

```python
import functools
import math

import jax
import jax.numpy as jnp
from jax import lax
from jax.experimental import pallas as pl
from jax.experimental.pallas import tpu as pltpu
from jax.sharding import PartitionSpec as P

EPSILON = 1e-06
F32 = jnp.float32
BF16 = jnp.bfloat16
LANES = 128
LAG = 2
LEAD = 2
SOLO = 8


def dot_nn(a, b):
    return lax.dot_general(a, b, (((1,), (0,)), ((), ())), preferred_element_type=F32)


def dot_nt(a, b):
    return lax.dot_general(a, b, (((1,), (1,)), ((), ())), preferred_element_type=F32)


def dot_tn(a, b):
    return lax.dot_general(a, b, (((0,), (0,)), ((), ())), preferred_element_type=F32)


def body(
    cfg,
    q_hbm, k_hbm, v_hbm, g_hbm, ld_hbm, gain_hbm,
    qg_ref, kg_ref, vg_ref, gg_ref,
    q_ref, k_ref, v_ref, g_ref, ld_ref, gain_ref, in_sem,
    cumc, cum_t, colb, att, vloc, fw, od_ref, acc_s, acc_p,
    gath, rows, coef, gp, gx, gy, gz,
    st_f, pr_f, tot_f, rx_f, sd_f, inc, pf_f,
    st_b, pr_b, tot_b, rx_b, sd_b, later, pf_b,
    entry, gm_s, gm_r, ga_s, ga_r, gx_s, gx_r, gy_s, gy_r, gz_s, gz_r,
    d1s_f, d1r_f, xs_f, xr_f, xe_f, d2s_f, d2r_f,
    d1s_b, xs_b, xr_b, xe_b, d2s_b,
):
    n, n_dp, steps, heads = cfg["n"], cfg["n_dp"], cfg["steps"], cfg["heads"]
    half = heads // 2
    unit = 2 if half % 2 == 0 else 1
    count = half // unit
    pos = q_ref.shape[0]
    feat = q_ref.shape[1]
    size = feat // heads
    width = feat // (n * n_dp)
    me = lax.axis_index("context")
    dp = lax.axis_index("dp")
    core = me % 2
    chip = me // 2
    mate = chip * 2 + (1 - core)

    fetch = [
        pltpu.make_async_copy(src, dst, in_sem.at[i])
        for i, (src, dst) in enumerate(
            [(ld_hbm, ld_ref), (q_hbm, q_ref), (g_hbm, g_ref), (gain_hbm, gain_ref)]
        )
    ]
    fetch[0].start()
    head_start = max(1, half // 4)

    def columns(src, dst, low, high, i):
        for side in (1 - core, core):
            at = pl.ds(pl.multiple_of((side * half + low) * size, LANES), (high - low) * size)
            pltpu.make_async_copy(src.at[:, at], dst.at[:, at], in_sem.at[i]).start()

    def columns_wait(src, dst, low, high, i):
        at = pl.ds(0, 2 * (high - low) * size)
        pltpu.make_async_copy(src.at[:, at], dst.at[:, at], in_sem.at[i]).wait()

    columns(k_hbm, k_ref, 0, head_start, 4)
    columns(v_hbm, v_ref, 0, head_start, 5)
    columns(k_hbm, k_ref, head_start, half, 6)
    columns(v_hbm, v_ref, head_start, half, 7)

    lead_of = n - 1
    leads = me == lead_of
    barrier = pltpu.get_barrier_semaphore()
    for r in range(1, n):
        peer = (me + r) % n

        @pl.when(peer != lead_of)
        def _():
            pl.semaphore_signal(barrier, inc=1, device_id={"context": peer}, device_id_type=pl.DeviceIdType.MESH)

    for r in range(1, n_dp):
        @pl.when(leads)
        def _():
            pl.semaphore_signal(barrier, inc=1, device_id={"dp": (dp + r) % n_dp}, device_id_type=pl.DeviceIdType.MESH)

    def remote(src, dst, send, recv, **where):
        return pltpu.make_async_remote_copy(
            src_ref=src, dst_ref=dst, send_sem=send, recv_sem=recv,
            device_id=where, device_id_type=pl.DeviceIdType.MESH,
        )

    row_i = lax.broadcasted_iota(jnp.int32, (pos, pos), 0)
    col_i = lax.broadcasted_iota(jnp.int32, (pos, pos), 1)
    tri = jnp.where(row_i <= col_i, 1.0, 0.0).astype(F32)
    cum_t[...] = jnp.zeros_like(cum_t)
    fetch[0].wait()
    cum_t[:heads, :] = lax.dot_general(
        ld_ref[...], tri, (((1,), (0,)), ((), ())),
        precision=lax.Precision.HIGHEST, preferred_element_type=F32,
    )
    cumc[...] = jnp.transpose(cum_t[...])
    cum = cumc[...]
    gath[me] = jnp.broadcast_to(cum[pos - 1 : pos, :], (8, LANES))

    @pl.when(jnp.logical_not(leads))
    def _():
        pl.semaphore_wait(barrier, n - 1)

    @pl.when(me == lead_of - 1)
    def _():
        pl.semaphore_signal(entry, inc=1, device_id={"context": lead_of}, device_id_type=pl.DeviceIdType.MESH)

    @pl.when(leads)
    def _():
        pl.semaphore_wait(entry, 1)

    def gather_copy(r):
        return remote(gath.at[me], gath.at[me], ga_s, ga_r, context=(me + r) % n)

    def gather_mate():
        return remote(gath.at[me], gath.at[me], gm_s, gm_r, context=mate)

    def gather_all():
        span = gath.at[pl.ds(0, n - 2)]
        return remote(span, span, ga_s, ga_r, context=mate)

    gather_mate().start()
    for r in range(1, n):
        @pl.when((me + r) % n != mate)
        def _():
            gather_copy(r).start()

    columns_wait(k_hbm, k_ref, 0, head_start, 4)
    columns_wait(v_hbm, v_ref, 0, head_start, 5)

    def lanes(h):
        return pl.ds(pl.multiple_of(h * size, size), size)

    def column(h):
        return colb[h]

    def block_last(h):
        return colb[h, pos - 1 : pos, :]

    def decay_of(h):
        col = colb[h]
        wide = jnp.concatenate([col] * (-(-pos // LANES)), axis=1)[:, :pos]
        return jnp.exp(jnp.where(row_i >= col_i, wide - cum_t[pl.ds(h, 1), :], -jnp.inf))

    class Scan:
        def __init__(self, forward, st, pr, tot, rx, sd, result, pf, d1s, d1r, xs, xr, xe, d2s, d2r):
            self.forward, self.st, self.pr, self.tot, self.rx = forward, st, pr, tot, rx
            self.sd, self.result, self.pf, self.xe = sd, result, pf, xe
            self.d1s, self.d1r, self.xs, self.xr, self.d2s, self.d2r = d1s, d1r, xs, xr, d2s, d2r
            self.first = (core == 0) if forward else (core == 1)
            self.base = 0 if forward else 6 + 3 * steps
            self.bits, self.partner, self.ups = [], [], []
            for s in range(steps):
                bit = (chip // (2**s)) % 2
                self.bits.append(bit)
                self.partner.append((chip + (1 - 2 * bit) * (2**s)) * 2 + core)
                self.ups.append((bit == 0) if forward else (bit == 1))

        def c(self, row, h):
            return coef[self.base + row, pl.ds(h, 1), :]

        def fill_near(self, mine, other):
            one = jnp.where(self.first, 1.0, 0.0)
            values = [one * other, (1.0 - one) * mine, (1.0 - one) * other, one * mine]
            for row, total in enumerate(values):
                rows[self.base + row : self.base + row + 1, :] = jnp.exp(total)

        def fill(self, last):
            ids = lax.broadcasted_iota(jnp.int32, last.shape, 0)
            chips = ids // 2

            def put(row, mask, keep=None):
                total = jnp.sum(jnp.where(mask, last, 0.0), axis=0, keepdims=True)
                value = jnp.exp(total)
                if keep is not None:
                    value = value * keep
                rows[self.base + row : self.base + row + 1, :] = value

            for s in range(steps):
                up = jnp.where(self.ups[s], 1, 0)
                mine = (chips // (2**s)) == (chip // (2**s))
                other = (chips // (2**s)) == ((self.partner[s] // 2) // (2**s))
                put(4 + 3 * s, other & (up == 1))
                put(5 + 3 * s, mine & (up == 0))
                ahead = (chips < chip) if self.forward else (chips > chip)
                put(6 + 3 * s, mine & ahead, keep=jnp.where(self.ups[s], 0.0, 1.0))
            if steps == 2:
                far, near = self.partner[1] // 2, self.partner[0] // 2

                def between(a, b):
                    return (chips > jnp.minimum(a, b)) & (chips < jnp.maximum(a, b))

                put(4 + 3 * steps, between(far, chip))
                put(5 + 3 * steps, between(far, near))

        def die1(self, k):
            return remote(self.st.at[(1 - core) * half + k], self.pr.at[k], self.d1s, self.d1r.at[k], context=mate)

        def link(self, s, k, slot=None, own=None):
            if steps == 2 and s == 0 and slot is None:
                own = self.xe.at[k // 2]
            group = self.xs.at[steps if slot == 1 else s]
            return remote(self.tot.at[s if slot is None else slot, k], self.rx.at[s, k], group, self.xr.at[s, k] if own is None else own, context=self.partner[s])

        def sent(self, group, count):
            span = self.rx.at[0, pl.ds(0, count)]
            return remote(span, span, self.xs.at[group], self.d2r.at[0], context=mate)

        def die2(self, k):
            return remote(self.sd.at[k], self.result.at[core * half + k], self.d2s, self.d2r.at[k // unit], context=mate)

        def die2_in(self, base):
            span = self.sd.at[pl.ds(0, unit)]
            return remote(span, span, self.d2s, self.d2r.at[base // unit], context=mate)

        def send(self, s, k):
            if s < steps - 1:
                self.link(s, k).start()
            else:
                @pl.when(self.ups[s])
                def _():
                    self.link(s, k).start()

        def send_first(self, k):
            if steps != 2:
                self.send(0, k)
                return

            @pl.when((k % 2 == 0) & (self.ups[0] | self.ups[1]))
            def _():
                self.send(0, k)

            @pl.when((k % 2 == 1) & self.ups[1])
            def _():
                self.link(1, k, 0).start()

        def step(self, s, k):
            if steps != 2:
                self.stage(s, k)
                return
            h = core * half + k
            up0, up1 = self.ups[0], self.ups[1]
            down0, down1 = jnp.logical_not(up0), jnp.logical_not(up1)
            even, odd = k % 2 == 0, k % 2 == 1

            if s == 0:
                @pl.when(even & (down0 | up1))
                def _():
                    self.stage(s, k)

                @pl.when(even & up0 & down1)
                def _():
                    self.pf[k] = jnp.zeros_like(self.pf[k])

                @pl.when(odd & up1 & up0)
                def _():
                    self.tot[1, k] = self.tot[0, k]
                    self.pf[k] = jnp.zeros_like(self.pf[k])

                @pl.when(odd & up1 & down0)
                def _():
                    self.pf[k] = jnp.zeros_like(self.pf[k])

                @pl.when(odd & down1)
                def _():
                    self.link(1, k, 0).wait_recv()
                    got = self.rx[1, k]
                    own = jnp.where(up0, 1.0, 0.0)
                    self.tot[1, k] = self.c(5 + 3 * steps, h) * got + own * self.tot[0, k]
                    self.pf[k] = self.c(4 + 3 * steps, h) * got

                @pl.when(odd & (up0 | down1))
                def _():
                    self.link(0, k, 1).start()
            else:
                @pl.when(even)
                def _():
                    self.stage(s, k)

                @pl.when(odd & (down0 | down1))
                def _():
                    self.link(0, k, 1).wait_recv()
                    self.pf[k] = self.pf[k] + self.rx[0, k]

                @pl.when(odd)
                def _():
                    self.hand(k)

        def combine(self, k):
            h = core * half + k
            self.die1(k).wait_recv()
            self.tot[0, k] = self.c(0, h) * self.st[h] + self.c(1, h) * self.pr[k]
            self.send_first(k)

        def stage(self, s, k):
            h = core * half + k
            if s < steps - 1:
                self.link(s, k).wait_recv()
                got = self.rx[s, k]
                self.tot[s + 1, k] = self.c(4 + 3 * s, h) * self.tot[s, k] + self.c(5 + 3 * s, h) * got
                self.send(s + 1, k)
                part = self.c(6 + 3 * s, h) * got
                self.pf[k] = part if s == 0 else self.pf[k] + part
                return

            @pl.when(jnp.logical_not(self.ups[s]))
            def _():
                self.link(s, k).wait_recv()
                part = self.c(6 + 3 * s, h) * self.rx[s, k]
                self.pf[k] = part if s == 0 else self.pf[k] + part

            if s == 0:
                @pl.when(self.ups[s])
                def _():
                    self.pf[k] = jnp.zeros_like(self.pf[k])

            self.hand(k)

        def hand(self, k):
            h = core * half + k
            prefix = self.pf[k]
            head_first = jnp.where(self.first, 1.0, 0.0)
            self.sd[k] = self.c(3, h) * prefix + head_first * self.st[h]
            self.die2(k).start()
            self.result[h] = self.c(2, h) * prefix + (1.0 - head_first) * self.pr[k]

        def drain(self):
            for group in (self.d1s, self.d2s):
                remote(self.sd, self.sd, group, self.d1r.at[0], context=mate).wait_send()
            if steps != 2:
                for s in range(steps - 1):
                    self.sent(s, half).wait_send()

                @pl.when(self.ups[steps - 1])
                def _():
                    self.sent(steps - 1, half).wait_send()

                return

            @pl.when(self.ups[0] | self.ups[1])
            def _():
                self.sent(0, half // 2).wait_send()

            @pl.when(self.ups[1])
            def _():
                self.sent(1, half).wait_send()

            @pl.when(self.ups[0] | jnp.logical_not(self.ups[1]))
            def _():
                self.sent(2, half // 2).wait_send()

    fwd = Scan(True, st_f, pr_f, tot_f, rx_f, sd_f, inc, pf_f, d1s_f, d1r_f, xs_f, xr_f, xe_f, d2s_f, d2r_f)
    bwd = Scan(False, st_b, pr_b, tot_b, rx_b, sd_b, later, pf_b, d1s_b, d1r_f, xs_b, xr_f if steps == 2 else xr_b, xe_b, d2s_b, d2r_f)

    def guarded(k, run):
        @pl.when((k >= 0) & (k < half))
        def _():
            run(k)

    def own_states(hs):
        made = []
        for h in hs:
            col = jnp.transpose(jnp.broadcast_to(cum_t[pl.ds(h, 1), :], (LANES, pos)))
            shrink = jnp.exp(col[pos - 1 : pos, :] - col)
            late = (k_ref[:, lanes(h)].astype(F32) * shrink).astype(BF16)
            made.append((h, col, dot_tn(late, v_ref[:, lanes(h)])))
        return made

    def keep_state(made):
        h, col, state = made
        st_f[h] = state
        colb[h] = col

    def states(k):
        far, near = own_states([(1 - core) * half + k, core * half + k])
        keep_state(far)
        fwd.die1(k).start()
        keep_state(near)

    def lead(k, carry):
        states(k)
        return carry

    lax.fori_loop(0, LEAD, lead, 0)
    gather_mate().wait_recv()
    rows[...] = jnp.zeros_like(rows)
    mine, other = gath[me, 0:1, :], gath[mate, 0:1, :]
    fwd.fill_near(mine, other)
    bwd.fill_near(mine, other)

    def spread_rows(picked):
        turned = jnp.transpose(rows[...])
        for r in picked:
            coef[r] = jnp.broadcast_to(turned[:heads, r : r + 1], (heads, LANES))

    near = [scan.base + row for scan in (fwd, bwd) for row in range(4)]
    spread_rows(near)
    columns_wait(k_hbm, k_ref, head_start, half, 6)
    columns_wait(v_hbm, v_ref, head_start, half, 7)
    for i in (1, 2, 3):
        fetch[i].start()
    ahead = (half + LEAD - SOLO) // 2 if unit == 2 and half > SOLO else 0

    def group(base):
        return [base + i for i in range(unit)]

    def feed(scan, produce, local, ready):
        def one(k, carry):
            guarded(k, produce)
            guarded(k - LEAD, scan.combine)
            if ahead:
                pl.when(k == SOLO)(ready)

                @pl.when((k > SOLO) & ((k - SOLO) % 2 == 1))
                def _():
                    local(group(core * half + k - SOLO - 1))

            return carry

        lax.fori_loop(scan.begun, half + LEAD, one, 0)
        if not ahead:
            ready()

    def intra(hs):
        made = []
        for h in hs:
            s = dot_nt(q_ref[:, lanes(h)], k_ref[:, lanes(h)])
            w = (s * decay_of(h)).astype(BF16)
            made.append((h, w, dot_nn(w, v_ref[:, lanes(h)])))
        for h, w, a in made:
            fw[h] = w
            att[:, lanes(h)] = a

    fwd.begun, bwd.begun = LEAD, 0

    def ready():
        for i in (1, 2, 3):
            fetch[i].wait()

    feed(fwd, states, intra, ready)
    gather_all().wait_recv()
    last = gath[:, 0, :]
    fwd.fill(last)
    bwd.fill(last)
    spread_rows([r for r in range(2 * (6 + 3 * steps)) if r not in near])
    acc_s[...] = jnp.zeros_like(acc_s)
    acc_p[...] = jnp.zeros_like(acc_p)

    def scaled_of(h):
        return gain_ref[:, lanes(h)] * g_ref[:, lanes(h)].astype(F32)

    def inter(hs):
        made = []
        for h in hs:
            far = dot_nn(q_ref[:, lanes(h)], inc[h].astype(BF16))
            a = att[:, lanes(h)] + jnp.exp(column(h)) * far
            made.append((h, a, scaled_of(h) * a))
        square, cross = acc_s[...], acc_p[...]
        for h, a, p in made:
            square, cross = square + a * a, cross + p
        acc_s[...], acc_p[...] = square, cross
        for h, a, p in made:
            att[:, lanes(h)] = a

    spread = -(-LAG // unit)
    lags = [0, count] if steps == 2 else [spread * s for s in range(steps)]
    lag_in = max(lags[-1] + spread, count)

    def pass_loop(scan, local, finish, extra=None):
        def one(it, carry):
            for s in range(steps):
                at = it - lags[s]

                @pl.when((at >= 0) & (at < count))
                def _():
                    for k in group(at * unit):
                        scan.step(s, k)

            turn = it + ahead

            @pl.when(turn < 2 * count)
            def _():
                late = turn // count
                who = core + late * (1 - 2 * core)
                local(group(who * half + (turn - late * count) * unit))

            if extra is not None:
                extra(it)

            own = it - lags[-1]

            @pl.when((own >= 0) & (own < count))
            def _():
                finish(group(core * half + own * unit))

            come = it - lag_in

            @pl.when((come >= 0) & (come < count))
            def _():
                scan.die2_in(come * unit).wait_recv()
                finish(group((1 - core) * half + come * unit))

            return carry

        lax.fori_loop(0, count + lag_in, one, 0)

    pass_loop(fwd, intra, inter)

    mean_sq = jnp.sum(acc_s[...], axis=1, keepdims=True) * (1.0 / feat)
    inverse = lax.rsqrt(mean_sq + EPSILON)
    proj = inverse * (jnp.sum(acc_p[...], axis=1, keepdims=True) * (1.0 / feat))
    acc_s[...] = jnp.broadcast_to(inverse, acc_s.shape)
    acc_p[...] = jnp.broadcast_to(proj, acc_p.shape)

    def delta(h):
        inv = acc_s[...]
        normed = att[:, lanes(h)] * inv
        wide = g_ref[:, lanes(h)].astype(F32)
        scaled = gain_ref[:, lanes(h)] * wide
        od = (inv * (scaled - normed * acc_p[...])).astype(BF16)
        terms = jnp.sum(wide * normed, axis=0, keepdims=True)
        early = (q_ref[:, lanes(h)].astype(F32) * jnp.exp(column(h))).astype(BF16)
        return h, od, terms, dot_tn(early, od)

    def keep_delta(made):
        h, od, terms, state = made
        st_b[h] = state
        od_ref[:, lanes(h)] = od
        gp[:, lanes(h)] = terms

    def deltas(k):
        far, near = delta((1 - core) * half + k), delta(core * half + k)
        keep_delta(far)
        bwd.die1(k).start()
        keep_delta(near)

    def local_back(hs):
        made = []
        for h in hs:
            od = od_ref[:, lanes(h)]
            q = q_ref[:, lanes(h)]
            key = k_ref[:, lanes(h)]
            bw = (dot_nt(od, v_ref[:, lanes(h)]) * decay_of(h)).astype(BF16)
            far = dot_nt(od, inc[h].astype(BF16))
            qg = (dot_nn(bw, key) + jnp.exp(column(h)) * far).astype(BF16)
            made.append((h, qg, dot_tn(bw, q), dot_tn(fw[h], od)))
        for h, qg, kl, vl in made:
            qg_ref[:, lanes(h)] = qg
            att[:, lanes(h)] = kl
            vloc[:, lanes(h)] = vl

    feed(bwd, deltas, local_back, lambda: None)

    part = feat // n_dp

    def gain_in():
        return remote(gp, gx.at[me], gx_s, gx_r, context=lead_of)

    def gain_in_all():
        span = gx.at[pl.ds(0, n - 1)]
        return remote(span, span, gx_s, gx_r, context=lead_of - 1)

    def gain_across(r):
        to = (dp + r) % n_dp
        return remote(gp.at[:, pl.ds(pl.multiple_of(to * part, LANES), part)], gz.at[r], gy_s, gy_r, dp=to)

    def gain_across_all():
        span = gz.at[pl.ds(1, n_dp - 1)]
        return remote(span, span, gy_s, gy_r, dp=(dp + 1) % n_dp)

    def gain_out(i):
        return remote(gy.at[i], gy.at[lead_of], gz_s, gz_r, context=i)

    def gain_out_all():
        span = gy.at[pl.ds(0, n - 1)]
        return remote(span, span, gz_s, gz_r, context=lead_of - 1)

    @pl.when(jnp.logical_not(leads))
    def _():
        gain_in().start()

    def gain_step(it):
        @pl.when(leads & (it == count))
        def _():
            gain_in_all().wait_recv()
            total = gp[...]
            for r in range(n - 1):
                total = total + gx[r]
            gp[...] = total
            if n_dp > 1:
                pl.semaphore_wait(barrier, n_dp - 1)
                for r in range(1, n_dp):
                    gain_across(r).start()

        @pl.when(leads & (it == 2 * count - 2))
        def _():
            total = gp[:, pl.ds(pl.multiple_of(dp * part, LANES), part)]
            if n_dp > 1:
                gain_across_all().wait_recv()
                for r in range(1, n_dp):
                    total = total + gz[r]
            for i in range(n):
                gy[i] = jnp.broadcast_to(total[:, i * width : (i + 1) * width], (8, width))
            for i in range(n - 1):
                gain_out(i).start()

    def finish_back(hs):
        made = []
        for h in hs:
            shrink = jnp.exp(block_last(h) - column(h))
            lt = later[h].astype(BF16)
            kg = att[:, lanes(h)] + shrink * dot_nt(v_ref[:, lanes(h)], lt)
            vg = vloc[:, lanes(h)] + shrink * dot_nn(k_ref[:, lanes(h)], lt)
            made.append((h, kg.astype(BF16), vg.astype(BF16)))
        for h, kg, vg in made:
            kg_ref[:, lanes(h)] = kg
            vg_ref[:, lanes(h)] = vg

    pass_loop(bwd, local_back, finish_back, gain_step)

    @pl.when(jnp.logical_not(leads))
    def _():
        gain_out(0).wait_recv()
        gain_in().wait_send()

    @pl.when(leads)
    def _():
        gain_out_all().wait_send()
        if n_dp > 1:
            gain_across_all().wait_send()

    gg_ref[...] = gy[lead_of][0:1, :] * cfg["norm"]
    gather_mate().wait_send()
    gather_all().wait_send()
    fwd.drain()
    bwd.drain()


def settle(count, *refs):
    srcs, dsts, sems = refs[:count], refs[count : 2 * count], refs[2 * count]
    copies = [pltpu.make_async_copy(srcs[i], dsts[i], sems.at[i]) for i in range(count)]
    for copy in copies:
        copy.start()
    for copy in copies:
        copy.wait()


def settled(arrays):
    count = len(arrays)
    return pl.pallas_call(
        functools.partial(settle, count),
        out_shape=tuple(jax.ShapeDtypeStruct(a.shape, a.dtype) for a in arrays),
        in_specs=[pl.BlockSpec(memory_space=pltpu.VMEM)] * count,
        out_specs=(pl.BlockSpec(memory_space=pl.ANY),) * count,
        scratch_shapes=[pltpu.SemaphoreType.DMA((count,))],
        compiler_params=pltpu.CompilerParams(vmem_limit_bytes=1 << 20),
    )(*[pltpu.with_memory_space_constraint(a, pltpu.VMEM) for a in arrays])


def per_device(queries, key_rows, value_rows, out_grad, log_decay, norm_gain):
    pos, feat = queries.shape[1:]
    heads = log_decay.shape[2]
    size = feat // heads
    half = heads // 2
    n, n_dp = lax.axis_size("context"), lax.axis_size("dp")
    steps = (n // 2).bit_length() - 1
    width = feat // (n * n_dp)
    cfg = dict(n=n, n_dp=n_dp, steps=steps, heads=heads, norm=1.0 / math.sqrt(pos * n * n_dp))
    vmem = pl.BlockSpec(memory_space=pltpu.VMEM)
    sem = pltpu.SemaphoreType.DMA

    def scan_buffers():
        return [
            pltpu.VMEM((heads, size, size), F32),
            pltpu.VMEM((half, size, size), F32),
            pltpu.VMEM((steps, half, size, size), F32),
            pltpu.VMEM((steps, half, size, size), F32),
            pltpu.VMEM((half, size, size), F32),
            pltpu.VMEM((heads, size, size), F32),
            pltpu.VMEM((half, size, size), F32),
        ]

    def scan_sems():
        evens = half // 2 if steps == 2 else 1
        odd_first = sem((steps, half))
        return [sem(()), sem((half,)), sem((steps + 1,)), odd_first, sem((evens,)), sem(()), sem((half // 2 if half % 2 == 0 else half,))]

    def scan_sems_more():
        first = scan_sems()
        return [first[0], first[2], sem((1, 1)) if steps == 2 else first[3], first[4], first[5]]

    rows_bf = pltpu.VMEM((pos, feat), BF16)
    scratch = [
        *([rows_bf] * 4), pltpu.VMEM((heads, pos), F32), pltpu.VMEM((1, feat), F32), sem((8,)),
        pltpu.VMEM((pos, LANES), F32),
        pltpu.VMEM((LANES, pos), F32),
        pltpu.VMEM((heads, pos, LANES), F32),
        pltpu.VMEM((pos, feat), F32),
        pltpu.VMEM((pos, feat), F32),
        pltpu.VMEM((heads, pos, pos), BF16),
        pltpu.VMEM((pos, feat), BF16),
        pltpu.VMEM((pos, LANES), F32),
        pltpu.VMEM((pos, LANES), F32),
        pltpu.VMEM((n, 8, LANES), F32),
        pltpu.VMEM((LANES, LANES), F32),
        pltpu.VMEM((2 * (6 + 3 * steps), heads, LANES), F32),
        pltpu.VMEM((1, feat), F32),
        pltpu.VMEM((n - 1, 1, feat), F32),
        pltpu.VMEM((n, 8, width), F32),
        pltpu.VMEM((n_dp, 1, feat // n_dp), F32),
        *scan_buffers(),
        *scan_buffers(),
        pltpu.SemaphoreType.REGULAR(()), *[sem(())] * 10,
        *scan_sems(),
        *scan_sems_more(),
    ]
    grid_out = pltpu.VMEM((pos, feat), BF16)
    spare = 3 * pos * feat * 2 + (1 << 20)
    qg, kg, vg, gg = pl.pallas_call(
        functools.partial(body, cfg),
        out_shape=(grid_out, grid_out, grid_out, pltpu.VMEM((1, width), F32)),
        in_specs=[pl.BlockSpec(memory_space=pl.ANY)] * 6,
        out_specs=(vmem,) * 4,
        scratch_shapes=scratch,
        compiler_params=pltpu.CompilerParams(
            collective_id=0, has_side_effects=True, vmem_limit_bytes=67043328 - spare
        ),
    )(queries[0], key_rows[0], value_rows[0], out_grad[0], log_decay[0].T, norm_gain[None])
    qg, kg, vg, gg = settled((qg, kg, vg, gg))
    return qg[None], kg[None], vg[None], gg[0]


def solution(mesh):
    rows = P("dp", "context", None)
    return jax.shard_map(
        per_device,
        mesh=mesh,
        in_specs=(rows,) * 5 + (P(),),
        out_specs=(rows, rows, rows, P(("dp", "context"))),
        check_vma=False,
    )
```

```python
import functools
import math

import jax
import jax.numpy as jnp
from jax import lax
from jax.experimental import pallas as pl
from jax.experimental.pallas import tpu as pltpu
from jax.sharding import PartitionSpec as P

EPSILON = 1e-06
F32 = jnp.float32
BF16 = jnp.bfloat16
LANES = 128
LAG = 2
LEAD = 2
SOLO = 8


def dot_nn(a, b):
    return lax.dot_general(a, b, (((1,), (0,)), ((), ())), preferred_element_type=F32)


def dot_nt(a, b):
    return lax.dot_general(a, b, (((1,), (1,)), ((), ())), preferred_element_type=F32)


def dot_tn(a, b):
    return lax.dot_general(a, b, (((0,), (0,)), ((), ())), preferred_element_type=F32)


def body(
    cfg,
    q_hbm, k_hbm, v_hbm, g_hbm, ld_hbm, gain_hbm,
    qg_ref, kg_ref, vg_ref, gg_ref,
    q_ref, k_ref, v_ref, g_ref, ld_ref, gain_ref, in_sem,
    cumc, cum_t, colb, att, vloc, fw, od_ref, acc_s, acc_p,
    gath, rows, coef, gp, gx, gy, gz,
    st_f, pr_f, tot_f, rx_f, sd_f, inc, pf_f,
    st_b, pr_b, tot_b, rx_b, sd_b, later, pf_b,
    entry, gm_s, gm_r, ga_s, ga_r, gx_s, gx_r, gy_s, gy_r, gz_s, gz_r,
    d1s_f, d1r_f, xs_f, xr_f, xe_f, d2s_f, d2r_f,
    d1s_b, xs_b, xr_b, xe_b, d2s_b,
):
    n, n_dp, steps, heads = cfg["n"], cfg["n_dp"], cfg["steps"], cfg["heads"]
    half = heads // 2
    unit = 2 if half % 2 == 0 else 1
    count = half // unit
    near_ring, back_ring = cfg["near_ring"], cfg["back_ring"]
    pos = q_ref.shape[0]
    feat = q_ref.shape[1]
    size = feat // heads
    width = feat // (n * n_dp)
    me = lax.axis_index("context")
    dp = lax.axis_index("dp")
    core = me % 2
    chip = me // 2
    mate = chip * 2 + (1 - core)

    fetch = [
        pltpu.make_async_copy(src, dst, in_sem.at[i])
        for i, (src, dst) in enumerate(
            [(ld_hbm, ld_ref), (q_hbm, q_ref), (g_hbm, g_ref), (gain_hbm, gain_ref)]
        )
    ]
    fetch[0].start()
    head_start = max(1, half // 4)

    def columns(src, dst, low, high, i):
        for side in (1 - core, core):
            at = pl.ds(pl.multiple_of((side * half + low) * size, LANES), (high - low) * size)
            pltpu.make_async_copy(src.at[:, at], dst.at[:, at], in_sem.at[i]).start()

    def columns_wait(src, dst, low, high, i):
        at = pl.ds(0, 2 * (high - low) * size)
        pltpu.make_async_copy(src.at[:, at], dst.at[:, at], in_sem.at[i]).wait()

    columns(k_hbm, k_ref, 0, head_start, 4)
    columns(v_hbm, v_ref, 0, head_start, 5)
    columns(k_hbm, k_ref, head_start, half, 6)
    columns(v_hbm, v_ref, head_start, half, 7)

    lead_of = n - 1
    leads = me == lead_of
    barrier = pltpu.get_barrier_semaphore()
    for r in range(1, n):
        peer = (me + r) % n

        @pl.when(peer != lead_of)
        def _():
            pl.semaphore_signal(barrier, inc=1, device_id={"context": peer}, device_id_type=pl.DeviceIdType.MESH)

    for r in range(1, n_dp):
        @pl.when(leads)
        def _():
            pl.semaphore_signal(barrier, inc=1, device_id={"dp": (dp + r) % n_dp}, device_id_type=pl.DeviceIdType.MESH)

    def remote(src, dst, send, recv, **where):
        return pltpu.make_async_remote_copy(
            src_ref=src, dst_ref=dst, send_sem=send, recv_sem=recv,
            device_id=where, device_id_type=pl.DeviceIdType.MESH,
        )

    row_i = lax.broadcasted_iota(jnp.int32, (pos, pos), 0)
    col_i = lax.broadcasted_iota(jnp.int32, (pos, pos), 1)
    tri = jnp.where(row_i <= col_i, 1.0, 0.0).astype(F32)
    cum_t[...] = jnp.zeros_like(cum_t)
    fetch[0].wait()
    cum_t[:heads, :] = lax.dot_general(
        ld_ref[...], tri, (((1,), (0,)), ((), ())),
        precision=lax.Precision.HIGHEST, preferred_element_type=F32,
    )
    cumc[...] = jnp.transpose(cum_t[...])
    cum = cumc[...]
    gath[me] = jnp.broadcast_to(cum[pos - 1 : pos, :], (8, LANES))

    @pl.when(jnp.logical_not(leads))
    def _():
        pl.semaphore_wait(barrier, n - 1)

    @pl.when(me == lead_of - 1)
    def _():
        pl.semaphore_signal(entry, inc=1, device_id={"context": lead_of}, device_id_type=pl.DeviceIdType.MESH)

    @pl.when(leads)
    def _():
        pl.semaphore_wait(entry, 1)

    def gather_copy(r):
        return remote(gath.at[me], gath.at[me], ga_s, ga_r, context=(me + r) % n)

    def gather_mate():
        return remote(gath.at[me], gath.at[me], gm_s, gm_r, context=mate)

    def gather_all():
        span = gath.at[pl.ds(0, n - 2)]
        return remote(span, span, ga_s, ga_r, context=mate)

    gather_mate().start()
    for r in range(1, n):
        @pl.when((me + r) % n != mate)
        def _():
            gather_copy(r).start()

    columns_wait(k_hbm, k_ref, 0, head_start, 4)
    columns_wait(v_hbm, v_ref, 0, head_start, 5)

    def lanes(h):
        return pl.ds(pl.multiple_of(h * size, size), size)

    def column(h):
        return colb[h]

    def block_last(h):
        return colb[h, pos - 1 : pos, :]

    def decay_of(h):
        col = colb[h]
        wide = jnp.concatenate([col] * (-(-pos // LANES)), axis=1)[:, :pos]
        return jnp.exp(jnp.where(row_i >= col_i, wide - cum_t[pl.ds(h, 1), :], -jnp.inf))

    class Scan:
        def __init__(self, forward, st, pr, tot, rx, sd, result, pf, d1s, d1r, xs, xr, xe, d2s, d2r):
            self.forward, self.st, self.pr, self.tot, self.rx = forward, st, pr, tot, rx
            self.sd, self.result, self.pf, self.xe = sd, result, pf, xe
            self.d1s, self.d1r, self.xs, self.xr, self.d2s, self.d2r = d1s, d1r, xs, xr, d2s, d2r
            self.first = (core == 0) if forward else (core == 1)
            self.base = 0 if forward else 6 + 3 * steps
            self.bits, self.partner, self.ups = [], [], []
            for s in range(steps):
                bit = (chip // (2**s)) % 2
                self.bits.append(bit)
                self.partner.append((chip + (1 - 2 * bit) * (2**s)) * 2 + core)
                self.ups.append((bit == 0) if forward else (bit == 1))

        def c(self, row, h):
            return coef[self.base + row, pl.ds(h, 1), :]

        def fill_near(self, mine, other):
            one = jnp.where(self.first, 1.0, 0.0)
            values = [one * other, (1.0 - one) * mine, (1.0 - one) * other, one * mine]
            for row, total in enumerate(values):
                rows[self.base + row : self.base + row + 1, :] = jnp.exp(total)

        def fill(self, last):
            ids = lax.broadcasted_iota(jnp.int32, last.shape, 0)
            chips = ids // 2

            def put(row, mask, keep=None):
                total = jnp.sum(jnp.where(mask, last, 0.0), axis=0, keepdims=True)
                value = jnp.exp(total)
                if keep is not None:
                    value = value * keep
                rows[self.base + row : self.base + row + 1, :] = value

            for s in range(steps):
                up = jnp.where(self.ups[s], 1, 0)
                mine = (chips // (2**s)) == (chip // (2**s))
                other = (chips // (2**s)) == ((self.partner[s] // 2) // (2**s))
                put(4 + 3 * s, other & (up == 1))
                put(5 + 3 * s, mine & (up == 0))
                ahead = (chips < chip) if self.forward else (chips > chip)
                put(6 + 3 * s, mine & ahead, keep=jnp.where(self.ups[s], 0.0, 1.0))
            if steps == 2:
                far, near = self.partner[1] // 2, self.partner[0] // 2

                def between(a, b):
                    return (chips > jnp.minimum(a, b)) & (chips < jnp.maximum(a, b))

                put(4 + 3 * steps, between(far, chip))
                put(5 + 3 * steps, between(far, near))

        def die1(self, k):
            return remote(self.st.at[(1 - core) * half + k], self.pr.at[k], self.d1s, self.d1r.at[k % near_ring], context=mate)

        def link(self, s, k, slot=None, own=None):
            if steps == 2 and s == 0 and slot is None:
                own = self.xe.at[k // 2]
            elif steps == 2:
                own = self.xr.at[{(0, 1): 0, (1, None): 1, (1, 0): 2}[s, slot], k // 2]
            group = self.xs.at[steps if slot == 1 else s]
            return remote(self.tot.at[s if slot is None else slot, k], self.rx.at[s, k], group, self.xr.at[s, k] if own is None else own, context=self.partner[s])

        def sent(self, group, count):
            span = self.rx.at[0, pl.ds(0, count)]
            return remote(span, span, self.xs.at[group], self.d2r.at[0], context=mate)

        def die2(self, k):
            return remote(self.sd.at[k], self.result.at[core * half + k], self.d2s, self.d2r.at[(k // unit) % back_ring], context=mate)

        def die2_in(self, base):
            span = self.sd.at[pl.ds(0, unit)]
            return remote(span, span, self.d2s, self.d2r.at[(base // unit) % back_ring], context=mate)

        def send(self, s, k):
            if s < steps - 1:
                self.link(s, k).start()
            else:
                @pl.when(self.ups[s])
                def _():
                    self.link(s, k).start()

        def send_first(self, k):
            if steps != 2:
                self.send(0, k)
                return

            @pl.when((k % 2 == 0) & (self.ups[0] | self.ups[1]))
            def _():
                self.send(0, k)

            @pl.when((k % 2 == 1) & self.ups[1])
            def _():
                self.link(1, k, 0).start()

        def step(self, s, k):
            if steps != 2:
                self.stage(s, k)
                return
            h = core * half + k
            up0, up1 = self.ups[0], self.ups[1]
            down0, down1 = jnp.logical_not(up0), jnp.logical_not(up1)
            even, odd = k % 2 == 0, k % 2 == 1

            if s == 0:
                @pl.when(even & (down0 | up1))
                def _():
                    self.stage(s, k)

                @pl.when(even & up0 & down1)
                def _():
                    self.pf[k] = jnp.zeros_like(self.pf[k])

                @pl.when(odd & up1 & up0)
                def _():
                    self.tot[1, k] = self.tot[0, k]
                    self.pf[k] = jnp.zeros_like(self.pf[k])

                @pl.when(odd & up1 & down0)
                def _():
                    self.pf[k] = jnp.zeros_like(self.pf[k])

                @pl.when(odd & down1)
                def _():
                    self.link(1, k, 0).wait_recv()
                    got = self.rx[1, k]
                    own = jnp.where(up0, 1.0, 0.0)
                    self.tot[1, k] = self.c(5 + 3 * steps, h) * got + own * self.tot[0, k]
                    self.pf[k] = self.c(4 + 3 * steps, h) * got

                @pl.when(odd & (up0 | down1))
                def _():
                    self.link(0, k, 1).start()
            else:
                @pl.when(even)
                def _():
                    self.stage(s, k)

                @pl.when(odd & (down0 | down1))
                def _():
                    self.link(0, k, 1).wait_recv()
                    self.pf[k] = self.pf[k] + self.rx[0, k]

                @pl.when(odd)
                def _():
                    self.hand(k)

        def combine(self, k):
            h = core * half + k
            self.die1(k).wait_recv()
            self.tot[0, k] = self.c(0, h) * self.st[h] + self.c(1, h) * self.pr[k]
            self.send_first(k)

        def stage(self, s, k):
            h = core * half + k
            if s < steps - 1:
                self.link(s, k).wait_recv()
                got = self.rx[s, k]
                self.tot[s + 1, k] = self.c(4 + 3 * s, h) * self.tot[s, k] + self.c(5 + 3 * s, h) * got
                self.send(s + 1, k)
                part = self.c(6 + 3 * s, h) * got
                self.pf[k] = part if s == 0 else self.pf[k] + part
                return

            @pl.when(jnp.logical_not(self.ups[s]))
            def _():
                self.link(s, k).wait_recv()
                part = self.c(6 + 3 * s, h) * self.rx[s, k]
                self.pf[k] = part if s == 0 else self.pf[k] + part

            if s == 0:
                @pl.when(self.ups[s])
                def _():
                    self.pf[k] = jnp.zeros_like(self.pf[k])

            self.hand(k)

        def hand(self, k):
            h = core * half + k
            prefix = self.pf[k]
            head_first = jnp.where(self.first, 1.0, 0.0)
            self.sd[k] = self.c(3, h) * prefix + head_first * self.st[h]
            self.die2(k).start()
            self.result[h] = self.c(2, h) * prefix + (1.0 - head_first) * self.pr[k]

        def drain(self):
            for group in (self.d1s, self.d2s):
                remote(self.sd, self.sd, group, self.d1r.at[0], context=mate).wait_send()
            if steps != 2:
                for s in range(steps - 1):
                    self.sent(s, half).wait_send()

                @pl.when(self.ups[steps - 1])
                def _():
                    self.sent(steps - 1, half).wait_send()

                return

            @pl.when(self.ups[0] | self.ups[1])
            def _():
                self.sent(0, half // 2).wait_send()

            @pl.when(self.ups[1])
            def _():
                self.sent(1, half).wait_send()

            @pl.when(self.ups[0] | jnp.logical_not(self.ups[1]))
            def _():
                self.sent(2, half // 2).wait_send()

    fwd = Scan(True, st_f, pr_f, tot_f, rx_f, sd_f, inc, pf_f, d1s_f, d1r_f, xs_f, xr_f, xe_f, d2s_f, d2r_f)
    bwd = Scan(False, st_b, pr_b, tot_b, rx_b, sd_b, later, pf_b, d1s_b, d1r_f, xs_b, xr_f if steps == 2 else xr_b, xe_b, d2s_b, d2r_f)

    def guarded(k, run):
        @pl.when((k >= 0) & (k < half))
        def _():
            run(k)

    def own_states(hs):
        made = []
        for h in hs:
            col = jnp.transpose(jnp.broadcast_to(cum_t[pl.ds(h, 1), :], (LANES, pos)))
            shrink = jnp.exp(col[pos - 1 : pos, :] - col)
            late = (k_ref[:, lanes(h)].astype(F32) * shrink).astype(BF16)
            made.append((h, col, dot_tn(late, v_ref[:, lanes(h)])))
        return made

    def keep_state(made):
        h, col, state = made
        st_f[h] = state
        colb[h] = col

    def states(k):
        far, near = own_states([(1 - core) * half + k, core * half + k])
        keep_state(far)
        fwd.die1(k).start()
        keep_state(near)

    def lead(k, carry):
        states(k)
        return carry

    lax.fori_loop(0, LEAD, lead, 0)
    gather_mate().wait_recv()
    rows[...] = jnp.zeros_like(rows)
    mine, other = gath[me, 0:1, :], gath[mate, 0:1, :]
    fwd.fill_near(mine, other)
    bwd.fill_near(mine, other)

    def spread_rows(picked):
        turned = jnp.transpose(rows[...])
        for r in picked:
            coef[r] = jnp.broadcast_to(turned[:heads, r : r + 1], (heads, LANES))

    near = [scan.base + row for scan in (fwd, bwd) for row in range(4)]
    spread_rows(near)
    columns_wait(k_hbm, k_ref, head_start, half, 6)
    columns_wait(v_hbm, v_ref, head_start, half, 7)
    for i in (1, 2, 3):
        fetch[i].start()
    ahead = (half + LEAD - SOLO) // 2 if unit == 2 and half > SOLO else 0

    def group(base):
        return [base + i for i in range(unit)]

    def feed(scan, produce, local, ready):
        def one(k, carry):
            guarded(k, produce)
            guarded(k - LEAD, scan.combine)
            if ahead:
                pl.when(k == SOLO)(ready)

                @pl.when((k > SOLO) & ((k - SOLO) % 2 == 1))
                def _():
                    local(group(core * half + k - SOLO - 1))

            return carry

        lax.fori_loop(scan.begun, half + LEAD, one, 0)
        if not ahead:
            ready()

    def intra(hs):
        made = []
        for h in hs:
            s = dot_nt(q_ref[:, lanes(h)], k_ref[:, lanes(h)])
            w = (s * decay_of(h)).astype(BF16)
            made.append((h, w, dot_nn(w, v_ref[:, lanes(h)])))
        for h, w, a in made:
            fw[h] = w
            att[:, lanes(h)] = a

    fwd.begun, bwd.begun = LEAD, 0

    def ready():
        for i in (1, 2, 3):
            fetch[i].wait()

    feed(fwd, states, intra, ready)
    gather_all().wait_recv()
    last = gath[:, 0, :]
    fwd.fill(last)
    bwd.fill(last)
    spread_rows([r for r in range(2 * (6 + 3 * steps)) if r not in near])
    acc_s[...] = jnp.zeros_like(acc_s)
    acc_p[...] = jnp.zeros_like(acc_p)

    def scaled_of(h):
        return gain_ref[:, lanes(h)] * g_ref[:, lanes(h)].astype(F32)

    def inter(hs):
        made = []
        for h in hs:
            far = dot_nn(q_ref[:, lanes(h)], inc[h].astype(BF16))
            a = att[:, lanes(h)] + jnp.exp(column(h)) * far
            made.append((h, a, scaled_of(h) * a))
        square, cross = acc_s[...], acc_p[...]
        for h, a, p in made:
            square, cross = square + a * a, cross + p
        acc_s[...], acc_p[...] = square, cross
        for h, a, p in made:
            att[:, lanes(h)] = a

    spread = -(-LAG // unit)
    lags = [0, count] if steps == 2 else [spread * s for s in range(steps)]
    lag_in = max(lags[-1] + spread, count)

    def pass_loop(scan, local, finish, extra=None):
        def one(it, carry):
            for s in range(steps):
                at = it - lags[s]

                @pl.when((at >= 0) & (at < count))
                def _():
                    for k in group(at * unit):
                        scan.step(s, k)

            turn = it + ahead

            @pl.when(turn < 2 * count)
            def _():
                late = turn // count
                who = core + late * (1 - 2 * core)
                local(group(who * half + (turn - late * count) * unit))

            if extra is not None:
                extra(it)

            own = it - lags[-1]

            @pl.when((own >= 0) & (own < count))
            def _():
                finish(group(core * half + own * unit))

            come = it - lag_in

            @pl.when((come >= 0) & (come < count))
            def _():
                scan.die2_in(come * unit).wait_recv()
                finish(group((1 - core) * half + come * unit))

            return carry

        lax.fori_loop(0, count + lag_in, one, 0)

    pass_loop(fwd, intra, inter)

    mean_sq = jnp.sum(acc_s[...], axis=1, keepdims=True) * (1.0 / feat)
    inverse = lax.rsqrt(mean_sq + EPSILON)
    proj = inverse * (jnp.sum(acc_p[...], axis=1, keepdims=True) * (1.0 / feat))
    acc_s[...] = jnp.broadcast_to(inverse, acc_s.shape)
    acc_p[...] = jnp.broadcast_to(proj, acc_p.shape)

    def delta(h):
        inv = acc_s[...]
        normed = att[:, lanes(h)] * inv
        wide = g_ref[:, lanes(h)].astype(F32)
        scaled = gain_ref[:, lanes(h)] * wide
        od = (inv * (scaled - normed * acc_p[...])).astype(BF16)
        terms = jnp.sum(wide * normed, axis=0, keepdims=True)
        early = (q_ref[:, lanes(h)].astype(F32) * jnp.exp(column(h))).astype(BF16)
        return h, od, terms, dot_tn(early, od)

    def keep_delta(made):
        h, od, terms, state = made
        st_b[h] = state
        od_ref[:, lanes(h)] = od
        gp[:, lanes(h)] = terms

    def deltas(k):
        far, near = delta((1 - core) * half + k), delta(core * half + k)
        keep_delta(far)
        bwd.die1(k).start()
        keep_delta(near)

    def local_back(hs):
        made = []
        for h in hs:
            od = od_ref[:, lanes(h)]
            q = q_ref[:, lanes(h)]
            key = k_ref[:, lanes(h)]
            bw = (dot_nt(od, v_ref[:, lanes(h)]) * decay_of(h)).astype(BF16)
            far = dot_nt(od, inc[h].astype(BF16))
            qg = (dot_nn(bw, key) + jnp.exp(column(h)) * far).astype(BF16)
            made.append((h, qg, dot_tn(bw, q), dot_tn(fw[h], od)))
        for h, qg, kl, vl in made:
            qg_ref[:, lanes(h)] = qg
            att[:, lanes(h)] = kl
            vloc[:, lanes(h)] = vl

    feed(bwd, deltas, local_back, lambda: None)

    part = feat // n_dp

    def gain_in():
        return remote(gp, gx.at[me], gx_s, gx_r, context=lead_of)

    def gain_in_all():
        span = gx.at[pl.ds(0, n - 1)]
        return remote(span, span, gx_s, gx_r, context=lead_of - 1)

    def gain_across(r):
        to = (dp + r) % n_dp
        return remote(gp.at[:, pl.ds(pl.multiple_of(to * part, LANES), part)], gz.at[r], gy_s, gy_r, dp=to)

    def gain_across_all():
        span = gz.at[pl.ds(1, n_dp - 1)]
        return remote(span, span, gy_s, gy_r, dp=(dp + 1) % n_dp)

    def gain_out(i):
        return remote(gy.at[i], gy.at[lead_of], gz_s, gz_r, context=i)

    def gain_out_all():
        span = gy.at[pl.ds(0, n - 1)]
        return remote(span, span, gz_s, gz_r, context=lead_of - 1)

    @pl.when(jnp.logical_not(leads))
    def _():
        gain_in().start()

    def gain_step(it):
        @pl.when(leads & (it == count))
        def _():
            gain_in_all().wait_recv()
            total = gp[...]
            for r in range(n - 1):
                total = total + gx[r]
            gp[...] = total
            if n_dp > 1:
                pl.semaphore_wait(barrier, n_dp - 1)
                for r in range(1, n_dp):
                    gain_across(r).start()

        @pl.when(leads & (it == 2 * count - 2))
        def _():
            total = gp[:, pl.ds(pl.multiple_of(dp * part, LANES), part)]
            if n_dp > 1:
                gain_across_all().wait_recv()
                for r in range(1, n_dp):
                    total = total + gz[r]
            for i in range(n):
                gy[i] = jnp.broadcast_to(total[:, i * width : (i + 1) * width], (8, width))
            for i in range(n - 1):
                gain_out(i).start()

    def finish_back(hs):
        made = []
        for h in hs:
            shrink = jnp.exp(block_last(h) - column(h))
            lt = later[h].astype(BF16)
            kg = att[:, lanes(h)] + shrink * dot_nt(v_ref[:, lanes(h)], lt)
            vg = vloc[:, lanes(h)] + shrink * dot_nn(k_ref[:, lanes(h)], lt)
            made.append((h, kg.astype(BF16), vg.astype(BF16)))
        for h, kg, vg in made:
            kg_ref[:, lanes(h)] = kg
            vg_ref[:, lanes(h)] = vg

    pass_loop(bwd, local_back, finish_back, gain_step)

    @pl.when(jnp.logical_not(leads))
    def _():
        gain_out(0).wait_recv()
        gain_in().wait_send()

    @pl.when(leads)
    def _():
        gain_out_all().wait_send()
        if n_dp > 1:
            gain_across_all().wait_send()

    gg_ref[...] = gy[lead_of][0:1, :] * cfg["norm"]
    gather_mate().wait_send()
    gather_all().wait_send()
    fwd.drain()
    bwd.drain()


def settle(count, *refs):
    srcs, dsts, sems = refs[:count], refs[count : 2 * count], refs[2 * count]
    copies = [pltpu.make_async_copy(srcs[i], dsts[i], sems.at[i]) for i in range(count)]
    for copy in copies:
        copy.start()
    for copy in copies:
        copy.wait()


def settled(arrays):
    count = len(arrays)
    return pl.pallas_call(
        functools.partial(settle, count),
        out_shape=tuple(jax.ShapeDtypeStruct(a.shape, a.dtype) for a in arrays),
        in_specs=[pl.BlockSpec(memory_space=pltpu.VMEM)] * count,
        out_specs=(pl.BlockSpec(memory_space=pl.ANY),) * count,
        scratch_shapes=[pltpu.SemaphoreType.DMA((count,))],
        compiler_params=pltpu.CompilerParams(vmem_limit_bytes=1 << 20),
    )(*[pltpu.with_memory_space_constraint(a, pltpu.VMEM) for a in arrays])


def per_device(queries, key_rows, value_rows, out_grad, log_decay, norm_gain):
    pos, feat = queries.shape[1:]
    heads = log_decay.shape[2]
    size = feat // heads
    half = heads // 2
    n, n_dp = lax.axis_size("context"), lax.axis_size("dp")
    steps = (n // 2).bit_length() - 1
    width = feat // (n * n_dp)
    pairs = half // 2 if half % 2 == 0 else half
    near_ring = 8 if half % 8 == 0 else half
    back_ring = 4 if steps == 2 and pairs % 4 == 0 else pairs
    cfg = dict(near_ring=near_ring, back_ring=back_ring, n=n, n_dp=n_dp, steps=steps, heads=heads, norm=1.0 / math.sqrt(pos * n * n_dp))
    vmem = pl.BlockSpec(memory_space=pltpu.VMEM)
    sem = pltpu.SemaphoreType.DMA

    def scan_buffers():
        return [
            pltpu.VMEM((heads, size, size), F32),
            pltpu.VMEM((half, size, size), F32),
            pltpu.VMEM((steps, half, size, size), F32),
            pltpu.VMEM((steps, half, size, size), F32),
            pltpu.VMEM((half, size, size), F32),
            pltpu.VMEM((heads, size, size), F32),
            pltpu.VMEM((half, size, size), F32),
        ]

    def scan_sems():
        evens = half // 2 if steps == 2 else 1
        links = sem((3, half // 2)) if steps == 2 else sem((steps, half))
        return [sem(()), sem((near_ring,)), sem((steps + 1,)), links, sem((evens,)), sem(()), sem((back_ring,))]

    def scan_sems_more():
        first = scan_sems()
        return [first[0], first[2], sem((1, 1)) if steps == 2 else first[3], first[4], first[5]]

    rows_bf = pltpu.VMEM((pos, feat), BF16)
    scratch = [
        *([rows_bf] * 4), pltpu.VMEM((heads, pos), F32), pltpu.VMEM((1, feat), F32), sem((8,)),
        pltpu.VMEM((pos, LANES), F32),
        pltpu.VMEM((LANES, pos), F32),
        pltpu.VMEM((heads, pos, LANES), F32),
        pltpu.VMEM((pos, feat), F32),
        pltpu.VMEM((pos, feat), F32),
        pltpu.VMEM((heads, pos, pos), BF16),
        pltpu.VMEM((pos, feat), BF16),
        pltpu.VMEM((pos, LANES), F32),
        pltpu.VMEM((pos, LANES), F32),
        pltpu.VMEM((n, 8, LANES), F32),
        pltpu.VMEM((LANES, LANES), F32),
        pltpu.VMEM((2 * (6 + 3 * steps), heads, LANES), F32),
        pltpu.VMEM((1, feat), F32),
        pltpu.VMEM((n, 1, feat), F32),
        pltpu.VMEM((n, 8, width), F32),
        pltpu.VMEM((n_dp, 1, feat // n_dp), F32),
        *scan_buffers(),
        *scan_buffers(),
        pltpu.SemaphoreType.REGULAR(()), *[sem(())] * 10,
        *scan_sems(),
        *scan_sems_more(),
    ]
    grid_out = pltpu.VMEM((pos, feat), BF16)
    spare = 3 * pos * feat * 2 + (1 << 20)
    qg, kg, vg, gg = pl.pallas_call(
        functools.partial(body, cfg),
        out_shape=(grid_out, grid_out, grid_out, pltpu.VMEM((1, width), F32)),
        in_specs=[pl.BlockSpec(memory_space=pl.ANY)] * 6,
        out_specs=(vmem,) * 4,
        scratch_shapes=scratch,
        compiler_params=pltpu.CompilerParams(
            collective_id=0, has_side_effects=True, vmem_limit_bytes=67043328 - spare
        ),
    )(queries[0], key_rows[0], value_rows[0], out_grad[0], log_decay[0].T, norm_gain[None])
    qg, kg, vg, gg = settled((qg, kg, vg, gg))
    return qg[None], kg[None], vg[None], gg[0]


def solution(mesh):
    rows = P("dp", "context", None)
    return jax.shard_map(
        per_device,
        mesh=mesh,
        in_specs=(rows,) * 5 + (P(),),
        out_specs=(rows, rows, rows, P(("dp", "context"))),
        check_vma=False,
    )
```

```python
import functools
import math

import jax
import jax.numpy as jnp
from jax import lax
from jax.experimental import pallas as pl
from jax.experimental.pallas import tpu as pltpu
from jax.sharding import PartitionSpec as P

EPSILON = 1e-06
F32 = jnp.float32
BF16 = jnp.bfloat16
LANES = 128
LAG = 2
LEAD = 2
SOLO = 8


def dot_nn(a, b):
    return lax.dot_general(a, b, (((1,), (0,)), ((), ())), preferred_element_type=F32)


def dot_nt(a, b):
    return lax.dot_general(a, b, (((1,), (1,)), ((), ())), preferred_element_type=F32)


def dot_tn(a, b):
    return lax.dot_general(a, b, (((0,), (0,)), ((), ())), preferred_element_type=F32)


def body(
    cfg,
    q_hbm, k_hbm, v_hbm, g_hbm, ld_hbm, gain_hbm,
    qg_ref, kg_ref, vg_ref, gg_ref,
    q_ref, k_ref, v_ref, g_ref, ld_ref, gain_ref, in_sem,
    cumc, cum_t, colb, att, vloc, fw, od_ref, acc_s, acc_p,
    gath, rows, coef, gp, gx, gy, gz,
    st_f, pr_f, tot_f, rx_f, sd_f, inc, pf_f,
    st_b, pr_b, tot_b, rx_b, sd_b, later, pf_b,
    entry, gm_s, gm_r, ga_s, ga_r, gx_s, gx_r, gy_s, gy_r, gz_s, gz_r,
    d1s_f, d1r_f, xs_f, xr_f, xe_f, d2s_f, d2r_f,
    d1s_b, xs_b, xr_b, xe_b, d2s_b,
):
    n, n_dp, steps, heads = cfg["n"], cfg["n_dp"], cfg["steps"], cfg["heads"]
    half = heads // 2
    unit = 2 if half % 2 == 0 else 1
    count = half // unit
    near_ring, back_ring = cfg["near_ring"], cfg["back_ring"]
    pos = q_ref.shape[0]
    feat = q_ref.shape[1]
    size = feat // heads
    width = feat // (n * n_dp)
    me = lax.axis_index("context")
    dp = lax.axis_index("dp")
    core = me % 2
    chip = me // 2
    mate = chip * 2 + (1 - core)

    fetch = [
        pltpu.make_async_copy(src, dst, in_sem.at[i])
        for i, (src, dst) in enumerate(
            [(ld_hbm, ld_ref), (q_hbm, q_ref), (g_hbm, g_ref), (gain_hbm, gain_ref)]
        )
    ]
    fetch[0].start()
    head_start = max(1, half // 4)

    def columns(src, dst, low, high, i):
        for side in (1 - core, core):
            at = pl.ds(pl.multiple_of((side * half + low) * size, LANES), (high - low) * size)
            pltpu.make_async_copy(src.at[:, at], dst.at[:, at], in_sem.at[i]).start()

    def columns_wait(src, dst, low, high, i):
        at = pl.ds(0, 2 * (high - low) * size)
        pltpu.make_async_copy(src.at[:, at], dst.at[:, at], in_sem.at[i]).wait()

    columns(k_hbm, k_ref, 0, head_start, 4)
    columns(v_hbm, v_ref, 0, head_start, 5)
    columns(k_hbm, k_ref, head_start, half, 6)
    columns(v_hbm, v_ref, head_start, half, 7)

    lead_of = n - 1
    leads = me == lead_of
    barrier = pltpu.get_barrier_semaphore()
    for r in range(1, n):
        peer = (me + r) % n

        @pl.when(peer != lead_of)
        def _():
            pl.semaphore_signal(barrier, inc=1, device_id={"context": peer}, device_id_type=pl.DeviceIdType.MESH)

    for r in range(1, n_dp):
        @pl.when(leads)
        def _():
            pl.semaphore_signal(barrier, inc=1, device_id={"dp": (dp + r) % n_dp}, device_id_type=pl.DeviceIdType.MESH)

    def remote(src, dst, send, recv, **where):
        return pltpu.make_async_remote_copy(
            src_ref=src, dst_ref=dst, send_sem=send, recv_sem=recv,
            device_id=where, device_id_type=pl.DeviceIdType.MESH,
        )

    row_i = lax.broadcasted_iota(jnp.int32, (pos, pos), 0)
    col_i = lax.broadcasted_iota(jnp.int32, (pos, pos), 1)
    tri = jnp.where(row_i <= col_i, 1.0, 0.0).astype(F32)
    cum_t[...] = jnp.zeros_like(cum_t)
    fetch[0].wait()
    cum_t[:heads, :] = lax.dot_general(
        ld_ref[...], tri, (((1,), (0,)), ((), ())),
        precision=lax.Precision.HIGHEST, preferred_element_type=F32,
    )
    cumc[...] = jnp.transpose(cum_t[...])
    cum = cumc[...]
    gath[me] = jnp.broadcast_to(cum[pos - 1 : pos, :], (8, LANES))

    @pl.when(jnp.logical_not(leads))
    def _():
        pl.semaphore_wait(barrier, n - 1)

    @pl.when(me == lead_of - 1)
    def _():
        pl.semaphore_signal(entry, inc=1, device_id={"context": lead_of}, device_id_type=pl.DeviceIdType.MESH)

    @pl.when(leads)
    def _():
        pl.semaphore_wait(entry, 1)

    def gather_copy(r):
        return remote(gath.at[me], gath.at[me], ga_s, ga_r, context=(me + r) % n)

    def gather_mate():
        return remote(gath.at[me], gath.at[me], gm_s, gm_r, context=mate)

    def gather_all():
        span = gath.at[pl.ds(0, n - 2)]
        return remote(span, span, ga_s, ga_r, context=mate)

    gather_mate().start()
    for r in range(1, n):
        @pl.when((me + r) % n != mate)
        def _():
            gather_copy(r).start()

    columns_wait(k_hbm, k_ref, 0, head_start, 4)
    columns_wait(v_hbm, v_ref, 0, head_start, 5)

    def lanes(h):
        return pl.ds(pl.multiple_of(h * size, size), size)

    def column(h):
        return colb[h]

    def block_last(h):
        return colb[h, pos - 1 : pos, :]

    def decay_of(h):
        col = colb[h]
        wide = jnp.concatenate([col] * (-(-pos // LANES)), axis=1)[:, :pos]
        return jnp.exp(jnp.where(row_i >= col_i, wide - cum_t[pl.ds(h, 1), :], -jnp.inf))

    class Scan:
        def __init__(self, forward, st, pr, tot, rx, sd, result, pf, d1s, d1r, xs, xr, xe, d2s, d2r):
            self.forward, self.st, self.pr, self.tot, self.rx = forward, st, pr, tot, rx
            self.sd, self.result, self.pf, self.xe = sd, result, pf, xe
            self.d1s, self.d1r, self.xs, self.xr, self.d2s, self.d2r = d1s, d1r, xs, xr, d2s, d2r
            self.first = (core == 0) if forward else (core == 1)
            self.base = 0 if forward else 6 + 3 * steps
            self.bits, self.partner, self.ups = [], [], []
            for s in range(steps):
                bit = (chip // (2**s)) % 2
                self.bits.append(bit)
                self.partner.append((chip + (1 - 2 * bit) * (2**s)) * 2 + core)
                self.ups.append((bit == 0) if forward else (bit == 1))

        def c(self, row, h):
            return coef[self.base + row, pl.ds(h, 1), :]

        def fill_near(self, mine, other):
            one = jnp.where(self.first, 1.0, 0.0)
            values = [one * other, (1.0 - one) * mine, (1.0 - one) * other, one * mine]
            for row, total in enumerate(values):
                rows[self.base + row : self.base + row + 1, :] = jnp.exp(total)

        def fill(self, last):
            ids = lax.broadcasted_iota(jnp.int32, last.shape, 0)
            chips = ids // 2

            def put(row, mask, keep=None):
                total = jnp.sum(jnp.where(mask, last, 0.0), axis=0, keepdims=True)
                value = jnp.exp(total)
                if keep is not None:
                    value = value * keep
                rows[self.base + row : self.base + row + 1, :] = value

            for s in range(steps):
                up = jnp.where(self.ups[s], 1, 0)
                mine = (chips // (2**s)) == (chip // (2**s))
                other = (chips // (2**s)) == ((self.partner[s] // 2) // (2**s))
                put(4 + 3 * s, other & (up == 1))
                put(5 + 3 * s, mine & (up == 0))
                ahead = (chips < chip) if self.forward else (chips > chip)
                put(6 + 3 * s, mine & ahead, keep=jnp.where(self.ups[s], 0.0, 1.0))
            if steps == 2:
                far, near = self.partner[1] // 2, self.partner[0] // 2

                def between(a, b):
                    return (chips > jnp.minimum(a, b)) & (chips < jnp.maximum(a, b))

                put(4 + 3 * steps, between(far, chip))
                put(5 + 3 * steps, between(far, near))

        def die1(self, k):
            return remote(self.st.at[(1 - core) * half + k], self.pr.at[k], self.d1s, self.d1r.at[k % near_ring], context=mate)

        def link(self, s, k, slot=None, own=None):
            if steps == 2 and s == 0 and slot is None:
                own = self.xe.at[k // 2]
            elif steps == 2:
                own = self.xr.at[{(0, 1): 0, (1, None): 1, (1, 0): 2}[s, slot], k // 2]
            group = self.xs.at[steps if slot == 1 else s]
            return remote(self.tot.at[s if slot is None else slot, k], self.rx.at[s, k], group, self.xr.at[s, k] if own is None else own, context=self.partner[s])

        def sent(self, group, count):
            span = self.rx.at[0, pl.ds(0, count)]
            return remote(span, span, self.xs.at[group], self.d2r.at[0], context=mate)

        def die2(self, k):
            return remote(self.sd.at[k], self.result.at[core * half + k], self.d2s, self.d2r.at[(k // unit) % back_ring], context=mate)

        def die2_in(self, base):
            span = self.sd.at[pl.ds(0, unit)]
            return remote(span, span, self.d2s, self.d2r.at[(base // unit) % back_ring], context=mate)

        def send(self, s, k):
            if s < steps - 1:
                self.link(s, k).start()
            else:
                @pl.when(self.ups[s])
                def _():
                    self.link(s, k).start()

        def send_first(self, k):
            if steps != 2:
                self.send(0, k)
                return

            @pl.when((k % 2 == 0) & (self.ups[0] | self.ups[1]))
            def _():
                self.send(0, k)

            @pl.when((k % 2 == 1) & self.ups[1])
            def _():
                self.link(1, k, 0).start()

        def step(self, s, k):
            if steps != 2:
                self.stage(s, k)
                return
            h = core * half + k
            up0, up1 = self.ups[0], self.ups[1]
            down0, down1 = jnp.logical_not(up0), jnp.logical_not(up1)
            even, odd = k % 2 == 0, k % 2 == 1

            if s == 0:
                @pl.when(even & (down0 | up1))
                def _():
                    self.stage(s, k)

                @pl.when(even & up0 & down1)
                def _():
                    self.pf[k] = jnp.zeros_like(self.pf[k])

                @pl.when(odd & up1 & up0)
                def _():
                    self.tot[1, k] = self.tot[0, k]
                    self.pf[k] = jnp.zeros_like(self.pf[k])

                @pl.when(odd & up1 & down0)
                def _():
                    self.pf[k] = jnp.zeros_like(self.pf[k])

                @pl.when(odd & down1)
                def _():
                    self.link(1, k, 0).wait_recv()
                    got = self.rx[1, k]
                    own = jnp.where(up0, 1.0, 0.0)
                    self.tot[1, k] = self.c(5 + 3 * steps, h) * got + own * self.tot[0, k]
                    self.pf[k] = self.c(4 + 3 * steps, h) * got

                @pl.when(odd & (up0 | down1))
                def _():
                    self.link(0, k, 1).start()
            else:
                @pl.when(even)
                def _():
                    self.stage(s, k)

                @pl.when(odd & (down0 | down1))
                def _():
                    self.link(0, k, 1).wait_recv()
                    self.pf[k] = self.pf[k] + self.rx[0, k]

                @pl.when(odd)
                def _():
                    self.hand(k)

        def combine(self, k):
            h = core * half + k
            self.die1(k).wait_recv()
            self.tot[0, k] = self.c(0, h) * self.st[h] + self.c(1, h) * self.pr[k]
            self.send_first(k)

        def stage(self, s, k):
            h = core * half + k
            if s < steps - 1:
                self.link(s, k).wait_recv()
                got = self.rx[s, k]
                self.tot[s + 1, k] = self.c(4 + 3 * s, h) * self.tot[s, k] + self.c(5 + 3 * s, h) * got
                self.send(s + 1, k)
                part = self.c(6 + 3 * s, h) * got
                self.pf[k] = part if s == 0 else self.pf[k] + part
                return

            @pl.when(jnp.logical_not(self.ups[s]))
            def _():
                self.link(s, k).wait_recv()
                part = self.c(6 + 3 * s, h) * self.rx[s, k]
                self.pf[k] = part if s == 0 else self.pf[k] + part

            if s == 0:
                @pl.when(self.ups[s])
                def _():
                    self.pf[k] = jnp.zeros_like(self.pf[k])

            self.hand(k)

        def hand(self, k):
            h = core * half + k
            prefix = self.pf[k]
            head_first = jnp.where(self.first, 1.0, 0.0)
            self.sd[k] = self.c(3, h) * prefix + head_first * self.st[h]
            self.die2(k).start()
            self.result[h] = self.c(2, h) * prefix + (1.0 - head_first) * self.pr[k]

        def drain(self):
            for group in (self.d1s, self.d2s):
                remote(self.sd, self.sd, group, self.d1r.at[0], context=mate).wait_send()
            if steps != 2:
                for s in range(steps - 1):
                    self.sent(s, half).wait_send()

                @pl.when(self.ups[steps - 1])
                def _():
                    self.sent(steps - 1, half).wait_send()

                return

            @pl.when(self.ups[0] | self.ups[1])
            def _():
                self.sent(0, half // 2).wait_send()

            @pl.when(self.ups[1])
            def _():
                self.sent(1, half).wait_send()

            @pl.when(self.ups[0] | jnp.logical_not(self.ups[1]))
            def _():
                self.sent(2, half // 2).wait_send()

    fwd = Scan(True, st_f, pr_f, tot_f, rx_f, sd_f, inc, pf_f, d1s_f, d1r_f, xs_f, xr_f, xe_f, d2s_f, d2r_f)
    bwd = Scan(False, st_b, pr_b, tot_b, rx_b, sd_b, later, pf_b, d1s_b, d1r_f, xs_b, xr_f if steps == 2 else xr_b, xe_b, d2s_b, d2r_f)

    def guarded(k, run):
        @pl.when((k >= 0) & (k < half))
        def _():
            run(k)

    def own_states(hs):
        made = []
        for h in hs:
            col = jnp.transpose(jnp.broadcast_to(cum_t[pl.ds(h, 1), :], (LANES, pos)))
            shrink = jnp.exp(col[pos - 1 : pos, :] - col)
            late = (k_ref[:, lanes(h)].astype(F32) * shrink).astype(BF16)
            made.append((h, col, dot_tn(late, v_ref[:, lanes(h)])))
        return made

    def keep_state(made):
        h, col, state = made
        st_f[h] = state
        colb[h] = col

    def states(k):
        far, near = own_states([(1 - core) * half + k, core * half + k])
        keep_state(far)
        fwd.die1(k).start()
        keep_state(near)

    def lead(k, carry):
        states(k)
        return carry

    lax.fori_loop(0, LEAD, lead, 0)
    gather_mate().wait_recv()
    rows[...] = jnp.zeros_like(rows)
    mine, other = gath[me, 0:1, :], gath[mate, 0:1, :]
    fwd.fill_near(mine, other)
    bwd.fill_near(mine, other)

    def spread_rows(picked):
        turned = jnp.transpose(rows[...])
        for r in picked:
            coef[r] = jnp.broadcast_to(turned[:heads, r : r + 1], (heads, LANES))

    near = [scan.base + row for scan in (fwd, bwd) for row in range(4)]
    spread_rows(near)
    columns_wait(k_hbm, k_ref, head_start, half, 6)
    columns_wait(v_hbm, v_ref, head_start, half, 7)
    ahead = (half + LEAD - SOLO) // 2 if unit == 2 and half > SOLO else 0

    def group(base):
        return [base + i for i in range(unit)]

    def feed(scan, produce, local, ready):
        def one(k, carry):
            guarded(k, produce)
            guarded(k - LEAD, scan.combine)
            if scan.forward:
                @pl.when(k == LEAD + 1)
                def _():
                    for i in (1, 2, 3):
                        fetch[i].start()

            if ahead:
                pl.when(k == SOLO)(ready)

                @pl.when((k > SOLO) & ((k - SOLO) % 2 == 1))
                def _():
                    local(group(core * half + k - SOLO - 1))

            return carry

        lax.fori_loop(scan.begun, half + LEAD, one, 0)
        if not ahead:
            ready()

    def intra(hs):
        made = []
        for h in hs:
            s = dot_nt(q_ref[:, lanes(h)], k_ref[:, lanes(h)])
            w = (s * decay_of(h)).astype(BF16)
            made.append((h, w, dot_nn(w, v_ref[:, lanes(h)])))
        for h, w, a in made:
            fw[h] = w
            att[:, lanes(h)] = a

    fwd.begun, bwd.begun = LEAD, 0

    def ready():
        for i in (1, 2, 3):
            fetch[i].wait()

    feed(fwd, states, intra, ready)
    gather_all().wait_recv()
    last = gath[:, 0, :]
    fwd.fill(last)
    bwd.fill(last)
    spread_rows([r for r in range(2 * (6 + 3 * steps)) if r not in near])
    acc_s[...] = jnp.zeros_like(acc_s)
    acc_p[...] = jnp.zeros_like(acc_p)

    def scaled_of(h):
        return gain_ref[:, lanes(h)] * g_ref[:, lanes(h)].astype(F32)

    def inter(hs):
        made = []
        for h in hs:
            far = dot_nn(q_ref[:, lanes(h)], inc[h].astype(BF16))
            a = att[:, lanes(h)] + jnp.exp(column(h)) * far
            made.append((h, a, scaled_of(h) * a))
        square, cross = acc_s[...], acc_p[...]
        for h, a, p in made:
            square, cross = square + a * a, cross + p
        acc_s[...], acc_p[...] = square, cross
        for h, a, p in made:
            att[:, lanes(h)] = a

    spread = -(-LAG // unit)
    lags = [0, max(count - 2, spread)] if steps == 2 else [spread * s for s in range(steps)]
    lag_in = max(lags[-1] + spread, count - ahead)

    def pass_loop(scan, local, finish, extra=None):
        def one(it, carry):
            for s in range(steps):
                at = it - lags[s]

                @pl.when((at >= 0) & (at < count))
                def _():
                    for k in group(at * unit):
                        scan.step(s, k)

            turn = it + ahead

            @pl.when(turn < 2 * count)
            def _():
                late = turn // count
                who = core + late * (1 - 2 * core)
                local(group(who * half + (turn - late * count) * unit))

            if extra is not None:
                extra(it)

            own = it - lags[-1]

            @pl.when((own >= 0) & (own < count))
            def _():
                finish(group(core * half + own * unit))

            come = it - lag_in

            @pl.when((come >= 0) & (come < count))
            def _():
                scan.die2_in(come * unit).wait_recv()
                finish(group((1 - core) * half + come * unit))

            return carry

        lax.fori_loop(0, count + lag_in, one, 0)

    pass_loop(fwd, intra, inter)

    mean_sq = jnp.sum(acc_s[...], axis=1, keepdims=True) * (1.0 / feat)
    inverse = lax.rsqrt(mean_sq + EPSILON)
    proj = inverse * (jnp.sum(acc_p[...], axis=1, keepdims=True) * (1.0 / feat))
    acc_s[...] = jnp.broadcast_to(inverse, acc_s.shape)
    acc_p[...] = jnp.broadcast_to(proj, acc_p.shape)

    def delta(h):
        inv = acc_s[...]
        normed = att[:, lanes(h)] * inv
        wide = g_ref[:, lanes(h)].astype(F32)
        scaled = gain_ref[:, lanes(h)] * wide
        od = (inv * (scaled - normed * acc_p[...])).astype(BF16)
        terms = jnp.sum(wide * normed, axis=0, keepdims=True)
        early = (q_ref[:, lanes(h)].astype(F32) * jnp.exp(column(h))).astype(BF16)
        return h, od, terms, dot_tn(early, od)

    def keep_delta(made):
        h, od, terms, state = made
        st_b[h] = state
        od_ref[:, lanes(h)] = od
        gp[:, lanes(h)] = terms

    def deltas(k):
        far, near = delta((1 - core) * half + k), delta(core * half + k)
        keep_delta(far)
        bwd.die1(k).start()
        keep_delta(near)

    def local_back(hs):
        made = []
        for h in hs:
            od = od_ref[:, lanes(h)]
            q = q_ref[:, lanes(h)]
            key = k_ref[:, lanes(h)]
            bw = (dot_nt(od, v_ref[:, lanes(h)]) * decay_of(h)).astype(BF16)
            far = dot_nt(od, inc[h].astype(BF16))
            qg = (dot_nn(bw, key) + jnp.exp(column(h)) * far).astype(BF16)
            made.append((h, qg, dot_tn(bw, q), dot_tn(fw[h], od)))
        for h, qg, kl, vl in made:
            qg_ref[:, lanes(h)] = qg
            att[:, lanes(h)] = kl
            vloc[:, lanes(h)] = vl

    feed(bwd, deltas, local_back, lambda: None)

    part = feat // n_dp

    def gain_in():
        return remote(gp, gx.at[me], gx_s, gx_r, context=lead_of)

    def gain_in_all():
        span = gx.at[pl.ds(0, n - 1)]
        return remote(span, span, gx_s, gx_r, context=lead_of - 1)

    def gain_across(r):
        to = (dp + r) % n_dp
        return remote(gp.at[:, pl.ds(pl.multiple_of(to * part, LANES), part)], gz.at[r], gy_s, gy_r, dp=to)

    def gain_across_all():
        span = gz.at[pl.ds(1, n_dp - 1)]
        return remote(span, span, gy_s, gy_r, dp=(dp + 1) % n_dp)

    def gain_out(i):
        return remote(gy.at[i], gy.at[lead_of], gz_s, gz_r, context=i)

    def gain_out_all():
        span = gy.at[pl.ds(0, n - 1)]
        return remote(span, span, gz_s, gz_r, context=lead_of - 1)

    @pl.when(jnp.logical_not(leads))
    def _():
        gain_in().start()

    def gain_step(it):
        @pl.when(leads & (it == count))
        def _():
            gain_in_all().wait_recv()
            total = gp[...]
            for r in range(n - 1):
                total = total + gx[r]
            gp[...] = total
            if n_dp > 1:
                pl.semaphore_wait(barrier, n_dp - 1)
                for r in range(1, n_dp):
                    gain_across(r).start()

        @pl.when(leads & (it == count + lag_in - 2))
        def _():
            total = gp[:, pl.ds(pl.multiple_of(dp * part, LANES), part)]
            if n_dp > 1:
                gain_across_all().wait_recv()
                for r in range(1, n_dp):
                    total = total + gz[r]
            for i in range(n):
                gy[i] = jnp.broadcast_to(total[:, i * width : (i + 1) * width], (8, width))
            for i in range(n - 1):
                gain_out(i).start()

    def finish_back(hs):
        made = []
        for h in hs:
            shrink = jnp.exp(block_last(h) - column(h))
            lt = later[h].astype(BF16)
            kg = att[:, lanes(h)] + shrink * dot_nt(v_ref[:, lanes(h)], lt)
            vg = vloc[:, lanes(h)] + shrink * dot_nn(k_ref[:, lanes(h)], lt)
            made.append((h, kg.astype(BF16), vg.astype(BF16)))
        for h, kg, vg in made:
            kg_ref[:, lanes(h)] = kg
            vg_ref[:, lanes(h)] = vg

    pass_loop(bwd, local_back, finish_back, gain_step)

    @pl.when(jnp.logical_not(leads))
    def _():
        gain_out(0).wait_recv()
        gain_in().wait_send()

    @pl.when(leads)
    def _():
        gain_out_all().wait_send()
        if n_dp > 1:
            gain_across_all().wait_send()

    gg_ref[...] = gy[lead_of][0:1, :] * cfg["norm"]
    gather_mate().wait_send()
    gather_all().wait_send()
    fwd.drain()
    bwd.drain()


def settle(count, *refs):
    srcs, dsts, sems = refs[:count], refs[count : 2 * count], refs[2 * count]
    for i in range(count):
        rows = srcs[i].shape[0]
        parts = 4 if rows % 64 == 0 else 1
        for j in range(parts):
            at = pl.ds(j * (rows // parts), rows // parts)
            pltpu.make_async_copy(srcs[i].at[at], dsts[i].at[at], sems.at[i]).start()
    for i in range(count):
        pltpu.make_async_copy(srcs[i], dsts[i], sems.at[i]).wait()


def settled(arrays):
    count = len(arrays)
    return pl.pallas_call(
        functools.partial(settle, count),
        out_shape=tuple(jax.ShapeDtypeStruct(a.shape, a.dtype) for a in arrays),
        in_specs=[pl.BlockSpec(memory_space=pltpu.VMEM)] * count,
        out_specs=(pl.BlockSpec(memory_space=pl.ANY),) * count,
        scratch_shapes=[pltpu.SemaphoreType.DMA((count,))],
        compiler_params=pltpu.CompilerParams(vmem_limit_bytes=1 << 20),
    )(*[pltpu.with_memory_space_constraint(a, pltpu.VMEM) for a in arrays])


def per_device(queries, key_rows, value_rows, out_grad, log_decay, norm_gain):
    pos, feat = queries.shape[1:]
    heads = log_decay.shape[2]
    size = feat // heads
    half = heads // 2
    n, n_dp = lax.axis_size("context"), lax.axis_size("dp")
    steps = (n // 2).bit_length() - 1
    width = feat // (n * n_dp)
    pairs = half // 2 if half % 2 == 0 else half
    near_ring = 8 if half % 8 == 0 else half
    back_ring = 4 if steps == 2 and pairs % 4 == 0 else pairs
    cfg = dict(near_ring=near_ring, back_ring=back_ring, n=n, n_dp=n_dp, steps=steps, heads=heads, norm=1.0 / math.sqrt(pos * n * n_dp))
    vmem = pl.BlockSpec(memory_space=pltpu.VMEM)
    sem = pltpu.SemaphoreType.DMA

    def scan_buffers():
        return [
            pltpu.VMEM((heads, size, size), F32),
            pltpu.VMEM((half, size, size), F32),
            pltpu.VMEM((steps, half, size, size), F32),
            pltpu.VMEM((steps, half, size, size), F32),
            pltpu.VMEM((half, size, size), F32),
            pltpu.VMEM((heads, size, size), F32),
            pltpu.VMEM((half, size, size), F32),
        ]

    def scan_sems():
        evens = half // 2 if steps == 2 else 1
        links = sem((3, half // 2)) if steps == 2 else sem((steps, half))
        return [sem(()), sem((near_ring,)), sem((steps + 1,)), links, sem((evens,)), sem(()), sem((back_ring,))]

    def scan_sems_more():
        first = scan_sems()
        return [first[0], first[2], sem((1, 1)) if steps == 2 else first[3], first[4], first[5]]

    rows_bf = pltpu.VMEM((pos, feat), BF16)
    scratch = [
        *([rows_bf] * 4), pltpu.VMEM((heads, pos), F32), pltpu.VMEM((1, feat), F32), sem((8,)),
        pltpu.VMEM((pos, LANES), F32),
        pltpu.VMEM((LANES, pos), F32),
        pltpu.VMEM((heads, pos, LANES), F32),
        pltpu.VMEM((pos, feat), F32),
        pltpu.VMEM((pos, feat), F32),
        pltpu.VMEM((heads, pos, pos), BF16),
        pltpu.VMEM((pos, feat), BF16),
        pltpu.VMEM((pos, LANES), F32),
        pltpu.VMEM((pos, LANES), F32),
        pltpu.VMEM((n, 8, LANES), F32),
        pltpu.VMEM((LANES, LANES), F32),
        pltpu.VMEM((2 * (6 + 3 * steps), heads, LANES), F32),
        pltpu.VMEM((1, feat), F32),
        pltpu.VMEM((n, 1, feat), F32),
        pltpu.VMEM((n, 8, width), F32),
        pltpu.VMEM((n_dp, 1, feat // n_dp), F32),
        *scan_buffers(),
        *scan_buffers(),
        pltpu.SemaphoreType.REGULAR(()), *[sem(())] * 10,
        *scan_sems(),
        *scan_sems_more(),
    ]
    grid_out = pltpu.VMEM((pos, feat), BF16)
    spare = 3 * pos * feat * 2 + (1 << 20)
    qg, kg, vg, gg = pl.pallas_call(
        functools.partial(body, cfg),
        out_shape=(grid_out, grid_out, grid_out, pltpu.VMEM((1, width), F32)),
        in_specs=[pl.BlockSpec(memory_space=pl.ANY)] * 6,
        out_specs=(vmem,) * 4,
        scratch_shapes=scratch,
        compiler_params=pltpu.CompilerParams(
            collective_id=0, has_side_effects=True, vmem_limit_bytes=67043328 - spare
        ),
    )(queries[0], key_rows[0], value_rows[0], out_grad[0], log_decay[0].T, norm_gain[None])
    qg, kg, vg, gg = settled((qg, kg, vg, gg))
    return qg[None], kg[None], vg[None], gg[0]


def solution(mesh):
    rows = P("dp", "context", None)
    return jax.shard_map(
        per_device,
        mesh=mesh,
        in_specs=(rows,) * 5 + (P(),),
        out_specs=(rows, rows, rows, P(("dp", "context"))),
        check_vma=False,
    )
```
